32 devices in a mesh: dp: 8 (over z, x), tensor: 4 (over y, core).
Axes of the slice: x: 2, y: 2, z: 4, core: 2. Of those that a mesh axis runs over, the one named last changes fastest.
Arguments:
- tokens: bfloat16 [64, 532, 768], P(('dp', 'tensor')), may hold values from -6 to 6
- segment_lengths: int32 [64], P(('dp', 'tensor')), may hold values from 256 to 512, as said below
- cotangent: bfloat16 [64, 532, 768], P(('dp', 'tensor')), may hold values from -6 to 6
- attention_master: float32 [3072, 768], P(('dp', 'tensor'))
- attention_mean: float32 [3072, 768], P(('dp', 'tensor')), may hold values from -32 to 32
- attention_square: float32 [3072, 768], P(('dp', 'tensor')), may hold values from 3.06432 to 12.25728
- up_master: float32 [768, 3072], P('dp', 'tensor'), may hold values from -0.21875 to 0.21875
- up_mean: float32 [768, 3072], P('dp', 'tensor'), may hold values from -32 to 32
- up_square: float32 [768, 3072], P('dp', 'tensor'), may hold values from 3.06432 to 12.25728
- down_master: float32 [768, 3072], P('dp', 'tensor'), may hold values from -0.109375 to 0.109375
- down_mean: float32 [768, 3072], P('dp', 'tensor'), may hold values from -32 to 32
- down_square: float32 [768, 3072], P('dp', 'tensor'), may hold values from 3.06432 to 12.25728
- vector_master: float32 [768, 12], P('dp')
- vector_mean: float32 [768, 12], P('dp'), may hold values from -64 to 64
- vector_square: float32 [768, 12], P('dp'), may hold values from 8.512 to 34.048
Outputs:
- block_output: bfloat16 [64, 532, 768], P(('dp', 'tensor'))
- input_grad: float32 [64, 532, 768], P(('dp', 'tensor'))
- attention_weights: float32 [3072, 768], P(('dp', 'tensor'))
- attention_first: float32 [3072, 768], P(('dp', 'tensor'))
- attention_second: float32 [3072, 768], P(('dp', 'tensor'))
- up_weights: float32 [768, 3072], P('dp', 'tensor')
- up_first: float32 [768, 3072], P('dp', 'tensor')
- up_second: float32 [768, 3072], P('dp', 'tensor')
- down_weights: float32 [768, 3072], P('dp', 'tensor')
- down_first: float32 [768, 3072], P('dp', 'tensor')
- down_second: float32 [768, 3072], P('dp', 'tensor')
- vector_params: float32 [768, 12], P('dp')
- vector_first: float32 [768, 12], P('dp')
- vector_second: float32 [768, 12], P('dp')
The draws below stay inside these ranges and needn't reach their ends.
Inputs may be any that keep to these rules, and one draw needn't show every extreme that they name: `segment_lengths`: live token slots per segment; some segment has all 512 live.
All inputs are finite; a program needn't handle non-finite values.
Results may differ from the reference program's by a relative error of at most 0.013.
The reference program's roundings to bfloat16 on the way count: a program that leaves them out, or rounds other values in their place, can miss the bound.
Values may be sent and summed in bfloat16 or wider, within the bound.
A program may use at most 256 MiB of HBM per device.

```python
import math
import jax
import jax.numpy as jnp
from jax import lax

D = 768
HEADS = 12
HEAD_DIM = 64
FF = 3072
MEM = 10
SEG_TOK = 512
STEPS = 5
ROWS = 532
SEGS = 64
ROWS_ALL = 34048
VEC_COLS = 12


def draw_segment_lengths(key, part):
    drawn = jax.random.randint(key, (SEGS,), SEG_TOK // 2, SEG_TOK + 1, dtype=jnp.int32)
    return drawn.at[0].set(SEG_TOK)


def draw_attention_master(key, part):
    base = jax.random.normal(key, (4 * D, D), jnp.float32)
    blocks = jnp.arange(4 * D) // D
    factors = jnp.array([1.5, 1.0, 1.0, 6.0], jnp.float32)[blocks] * D ** (-0.5)
    return base * factors[:, None]


def draw_vector_master(key, part):
    base = jax.random.normal(key, (D, VEC_COLS), jnp.float32)
    column = jnp.arange(VEC_COLS)
    is_gain = (column == 3) | (column == 5)
    return jnp.where(is_gain[None, :], 1.0 + 0.1 * base, 0.3 * base)


def level_of(stream_key, shape, cuts, least, largest):
    factor_of = 1.0
    for dim, shards_of in cuts:
        heights = jax.random.uniform(jax.random.fold_in(jax.random.fold_in(stream_key, 6), dim), (shards_of,), jnp.float32, least / len(cuts), largest / len(cuts))
        factor_of = factor_of * jnp.repeat(jnp.exp(heights), shape[dim] // shards_of).reshape((-1,) + (1,) * (len(shape) - 1 - dim))
    return factor_of


def centred(stream_key, shape, scale, reach, split=(), kind=jnp.bfloat16):
    factor_of = level_of(stream_key, shape, split, -0.22, 0.18) if split else 1.0
    values = jax.random.normal(stream_key, shape, jnp.float32) * scale * factor_of
    return jnp.minimum(jnp.maximum(values, -reach), reach).astype(kind)


def setup_inputs(seed: int = 0) -> dict:
    arg_keys = jax.random.split(jax.random.key(seed), 16)
    return {
        "tokens": centred(arg_keys[0], (SEGS, ROWS, D), 1.0, 6.0, ((0, 32),)),
        "segment_lengths": draw_segment_lengths(jax.random.fold_in(arg_keys[15], 71), 0),
        "cotangent": centred(arg_keys[2], (SEGS, ROWS, D), 1.0, 6.0, ((0, 32),)),
        "attention_master": draw_attention_master(jax.random.fold_in(arg_keys[15], 71), 0),
        "attention_mean": centred(arg_keys[4], (4 * D, D), (0.03 * ROWS_ALL ** 0.5), 32.0, ((0, 32),), jnp.float32),
        "attention_square": jnp.clip(jnp.exp(math.log(12.25728) - 1.3862944 * jax.random.uniform(arg_keys[5], (4 * D, D), jnp.float32) ** level_of(arg_keys[5], (4 * D, D), ((0, 32),), -0.2, 0.2)), 3.06432, 12.25728),
        "up_master": centred(arg_keys[6], (D, FF), D ** -0.5, 0.21875, ((0, 8), (1, 4)), jnp.float32),
        "up_mean": centred(arg_keys[7], (D, FF), (0.03 * ROWS_ALL ** 0.5), 32.0, ((0, 8), (1, 4)), jnp.float32),
        "up_square": jnp.clip(jnp.exp(math.log(12.25728) - 1.3862944 * jax.random.uniform(arg_keys[8], (D, FF), jnp.float32) ** level_of(arg_keys[8], (D, FF), ((0, 8), (1, 4)), -0.2, 0.2)), 3.06432, 12.25728),
        "down_master": centred(arg_keys[9], (D, FF), FF ** -0.5, 0.109375, ((0, 8), (1, 4)), jnp.float32),
        "down_mean": centred(arg_keys[10], (D, FF), (0.03 * ROWS_ALL ** 0.5), 32.0, ((0, 8), (1, 4)), jnp.float32),
        "down_square": jnp.clip(jnp.exp(math.log(12.25728) - 1.3862944 * jax.random.uniform(arg_keys[11], (D, FF), jnp.float32) ** level_of(arg_keys[11], (D, FF), ((0, 8), (1, 4)), -0.2, 0.2)), 3.06432, 12.25728),
        "vector_master": draw_vector_master(jax.random.fold_in(arg_keys[15], 71), 0),
        "vector_mean": centred(arg_keys[13], (D, VEC_COLS), (0.06 * ROWS_ALL ** 0.5), 64.0, ((0, 8),), jnp.float32),
        "vector_square": jnp.clip(jnp.exp(math.log(34.048) - 1.3862944 * jax.random.uniform(arg_keys[14], (D, VEC_COLS), jnp.float32) ** level_of(arg_keys[14], (D, VEC_COLS), ((0, 8),), -0.2, 0.2)), 8.512, 34.048),
    }


@jax.custom_vjp
def low(v):
    return lax.optimization_barrier(v.astype(jnp.bfloat16)).astype(jnp.float32)

@jax.custom_vjp
def low_back(v):
    return v

def low_keep(v):
    return (low(v), None)

def low_pass(kept, grad):
    return (grad,)

def back_keep(v):
    return (v, None)

def back_low(kept, grad):
    return (low(grad),)
low.defvjp(low_keep, low_pass)
low_back.defvjp(back_keep, back_low)
highest = lax.Precision.HIGHEST
norm_epsilon = 1e-12
beta_first = 0.9
beta_second = 0.999
adam_epsilon = 1e-08
matrix_rate = 0.06
vector_rate = 0.2
weight_decay = 0.01

def layer_norm(signal, norm_gain, norm_shift):
    centre = signal - lax.optimization_barrier(jnp.mean(signal, axis=-1, keepdims=True))
    variance = lax.optimization_barrier(jnp.mean(centre * centre, axis=-1, keepdims=True))
    return centre * lax.rsqrt(variance + norm_epsilon) * norm_gain + norm_shift

def project(left, right):
    return jnp.dot(left, right, precision=highest)

def forward(segment_in, length, attention, upper, lower, vectors):
    blocks = low(attention).reshape(4, D, D)
    upper_low = low(upper)
    lower_low = low(lower)
    table = low(vectors)
    queries = low(low_back(project(segment_in, blocks[0]) + table[:, 0])).reshape(ROWS, HEADS, HEAD_DIM)
    key_rows = low(low_back(project(segment_in, blocks[1]))).reshape(ROWS, HEADS, HEAD_DIM)
    values = low(low_back(project(segment_in, blocks[2]) + table[:, 1])).reshape(ROWS, HEADS, HEAD_DIM)
    scores = low_back(jnp.einsum('qhe,khe->hqk', queries, key_rows, precision=highest) * HEAD_DIM ** (-0.5))
    position = jnp.arange(ROWS)
    usable = (position < MEM + length) | (position >= MEM + SEG_TOK)
    scores = jnp.where(usable[None, None, :], scores, -1e+30)
    probs = low(jax.nn.softmax(scores, axis=-1))
    context = low(low_back(jnp.einsum('hqk,khe->qhe', probs, values, precision=highest))).reshape(ROWS, D)
    attended = low_back(project(context, blocks[3]) + table[:, 2])
    normed = layer_norm(segment_in + attended, table[:, 3], table[:, 4])
    branch_in = low(low_back(normed))
    bias_hidden = table[:, 8:].T.reshape(FF)
    hidden_pre = low_back(project(branch_in, upper_low) + bias_hidden)
    hidden = low(jax.nn.gelu(hidden_pre, approximate=False))
    branch_out = low_back(jnp.dot(hidden, lower_low.T, precision=highest) + table[:, 7])
    return layer_norm(normed + branch_out, table[:, 5], table[:, 6])

def adam(weight, moment_one, moment_two, gradient, step_rate, decay_rate):
    first_new = beta_first * moment_one + (1.0 - beta_first) * gradient
    second_new = beta_second * moment_two + (1.0 - beta_second) * gradient * gradient
    first_hat = first_new / (1.0 - beta_first ** STEPS)
    second_hat = second_new / (1.0 - beta_second ** STEPS)
    update = first_hat / (jnp.sqrt(second_hat) + adam_epsilon)
    return (weight - step_rate * (update + decay_rate * weight), first_new, second_new)

def reference(tokens, segment_lengths, cotangent, attention_master, attention_mean, attention_square, up_master, up_mean, up_square, down_master, down_mean, down_square, vector_master, vector_mean, vector_square):

    def one_segment(totals, segment_items):
        segment_in, length, grad_out = segment_items

        def segment_fn(signal, attention, upper, lower, vectors):
            return forward(signal, length, attention, upper, lower, vectors)
        segment_out, pullback = jax.vjp(segment_fn, segment_in.astype(jnp.float32), attention_master, up_master, down_master, vector_master)
        gradients = pullback(grad_out.astype(jnp.float32))
        totals = tuple((total + piece for total, piece in zip(totals, gradients[1:])))
        return (totals, (segment_out.astype(jnp.bfloat16), gradients[0]))
    zeros = (jnp.zeros_like(attention_master), jnp.zeros_like(up_master), jnp.zeros_like(down_master), jnp.zeros_like(vector_master))
    totals, (outputs, input_grads) = lax.scan(one_segment, zeros, (tokens, segment_lengths, cotangent))
    attention_new = adam(attention_master, attention_mean, attention_square, totals[0], matrix_rate, weight_decay)
    up_new = adam(up_master, up_mean, up_square, totals[1], matrix_rate, weight_decay)
    down_new = adam(down_master, down_mean, down_square, totals[2], matrix_rate, weight_decay)
    vector_new = adam(vector_master, vector_mean, vector_square, totals[3], vector_rate, 0.0)
    return (outputs, input_grads, attention_new[0], attention_new[1], attention_new[2], up_new[0], up_new[1], up_new[2], down_new[0], down_new[1], down_new[2], vector_new[0], vector_new[1], vector_new[2])
```

```python
import functools

import jax
import jax.numpy as jnp
from jax import lax
from jax.experimental import pallas as pl
from jax.experimental.pallas import tpu as pltpu
from jax.sharding import PartitionSpec as P


HEAD_DIM = 64
MEM = 10
norm_epsilon = 1e-12
inv_root_two = 0.7071067811865476
inv_root_tau = 0.3989422804014327
F32, BF = jnp.float32, jnp.bfloat16
NT = (((1,), (1,)), ((), ()))
TN = (((0,), (0,)), ((), ()))
NN = (((1,), (0,)), ((), ()))

def mm(a, b, dims=NN):
    return lax.dot_general(a, b, dims, preferred_element_type=F32)

def whole(shape=None):
    return pl.BlockSpec(memory_space=pltpu.VMEM)

def norm_stats(signal, width):
    centre = signal - jnp.sum(signal, axis=-1, keepdims=True) * (1.0 / width)
    inverse = lax.rsqrt(jnp.sum(centre * centre, axis=-1, keepdims=True) * (1.0 / width) + norm_epsilon)
    return centre * inverse, inverse

def norm_back(up, scaled, inverse, width):
    return inverse * (up - jnp.sum(up, axis=-1, keepdims=True) * (1.0 / width)
                      - scaled * (jnp.sum(up * scaled, axis=-1, keepdims=True) * (1.0 / width)))

def attn_fwd_kernel(seg_rows, len_ref, x_ref, w_ref, tab_ref, q_ref, k_ref, v_ref, c_ref, n_ref, inv_ref, ab_ref, lse_ref, xs, ct):
    rows, width = xs.shape
    heads = width // HEAD_DIM
    xs[pl.ds(0, seg_rows), :] = x_ref[0]
    xs[pl.ds(seg_rows, rows - seg_rows), :] = jnp.zeros((rows - seg_rows, width), BF)
    x = xs[...]
    q_ref[0] = ((mm(x, w_ref[0]) + tab_ref[0:1, :]).astype(BF) * BF(HEAD_DIM ** -0.5)).astype(BF)
    k_ref[0] = mm(x, w_ref[1]).astype(BF)
    v_ref[0] = (mm(x, w_ref[2]) + tab_ref[1:2, :]).astype(BF)
    live = len_ref[pl.program_id(0)] + MEM
    key_at = lax.broadcasted_iota(jnp.int32, (rows, 1), 0)
    usable = (key_at < live) | ((key_at >= seg_rows - MEM) & (key_at < seg_rows))
    bias = jnp.where(usable, 0.0, -1e30).astype(F32)
    lane = lax.broadcasted_iota(jnp.int32, (rows, 2 * HEAD_DIM), 1)
    zero = jnp.zeros((), BF)

    def pair(i, carry):
        at = pl.ds(pl.multiple_of(i * 2 * HEAD_DIM, 2 * HEAD_DIM), 2 * HEAD_DIM)
        q2, k2, v2 = q_ref[0, :, at], k_ref[0, :, at], v_ref[0, :, at]
        vt = v2.T
        for h in range(2):
            mine = (lane < HEAD_DIM) if h == 0 else (lane >= HEAD_DIM)
            qh = jnp.where(mine, q2, zero)
            s = mm(k2, qh, NT) + bias
            top = jnp.max(s, axis=0, keepdims=True)
            e = jnp.exp(s - top)
            tot = jnp.sum(e, axis=0, keepdims=True)
            p = (e * (1.0 / tot)).astype(BF)
            ct[pl.ds(pl.multiple_of(i * 2 * HEAD_DIM + h * HEAD_DIM, HEAD_DIM), HEAD_DIM), :] = mm(vt[h * HEAD_DIM:(h + 1) * HEAD_DIM], p)
            lse_ref[0, pl.ds(2 * i + h, 1), :] = top + jnp.log(tot)
        return carry
    lax.fori_loop(0, heads // 2, pair, 0)
    c = ct[...].T.astype(BF)
    c_ref[0] = c
    r = x.astype(F32) + mm(c, w_ref[3]) + tab_ref[2:3, :]
    n, inv = norm_stats(r, width)
    n_ref[0] = n
    inv_ref[0] = jnp.broadcast_to(inv, (rows, 128))
    ab_ref[0] = (n * tab_ref[3:4, :] + tab_ref[4:5, :]).astype(BF)

def attn_fwd(lengths, tokens, weights, table):
    segs, seg_rows, width = tokens.shape
    rows = -(-seg_rows // 16) * 16
    heads = width // HEAD_DIM
    hp = -(-heads // 8) * 8
    seg = lambda *s: pl.BlockSpec((1,) + s, lambda i, L: (i,) + (0,) * len(s))
    full = lambda *s: pl.BlockSpec(s, lambda i, L: (0,) * len(s), pipeline_mode=pl.Buffered(1))
    sd = jax.ShapeDtypeStruct
    return pl.pallas_call(
        functools.partial(attn_fwd_kernel, seg_rows),
        grid_spec=pltpu.PrefetchScalarGridSpec(
            num_scalar_prefetch=1, grid=(segs,),
            in_specs=[seg(seg_rows, width), full(*weights.shape), full(*table.shape)],
            out_specs=[seg(rows, width)] * 5 + [seg(rows, 128), seg(rows, width), seg(hp, rows)],
            scratch_shapes=[pltpu.VMEM((rows, width), BF), pltpu.VMEM((width, rows), F32)]),
        out_shape=[sd((segs, rows, width), BF)] * 4 + [sd((segs, rows, width), F32), sd((segs, rows, 128), F32), sd((segs, rows, width), BF), sd((segs, hp, rows), F32)],
        compiler_params=pltpu.CompilerParams(vmem_limit_bytes=56 << 20),
        name="attention_forward",
    )(lengths, tokens, weights, table)

def ffn_kernel(seg_rows, block, ab_ref, n1_ref, inv_ref, cot_ref, up_ref, down_ref, tab_ref,
               out_ref, dr1_ref, dup_ref, ddown_ref, dvec_ref, hid, slope, dy, du):
    segs, rows, width = n1_ref.shape
    total = segs * rows
    chunks = up_ref.shape[0]
    per = rows // block
    nb = total // block
    def rb(i):
        return pl.ds(pl.multiple_of(i * block, block), block)
    y = dr1_ref
    def fwd(i, carry):
        a = ab_ref[rb(i), :]
        acc = jnp.zeros((block, width), F32)
        for j in range(chunks):
            u = mm(a, up_ref[j]) + tab_ref[8 + j:9 + j, :]
            phi = 0.5 * (1.0 + lax.erf(u * inv_root_two))
            h = (u * phi).astype(BF)
            hid[j, rb(i), :] = h
            slope[j, rb(i), :] = phi + u * jnp.exp(-0.5 * u * u) * inv_root_tau
            acc = acc + mm(h, down_ref[j], NT)
        y[rb(i), :] = acc
        return carry
    lax.fori_loop(0, nb, fwd, 0)
    dvec_ref[...] = jnp.zeros_like(dvec_ref)
    for s in range(segs):
        at = pl.ds(s * rows, rows)
        n1 = n1_ref[s]
        r2 = n1 * tab_ref[3:4, :] + tab_ref[4:5, :] + (y[at, :] + tab_ref[7:8, :])
        n2, inv2 = norm_stats(r2, width)
        out_ref[s] = (n2 * tab_ref[5:6, :] + tab_ref[6:7, :])[:seg_rows].astype(BF)
        live = lax.broadcasted_iota(jnp.int32, (rows, 1), 0) < seg_rows
        e = jnp.concatenate([cot_ref[s].astype(F32), jnp.zeros((rows - seg_rows, width), F32)], axis=0)
        dvec_ref[5:6, :] += jnp.sum(e * n2, axis=0, keepdims=True)
        dvec_ref[6:7, :] += jnp.sum(e, axis=0, keepdims=True)
        dr2 = norm_back(e * tab_ref[5:6, :], n2, inv2, width)
        d16 = dr2.astype(BF)
        y[at, :] = dr2
        dy[at, :] = d16
        dvec_ref[7:8, :] += jnp.sum(d16.astype(F32), axis=0, keepdims=True)
    dyt = dy[...].T
    abt = ab_ref[...].T
    for j in range(chunks):
        def back(i, carry):
            g = dy[rb(i), :]
            d = (mm(g, down_ref[j]) * slope[j, rb(i), :]).astype(BF)
            du[rb(i), :] = d
            return carry + jnp.sum(d.astype(F32), axis=0, keepdims=True)
        dvec_ref[8 + j:9 + j, :] = lax.fori_loop(0, nb, back, jnp.zeros((1, width), F32))
        ddown_ref[j] = mm(dyt, hid[j]).astype(BF)
        dup_ref[j] = mm(abt, du[...]).astype(BF)
        def inner(i, carry):
            part = mm(du[rb(i), :], up_ref[j], NT)
            slope[0, rb(i), :] = part if j == 0 else slope[0, rb(i), :] + part
            return carry
        lax.fori_loop(0, nb, inner, 0)
    for s in range(segs):
        at = pl.ds(s * rows, rows)
        da = y[at, :] + slope[0, at, :].astype(BF).astype(F32)
        n1 = n1_ref[s]
        dvec_ref[3:4, :] += jnp.sum(da * n1, axis=0, keepdims=True)
        dvec_ref[4:5, :] += jnp.sum(da, axis=0, keepdims=True)
        dr1 = norm_back(da * tab_ref[3:4, :], n1, inv_ref[s][:, 0:1], width)
        dr1_ref[at, :] = dr1
        dvec_ref[2:3, :] += jnp.sum(dr1.astype(BF).astype(F32), axis=0, keepdims=True)

def ffn(ab, n1, inv, cot, up, down, table):
    segs, rows, width = n1.shape
    seg_rows = cot.shape[1]
    total = segs * rows
    chunks = up.shape[0]
    sd = jax.ShapeDtypeStruct
    return pl.pallas_call(
        functools.partial(ffn_kernel, seg_rows, rows // 2),
        in_specs=[whole()] * 7, out_specs=[whole()] * 5,
        out_shape=[sd(cot.shape, BF), sd((total, width), F32), sd(up.shape, BF), sd(down.shape, BF), sd((16, width), F32)],
        scratch_shapes=[pltpu.VMEM((chunks, total, width), BF), pltpu.VMEM((chunks, total, width), F32), pltpu.VMEM((total, width), BF), pltpu.VMEM((total, width), BF)],
        compiler_params=pltpu.CompilerParams(vmem_limit_bytes=63 << 20),
        name="feed_forward",
    )(ab.reshape(total, width), n1, inv, cot, up, down, table)

def attn_bwd_kernel(seg_rows, len_ref, x_ref, w_ref, q_ref, k_ref, v_ref, c_ref, lse_ref, dr1_ref,
                    ig_ref, dw_ref, dvec_ref, dao, dc, dq, dk, dv, xs):
    segs, rows, width = q_ref.shape
    total = segs * rows
    heads = width // HEAD_DIM
    for s in range(segs):
        xs[pl.ds(s * rows, seg_rows), :] = x_ref[s]
        xs[pl.ds(s * rows + seg_rows, rows - seg_rows), :] = jnp.zeros((rows - seg_rows, width), BF)
    dao[...] = dr1_ref[...].astype(BF)
    dw_ref[3] = mm(c_ref[...].reshape(total, width).T, dao[...]).astype(BF)
    dc[...] = mm(dao[...], w_ref[3], NT).astype(BF)
    key_at = lax.broadcasted_iota(jnp.int32, (rows, 1), 0)
    lane = lax.broadcasted_iota(jnp.int32, (rows, 2 * HEAD_DIM), 1)
    zero = jnp.zeros((), BF)
    for s in range(segs):
        live = len_ref[s] + MEM
        usable = (key_at < live) | ((key_at >= seg_rows - MEM) & (key_at < seg_rows))
        bias = jnp.where(usable, 0.0, -1e30).astype(F32)
        at_rows = pl.ds(s * rows, rows)
        def pair(i, carry):
            at = pl.ds(pl.multiple_of(i * 2 * HEAD_DIM, 2 * HEAD_DIM), 2 * HEAD_DIM)
            q2, k2, v2 = q_ref[s, :, at], k_ref[s, :, at], v_ref[s, :, at]
            g2 = dc[at_rows, at]
            kt = k2.T
            dvp = jnp.zeros((rows, 2 * HEAD_DIM), F32)
            dkp = jnp.zeros((rows, 2 * HEAD_DIM), F32)
            dqt = []
            for h in range(2):
                mine = (lane < HEAD_DIM) if h == 0 else (lane >= HEAD_DIM)
                qh = jnp.where(mine, q2, zero)
                gh = jnp.where(mine, g2, zero)
                p = jnp.exp((mm(k2, qh, NT) + bias) - lse_ref[s, pl.ds(2 * i + h, 1), :])
                dp = mm(v2, gh, NT)
                dvp = dvp + mm(p.astype(BF), gh)
                ds = (p * (dp - jnp.sum(p * dp, axis=0, keepdims=True))).astype(BF)
                dkp = dkp + mm(ds, qh)
                dqt.append(mm(kt[h * HEAD_DIM:(h + 1) * HEAD_DIM], ds))
            dv[at_rows, at] = dvp.astype(BF)
            dk[at_rows, at] = dkp.astype(BF)
            dq[at_rows, at] = (jnp.concatenate(dqt, axis=0).T * (HEAD_DIM ** -0.5)).astype(BF)
            return carry
        lax.fori_loop(0, heads // 2, pair, 0)
    xt = xs[...].T
    dvec_ref[...] = jnp.zeros_like(dvec_ref)
    for j, g in enumerate((dq, dk, dv)):
        dw_ref[j] = mm(xt, g[...]).astype(BF)
    dvec_ref[0:1, :] = jnp.sum(dq[...].astype(F32), axis=0, keepdims=True)
    dvec_ref[1:2, :] = jnp.sum(dv[...].astype(F32), axis=0, keepdims=True)
    for s in range(segs):
        at = pl.ds(s * rows, rows)
        r = dr1_ref[at, :] + mm(dq[at, :], w_ref[0], NT) + mm(dk[at, :], w_ref[1], NT) + mm(dv[at, :], w_ref[2], NT)
        ig_ref[s] = r[:seg_rows]

def attn_bwd(lengths, tokens, weights, q, k, v, c, lse, dr1):
    segs, seg_rows, width = tokens.shape
    rows = q.shape[1]
    total = segs * rows
    sd = jax.ShapeDtypeStruct
    return pl.pallas_call(
        functools.partial(attn_bwd_kernel, seg_rows),
        in_specs=[pl.BlockSpec(memory_space=pltpu.SMEM)] + [whole()] * 8, out_specs=[whole()] * 3,
        out_shape=[sd(tokens.shape, F32), sd(weights.shape, BF), sd((16, width), F32)],
        scratch_shapes=[pltpu.VMEM((total, width), BF)] * 6,
        compiler_params=pltpu.CompilerParams(vmem_limit_bytes=63 << 20),
        name="attention_backward",
    )(lengths, tokens, weights, q, k, v, c, lse, dr1)

MESH = pl.DeviceIdType.MESH
F32, BF = jnp.float32, jnp.bfloat16
DMA = pltpu.SemaphoreType.DMA

def place():
    d, t = lax.axis_index("dp"), lax.axis_index("tensor")
    return d // 2, d % 2, t // 2, t % 2

def dev(z, x, y, c):
    return {"dp": z * 2 + x, "tensor": y * 2 + c}

def greet(z, x, y, c):
    b = pltpu.get_barrier_semaphore()
    for p in [((z + k) % 4, x, y, c) for k in (1, 2, 3)] + [(z, 1 - x, y, c), (z, x, 1 - y, c), (z, x, y, 1 - c)]:
        pl.semaphore_signal(b, inc=1, device_id=dev(*p), device_id_type=MESH)
    pl.semaphore_wait(b, 6)

def pick(ref, order, rows=None, **at):
    idx = tuple(at.get(ch, slice(None)) for ch in order)
    return ref.at[idx + ((rows,) if rows is not None else ())]

def send(src, dst, s, r, p):
    cp = pltpu.make_async_remote_copy(src, dst, s, r, device_id=dev(*p), device_id_type=MESH)
    cp.start()
    return cp

SHAPE = {"z": 4, "x": 2, "y": 2, "c": 2}

def gather_kernel(orders, half, *refs):
    nm = len(orders)
    ins, vec = refs[:nm], refs[nm]
    outs, vouts = refs[nm + 1:2 * nm + 1], refs[2 * nm + 1]
    loc, ssem, zs, xs, ys, cs, vs, vr = refs[2 * nm + 2:]
    z, x, y, c = place()
    greet(z, x, y, c)
    units = [(m, h) for m in range(nm) for h in range(2)]
    rows = lambda h: pl.ds(h * half, half)
    pend, locs, zc = [], [], {}
    for m in range(nm):
        cp = pltpu.make_async_copy(ins[m], pick(outs[m], orders[m], z=z, x=x, y=y, c=c), loc.at[m]); cp.start(); locs.append(cp)
    cp = pltpu.make_async_copy(vec, vouts.at[z, x], loc.at[nm]); cp.start(); locs.append(cp)
    vz = []
    for k in (1, 2, 3):
        cp = send(vec, vouts.at[z, x], vs.at[k - 1], vr.at[k - 1], ((z + k) % 4, x, y, c)); vz.append(cp); pend.append(cp)
    for u, (m, h) in enumerate(units):
        for k in (1, 2, 3):
            cp = send(ins[m].at[rows(h)], pick(outs[m], orders[m], rows(h), z=z, x=x, y=y, c=c), ssem.at[u, k - 1], zs.at[u, k - 1], ((z + k) % 4, x, y, c))
            zc[u, k] = cp; pend.append(cp)
    for cp in locs:
        cp.wait()
    for cp in vz:
        cp.wait_recv()
    vx = send(vouts.at[:, x], vouts.at[:, x], vs.at[3], vr.at[3], (z, 1 - x, y, c)); pend.append(vx)
    def st1(u):
        m, h = units[u]
        for k in (1, 2, 3):
            zc[u, k].wait_recv()
        src = pick(outs[m], orders[m], rows(h), x=x, y=y, c=c)
        p = (z, 1 - x, y, c) if h == 0 else (z, x, 1 - y, c)
        a = send(src, src, ssem.at[u, 3], xs.at[u], p)
        b = send(src, src, ssem.at[u, 4], cs.at[u, 0], (z, x, y, 1 - c))
        pend.extend((a, b))
        return a, b
    def st2(u, a):
        m, h = units[u]
        a.wait_recv()
        if h == 0:
            src, fresh, p = pick(outs[m], orders[m], rows(h), y=y, c=c), pick(outs[m], orders[m], rows(h), x=1 - x, y=y, c=c), (z, x, 1 - y, c)
        else:
            src, fresh, p = pick(outs[m], orders[m], rows(h), x=x, c=c), pick(outs[m], orders[m], rows(h), x=x, y=1 - y, c=c), (z, 1 - x, y, c)
        a2 = send(src, src, ssem.at[u, 5], ys.at[u], p)
        b2 = send(fresh, fresh, ssem.at[u, 6], cs.at[u, 1], (z, x, y, 1 - c))
        pend.extend((a2, b2))
        return a2, b2
    def st3(u, a2):
        m, h = units[u]
        a2.wait_recv()
        src = pick(outs[m], orders[m], rows(h), **({"y": 1 - y} if h == 0 else {"x": 1 - x}), c=c)
        b3 = send(src, src, ssem.at[u, 7], cs.at[u, 2], (z, x, y, 1 - c))
        pend.append(b3)
        return b3
    n = len(units)
    A, B, A2, B2, B3 = {}, {}, {}, {}, {}
    lag = 2
    for s in range(n + 2 * lag):
        if s < n:
            A[s], B[s] = st1(s)
        if 0 <= s - lag < n:
            A2[s - lag], B2[s - lag] = st2(s - lag, A[s - lag])
        if 0 <= s - 2 * lag < n:
            B3[s - 2 * lag] = st3(s - 2 * lag, A2[s - 2 * lag])
    vx.wait_recv()
    for u in range(n):
        for q in (B[u], B2[u], B3[u]):
            q.wait_recv()
    for cp in pend:
        cp.wait_send()

def gather(orders, shards, vec):
    nm = len(shards)
    rows, width = shards[0].shape
    nu = 2 * nm
    any_ = pl.BlockSpec(memory_space=pl.ANY)
    return pl.pallas_call(
        functools.partial(gather_kernel, orders, rows // 2),
        out_shape=[jax.ShapeDtypeStruct(tuple(SHAPE[ch] for ch in o) + (rows, width), s.dtype) for o, s in zip(orders, shards)] + [jax.ShapeDtypeStruct((4, 2) + vec.shape, vec.dtype)],
        in_specs=[any_] * (nm + 1), out_specs=[any_] * (nm + 1),
        scratch_shapes=[DMA((nm + 1,)), DMA((nu, 8)), DMA((nu, 3)), DMA((nu,)), DMA((nu,)), DMA((nu, 3)), DMA((4,)), DMA((4,))],
        compiler_params=pltpu.CompilerParams(collective_id=0, has_side_effects=True),
        name="gather_weights",
    )(*shards, vec)

def scatter_kernel(orders, half, *refs):
    nm = len(orders)
    ins, vec = refs[:nm], refs[nm]
    outs, vout = refs[nm + 1:2 * nm + 1], refs[2 * nm + 1]
    rest = refs[2 * nm + 2:]
    own, rc = rest[:nm], rest[nm:2 * nm]
    r1 = rest[2 * nm:4 * nm]
    r2, rz, vbuf, lsem, ssem, rsem, vs, vr = rest[4 * nm:]
    z, x, y, c = place()
    me = dict(z=z, x=x, y=y, c=c)
    greet(z, x, y, c)
    units = [(m, h) for m in range(nm) for h in range(2)]
    n = len(units)
    rows = lambda h: pl.ds(h * half, half)
    inner = [o.replace("c", "") for o in orders]
    pend = []
    core, xp, yp = (z, x, y, 1 - c), (z, 1 - x, y, c), (z, x, 1 - y, c)
    L, C0, C1, C2, C3 = {}, {}, {}, {}, {}
    for u, (m, h) in enumerate(units):
        C0[u] = send(pick(ins[m], orders[m], rows(h), c=1 - c), rc[m].at[h], ssem.at[u, 0], rsem.at[u, 0], core)
        L[u] = pltpu.make_async_copy(pick(ins[m], orders[m], rows(h), c=c), own[m].at[h], lsem.at[u])
        L[u].start()
        pend.append(C0[u])
    vbuf[0] = vec[...]
    V0 = send(vbuf.at[0], vbuf.at[1], vs.at[0], vr.at[0], core)

    def first(h):
        return "y" if h == 0 else "x"
    def second(h):
        return "x" if h == 0 else "y"
    def st1(u):
        m, h = units[u]
        C0[u].wait_recv()
        L[u].wait()
        o, r, dims = own[m].at[h], rc[m].at[h], inner[m]
        sh = [SHAPE[ch] for ch in dims]
        def body(i, _):
            at = (i // (sh[1] * sh[2]), (i // sh[2]) % sh[1], i % sh[2])
            o[at] = (o[at].astype(F32) + r[at].astype(F32)).astype(BF)
            return 0
        lax.fori_loop(0, sh[0] * sh[1] * sh[2], body, 0)
        f = first(h)
        C1[u] = send(pick(o, dims, **{f: 1 - me[f]}), r1[u], ssem.at[u, 1], rsem.at[u, 1], yp if h == 0 else xp)
        pend.append(C1[u])
    def st2(u):
        m, h = units[u]
        C1[u].wait_recv()
        f, s = first(h), second(h)
        o = pick(own[m].at[h], inner[m], **{f: me[f]})
        left = inner[m].replace(f, "")
        sh = [SHAPE[ch] for ch in left]
        def body(i, _):
            at = (i // sh[1], i % sh[1])
            o[at] = (o[at].astype(F32) + r1[u][at].astype(F32)).astype(BF)
            return 0
        lax.fori_loop(0, 8, body, 0)
        C2[u] = send(pick(o, left, **{s: 1 - me[s]}), r2.at[u], ssem.at[u, 2], rsem.at[u, 2], xp if h == 0 else yp)
        pend.append(C2[u])
    def st3(u):
        m, h = units[u]
        C2[u].wait_recv()
        o = pick(own[m].at[h], inner[m], x=x, y=y)
        def body(i, _):
            o[i] = (o[i].astype(F32) + r2[u, i].astype(F32)).astype(BF)
            return 0
        lax.fori_loop(0, 4, body, 0)
        for k in (1, 2, 3):
            C3[u, k] = send(o.at[(z + k) % 4], rz.at[u, k - 1], ssem.at[u, 2 + k], rsem.at[u, 2 + k], ((z + k) % 4, x, y, c))
            pend.append(C3[u, k])
    def st4(u):
        m, h = units[u]
        for k in (1, 2, 3):
            C3[u, k].wait_recv()
        o = pick(own[m].at[h], inner[m], x=x, y=y)
        outs[m][rows(h)] = ((o[z].astype(F32) + rz[u, 0].astype(F32)) + rz[u, 1].astype(F32)) + rz[u, 2].astype(F32)
    vstage = []
    def v1():
        V0.wait_recv()
        vbuf[0] = vbuf[0] + vbuf[1]
    steps = n + 3
    vq = {}
    lag = (0, 1, 2, 3)
    for s in range(n + 3):
        for k, st in enumerate((st1, st2, st3, st4)):
            u = s - k
            if 0 <= u < n:
                st(u)
        if s == 0:
            V0.wait_recv(); V0.wait_send()
            vbuf[0] = vbuf[0] + vbuf[1]
            vq["y"] = send(vbuf.at[0], vbuf.at[2], vs.at[1], vr.at[1], yp)
        if s == 1:
            vq["y"].wait_recv(); vq["y"].wait_send()
            vbuf[0] = vbuf[0] + vbuf[2]
            vq["x"] = send(vbuf.at[0], vbuf.at[3], vs.at[2], vr.at[2], xp)
        if s == 2:
            vq["x"].wait_recv(); vq["x"].wait_send()
            vbuf[4 + z] = vbuf[0] + vbuf[3]
            for k in (1, 2, 3):
                vq[k] = send(vbuf.at[4 + z], vbuf.at[4 + z], vs.at[2 + k], vr.at[2 + k], ((z + k) % 4, x, y, c))
        if s == 3:
            for k in (1, 2, 3):
                vq[k].wait_recv()
            vout[...] = ((vbuf[4] + vbuf[5]) + vbuf[6]) + vbuf[7]
            pend.extend(vq[k] for k in (1, 2, 3))
    for cp in pend:
        cp.wait_send()

def scatter(orders, grads, vec):
    nm = len(grads)
    rows, width = grads[0].shape[-2:]
    half = rows // 2
    nu = 2 * nm
    any_ = pl.BlockSpec(memory_space=pl.ANY)
    vm = pl.BlockSpec(memory_space=pltpu.VMEM)
    shp = lambda o: tuple(SHAPE[ch] for ch in o.replace("c", ""))
    st = [pltpu.VMEM((2,) + shp(o) + (half, width), BF) for o in orders]
    return pl.pallas_call(
        functools.partial(scatter_kernel, orders, half),
        out_shape=[jax.ShapeDtypeStruct((rows, width), F32)] * nm + [jax.ShapeDtypeStruct(vec.shape, F32)],
        in_specs=[any_] * nm + [vm], out_specs=[vm] * (nm + 1),
        scratch_shapes=st + st + [*[pltpu.VMEM((4, 2, half, width), BF) if (h == 0 or o == "zxyc") else pltpu.VMEM((2, 4, half, width), BF) for o in orders for h in range(2)], pltpu.VMEM((nu, 4, half, width), BF), pltpu.VMEM((nu, 3, half, width), BF), pltpu.VMEM((8,) + vec.shape, F32),
            DMA((nu,)), DMA((nu, 6)), DMA((nu, 6)), DMA((6,)), DMA((6,))],
        compiler_params=pltpu.CompilerParams(collective_id=1, has_side_effects=True, vmem_limit_bytes=56 << 20),
        name="scatter_sums",
    )(*grads, vec)

STEPS = 5
beta_first = 0.9
beta_second = 0.999
adam_epsilon = 1e-08
matrix_rate = 0.06
vector_rate = 0.2
weight_decay = 0.01
ORDERS = ("zxyc", "yczx", "yczx")


def adam(weight, moment_one, moment_two, gradient, step_rate, decay_rate):
    first_new = beta_first * moment_one + (1.0 - beta_first) * gradient
    second_new = beta_second * moment_two + (1.0 - beta_second) * gradient * gradient
    first_hat = first_new / (1.0 - beta_first**STEPS)
    second_hat = second_new / (1.0 - beta_second**STEPS)
    update = first_hat / (jnp.sqrt(second_hat) + adam_epsilon)
    return (weight - step_rate * (update + decay_rate * weight), first_new, second_new)


def shards(
    own_plan,
    tokens,
    segment_lengths,
    cotangent,
    attention_master,
    attention_mean,
    attention_square,
    up_master,
    up_mean,
    up_square,
    down_master,
    down_mean,
    down_square,
    vector_master,
    vector_mean,
    vector_square,
):
    width = tokens.shape[2]
    dp_count, tensor_count = lax.axis_size("dp"), lax.axis_size("tensor")
    part, columns = vector_master.shape
    spare = 16 - columns
    low = [m.astype(BF) for m in (attention_master, up_master, down_master)]
    vec_low = vector_master.astype(BF).T
    if own_plan:
        piece = jnp.pad(vec_low, ((0, spare), (0, 128 - part)))
        w_all, up_all, down_all, pieces = gather(ORDERS, low, piece)
        table = pieces.reshape(dp_count, 16, 128)[:, :, :part].transpose(1, 0, 2).reshape(16, width).astype(F32)
    else:
        w_all = lax.all_gather(low[0], ("dp", "tensor"), axis=0, tiled=True)
        up_all, down_all = (lax.all_gather(m, ("tensor", "dp"), axis=0, tiled=True) for m in low[1:])
        rows = lax.all_gather(vec_low, "dp", axis=1, tiled=True).astype(F32)
        table = jnp.pad(rows, ((0, spare), (0, 0)))
    w_all = w_all.reshape(4, width, width)
    up_all = up_all.reshape(tensor_count, width, width)
    down_all = down_all.reshape(tensor_count, width, width)

    q, k, v, c, n1, inv, ab, lse = attn_fwd(segment_lengths, tokens, w_all, table)
    block_output, dr1, d_up, d_down, dvec_ffn = ffn(ab, n1, inv, cotangent, up_all, down_all, table)
    input_grad, d_attention, dvec_att = attn_bwd(segment_lengths, tokens, w_all, q, k, v, c, lse, dr1)
    d_vec = dvec_ffn + dvec_att

    if own_plan:
        cut = lambda g, order: g.reshape(tuple(SHAPE[ch] for ch in order) + (g.shape[0] * width // (dp_count * tensor_count), width))
        grads = [cut(g, o) for g, o in zip((d_attention, d_up, d_down), ORDERS)]
        s_attention, s_up, s_down, s_vec = scatter(ORDERS, grads, d_vec)
        s_vec = lax.dynamic_slice_in_dim(s_vec, lax.axis_index("dp") * part, part, axis=1)
    else:
        flat = lambda g: g.astype(F32).reshape(-1, width)
        s_attention = lax.psum_scatter(flat(d_attention), ("dp", "tensor"), scatter_dimension=0, tiled=True)
        s_up, s_down = (lax.psum_scatter(flat(g), ("tensor", "dp"), scatter_dimension=0, tiled=True) for g in (d_up, d_down))
        s_vec = lax.psum(lax.psum_scatter(d_vec, "dp", scatter_dimension=1, tiled=True), "tensor")
    s_vec = s_vec[:columns].T

    attention_new = adam(attention_master, attention_mean, attention_square, s_attention, matrix_rate, weight_decay)
    up_new = adam(up_master, up_mean, up_square, s_up, matrix_rate, weight_decay)
    down_new = adam(down_master, down_mean, down_square, s_down, matrix_rate, weight_decay)
    vector_new = adam(vector_master, vector_mean, vector_square, s_vec, vector_rate, 0.0)
    return (block_output, input_grad, *attention_new, *up_new, *down_new, *vector_new)


def solution(mesh):
    rows, cols = P(("dp", "tensor")), P("dp", "tensor")
    own_plan = mesh.shape["dp"] == 8 and mesh.shape["tensor"] == 4
    return jax.shard_map(
        functools.partial(shards, own_plan),
        mesh=mesh,
        in_specs=(rows,) * 6 + (cols,) * 6 + (P("dp"),) * 3,
        out_specs=(rows,) * 5 + (cols,) * 6 + (P("dp"),) * 3,
        check_vma=False,
    )
```

```python
import functools

import jax
import jax.numpy as jnp
from jax import lax
from jax.experimental import pallas as pl
from jax.experimental.pallas import tpu as pltpu
from jax.sharding import PartitionSpec as P


HEAD_DIM = 64
MEM = 10
norm_epsilon = 1e-12
inv_root_two = 0.7071067811865476
inv_root_tau = 0.3989422804014327
F32, BF = jnp.float32, jnp.bfloat16
NT = (((1,), (1,)), ((), ()))
TN = (((0,), (0,)), ((), ()))
NN = (((1,), (0,)), ((), ()))

def mm(a, b, dims=NN):
    return lax.dot_general(a, b, dims, preferred_element_type=F32)

def whole(shape=None):
    return pl.BlockSpec(memory_space=pltpu.VMEM)

def norm_stats(signal, width):
    centre = signal - jnp.sum(signal, axis=-1, keepdims=True) * (1.0 / width)
    inverse = lax.rsqrt(jnp.sum(centre * centre, axis=-1, keepdims=True) * (1.0 / width) + norm_epsilon)
    return centre * inverse, inverse

def norm_back(up, scaled, inverse, width):
    return inverse * (up - jnp.sum(up, axis=-1, keepdims=True) * (1.0 / width)
                      - scaled * (jnp.sum(up * scaled, axis=-1, keepdims=True) * (1.0 / width)))

def attn_fwd_kernel(seg_rows, len_ref, x_ref, w_ref, tab_ref, q_ref, k_ref, v_ref, c_ref, n_ref, inv_ref, ab_ref, lse_ref, xs, ct):
    rows, width = xs.shape
    heads = width // HEAD_DIM
    xs[pl.ds(0, seg_rows), :] = x_ref[0]
    xs[pl.ds(seg_rows, rows - seg_rows), :] = jnp.zeros((rows - seg_rows, width), BF)
    x = xs[...]
    q_ref[0] = ((mm(x, w_ref[0]) + tab_ref[0:1, :]).astype(BF) * BF(HEAD_DIM ** -0.5)).astype(BF)
    k_ref[0] = mm(x, w_ref[1]).astype(BF)
    v_ref[0] = (mm(x, w_ref[2]) + tab_ref[1:2, :]).astype(BF)
    live = len_ref[pl.program_id(0)] + MEM
    key_at = lax.broadcasted_iota(jnp.int32, (rows, 1), 0)
    usable = (key_at < live) | ((key_at >= seg_rows - MEM) & (key_at < seg_rows))
    bias = jnp.where(usable, 0.0, -1e30).astype(F32)
    lane = lax.broadcasted_iota(jnp.int32, (rows, 2 * HEAD_DIM), 1)
    zero = jnp.zeros((), BF)

    def pair(i, carry):
        at = pl.ds(pl.multiple_of(i * 2 * HEAD_DIM, 2 * HEAD_DIM), 2 * HEAD_DIM)
        q2, k2, v2 = q_ref[0, :, at], k_ref[0, :, at], v_ref[0, :, at]
        vt = v2.T
        for h in range(2):
            mine = (lane < HEAD_DIM) if h == 0 else (lane >= HEAD_DIM)
            qh = jnp.where(mine, q2, zero)
            s = mm(k2, qh, NT) + bias
            top = jnp.max(s, axis=0, keepdims=True)
            e = jnp.exp(s - top)
            tot = jnp.sum(e, axis=0, keepdims=True)
            p = (e * (1.0 / tot)).astype(BF)
            ct[pl.ds(pl.multiple_of(i * 2 * HEAD_DIM + h * HEAD_DIM, HEAD_DIM), HEAD_DIM), :] = mm(vt[h * HEAD_DIM:(h + 1) * HEAD_DIM], p)
            lse_ref[0, pl.ds(2 * i + h, 1), :] = top + jnp.log(tot)
        return carry
    lax.fori_loop(0, heads // 2, pair, 0)
    c = ct[...].T.astype(BF)
    c_ref[0] = c
    r = x.astype(F32) + mm(c, w_ref[3]) + tab_ref[2:3, :]
    n, inv = norm_stats(r, width)
    n_ref[0] = n
    inv_ref[0] = jnp.broadcast_to(inv, (rows, 128))
    ab_ref[0] = (n * tab_ref[3:4, :] + tab_ref[4:5, :]).astype(BF)

def attn_fwd(lengths, tokens, weights, table):
    segs, seg_rows, width = tokens.shape
    rows = -(-seg_rows // 16) * 16
    heads = width // HEAD_DIM
    hp = -(-heads // 8) * 8
    seg = lambda *s: pl.BlockSpec((1,) + s, lambda i, L: (i,) + (0,) * len(s))
    full = lambda *s: pl.BlockSpec(s, lambda i, L: (0,) * len(s), pipeline_mode=pl.Buffered(1))
    sd = jax.ShapeDtypeStruct
    return pl.pallas_call(
        functools.partial(attn_fwd_kernel, seg_rows),
        grid_spec=pltpu.PrefetchScalarGridSpec(
            num_scalar_prefetch=1, grid=(segs,),
            in_specs=[seg(seg_rows, width), full(*weights.shape), full(*table.shape)],
            out_specs=[seg(rows, width)] * 5 + [seg(rows, 128), seg(rows, width), seg(hp, rows)],
            scratch_shapes=[pltpu.VMEM((rows, width), BF), pltpu.VMEM((width, rows), F32)]),
        out_shape=[sd((segs, rows, width), BF)] * 4 + [sd((segs, rows, width), F32), sd((segs, rows, 128), F32), sd((segs, rows, width), BF), sd((segs, hp, rows), F32)],
        compiler_params=pltpu.CompilerParams(vmem_limit_bytes=56 << 20),
        name="attention_forward",
    )(lengths, tokens, weights, table)

def ffn_kernel(seg_rows, block, ab_ref, n1_ref, inv_ref, cot_ref, up_ref, down_ref, tab_ref,
               out_ref, dr1_ref, dup_ref, ddown_ref, dvec_ref, hid, slope, dy, du):
    segs, rows, width = n1_ref.shape
    total = segs * rows
    chunks = up_ref.shape[0]
    per = rows // block
    nb = total // block
    def rb(i):
        return pl.ds(pl.multiple_of(i * block, block), block)
    y = dr1_ref
    def fwd(i, carry):
        a = ab_ref[rb(i), :]
        acc = jnp.zeros((block, width), F32)
        for j in range(chunks):
            u = mm(a, up_ref[j]) + tab_ref[8 + j:9 + j, :]
            phi = 0.5 * (1.0 + lax.erf(u * inv_root_two))
            h = (u * phi).astype(BF)
            hid[j, rb(i), :] = h
            slope[j, rb(i), :] = phi + u * jnp.exp(-0.5 * u * u) * inv_root_tau
            acc = acc + mm(h, down_ref[j], NT)
        y[rb(i), :] = acc
        return carry
    lax.fori_loop(0, nb, fwd, 0)
    dvec_ref[...] = jnp.zeros_like(dvec_ref)
    for s in range(segs):
        at = pl.ds(s * rows, rows)
        n1 = n1_ref[s]
        r2 = n1 * tab_ref[3:4, :] + tab_ref[4:5, :] + (y[at, :] + tab_ref[7:8, :])
        n2, inv2 = norm_stats(r2, width)
        out_ref[s] = (n2 * tab_ref[5:6, :] + tab_ref[6:7, :])[:seg_rows].astype(BF)
        live = lax.broadcasted_iota(jnp.int32, (rows, 1), 0) < seg_rows
        e = jnp.concatenate([cot_ref[s].astype(F32), jnp.zeros((rows - seg_rows, width), F32)], axis=0)
        dvec_ref[5:6, :] += jnp.sum(e * n2, axis=0, keepdims=True)
        dvec_ref[6:7, :] += jnp.sum(e, axis=0, keepdims=True)
        dr2 = norm_back(e * tab_ref[5:6, :], n2, inv2, width)
        d16 = dr2.astype(BF)
        y[at, :] = dr2
        dy[at, :] = d16
        dvec_ref[7:8, :] += jnp.sum(d16.astype(F32), axis=0, keepdims=True)
    dyt = dy[...].T
    abt = ab_ref[...].T
    for j in range(chunks):
        def back(i, carry):
            g = dy[rb(i), :]
            d = (mm(g, down_ref[j]) * slope[j, rb(i), :]).astype(BF)
            du[rb(i), :] = d
            return carry + jnp.sum(d.astype(F32), axis=0, keepdims=True)
        dvec_ref[8 + j:9 + j, :] = lax.fori_loop(0, nb, back, jnp.zeros((1, width), F32))
        ddown_ref[j] = mm(dyt, hid[j]).astype(BF)
        dup_ref[j] = mm(abt, du[...]).astype(BF)
        def inner(i, carry):
            part = mm(du[rb(i), :], up_ref[j], NT)
            slope[0, rb(i), :] = part if j == 0 else slope[0, rb(i), :] + part
            return carry
        lax.fori_loop(0, nb, inner, 0)
    for s in range(segs):
        at = pl.ds(s * rows, rows)
        da = y[at, :] + slope[0, at, :].astype(BF).astype(F32)
        n1 = n1_ref[s]
        dvec_ref[3:4, :] += jnp.sum(da * n1, axis=0, keepdims=True)
        dvec_ref[4:5, :] += jnp.sum(da, axis=0, keepdims=True)
        dr1 = norm_back(da * tab_ref[3:4, :], n1, inv_ref[s][:, 0:1], width)
        dr1_ref[at, :] = dr1
        dvec_ref[2:3, :] += jnp.sum(dr1.astype(BF).astype(F32), axis=0, keepdims=True)

def ffn(ab, n1, inv, cot, up, down, table):
    segs, rows, width = n1.shape
    seg_rows = cot.shape[1]
    total = segs * rows
    chunks = up.shape[0]
    sd = jax.ShapeDtypeStruct
    return pl.pallas_call(
        functools.partial(ffn_kernel, seg_rows, rows // 2),
        in_specs=[whole()] * 7, out_specs=[whole()] * 5,
        out_shape=[sd(cot.shape, BF), sd((total, width), F32), sd(up.shape, BF), sd(down.shape, BF), sd((16, width), F32)],
        scratch_shapes=[pltpu.VMEM((chunks, total, width), BF), pltpu.VMEM((chunks, total, width), F32), pltpu.VMEM((total, width), BF), pltpu.VMEM((total, width), BF)],
        compiler_params=pltpu.CompilerParams(vmem_limit_bytes=63 << 20),
        name="feed_forward",
    )(ab.reshape(total, width), n1, inv, cot, up, down, table)

def attn_bwd_kernel(seg_rows, len_ref, x_ref, w_ref, q_ref, k_ref, v_ref, c_ref, lse_ref, dr1_ref,
                    ig_ref, dw_ref, dvec_ref, dao, dc, dq, dk, dv, xs):
    segs, rows, width = q_ref.shape
    total = segs * rows
    heads = width // HEAD_DIM
    for s in range(segs):
        xs[pl.ds(s * rows, seg_rows), :] = x_ref[s]
        xs[pl.ds(s * rows + seg_rows, rows - seg_rows), :] = jnp.zeros((rows - seg_rows, width), BF)
    dao[...] = dr1_ref[...].astype(BF)
    dw_ref[3] = mm(c_ref[...].reshape(total, width).T, dao[...]).astype(BF)
    dc[...] = mm(dao[...], w_ref[3], NT).astype(BF)
    key_at = lax.broadcasted_iota(jnp.int32, (rows, 1), 0)
    lane = lax.broadcasted_iota(jnp.int32, (rows, 2 * HEAD_DIM), 1)
    zero = jnp.zeros((), BF)
    for s in range(segs):
        live = len_ref[s] + MEM
        usable = (key_at < live) | ((key_at >= seg_rows - MEM) & (key_at < seg_rows))
        bias = jnp.where(usable, 0.0, -1e30).astype(F32)
        at_rows = pl.ds(s * rows, rows)
        def pair(i, carry):
            at = pl.ds(pl.multiple_of(i * 2 * HEAD_DIM, 2 * HEAD_DIM), 2 * HEAD_DIM)
            q2, k2, v2 = q_ref[s, :, at], k_ref[s, :, at], v_ref[s, :, at]
            g2 = dc[at_rows, at]
            kt = k2.T
            dvp = jnp.zeros((rows, 2 * HEAD_DIM), F32)
            dkp = jnp.zeros((rows, 2 * HEAD_DIM), F32)
            dqt = []
            for h in range(2):
                mine = (lane < HEAD_DIM) if h == 0 else (lane >= HEAD_DIM)
                qh = jnp.where(mine, q2, zero)
                gh = jnp.where(mine, g2, zero)
                p = jnp.exp((mm(k2, qh, NT) + bias) - lse_ref[s, pl.ds(2 * i + h, 1), :])
                dp = mm(v2, gh, NT)
                dvp = dvp + mm(p.astype(BF), gh)
                ds = (p * (dp - jnp.sum(p * dp, axis=0, keepdims=True))).astype(BF)
                dkp = dkp + mm(ds, qh)
                dqt.append(mm(kt[h * HEAD_DIM:(h + 1) * HEAD_DIM], ds))
            dv[at_rows, at] = dvp.astype(BF)
            dk[at_rows, at] = dkp.astype(BF)
            dq[at_rows, at] = (jnp.concatenate(dqt, axis=0).T * (HEAD_DIM ** -0.5)).astype(BF)
            return carry
        lax.fori_loop(0, heads // 2, pair, 0)
    xt = xs[...].T
    dvec_ref[...] = jnp.zeros_like(dvec_ref)
    for j, g in enumerate((dq, dk, dv)):
        dw_ref[j] = mm(xt, g[...]).astype(BF)
    dvec_ref[0:1, :] = jnp.sum(dq[...].astype(F32), axis=0, keepdims=True)
    dvec_ref[1:2, :] = jnp.sum(dv[...].astype(F32), axis=0, keepdims=True)
    for s in range(segs):
        at = pl.ds(s * rows, rows)
        r = dr1_ref[at, :] + mm(dq[at, :], w_ref[0], NT) + mm(dk[at, :], w_ref[1], NT) + mm(dv[at, :], w_ref[2], NT)
        ig_ref[s] = r[:seg_rows]

def attn_bwd(lengths, tokens, weights, q, k, v, c, lse, dr1):
    segs, seg_rows, width = tokens.shape
    rows = q.shape[1]
    total = segs * rows
    sd = jax.ShapeDtypeStruct
    return pl.pallas_call(
        functools.partial(attn_bwd_kernel, seg_rows),
        in_specs=[pl.BlockSpec(memory_space=pltpu.SMEM)] + [whole()] * 8, out_specs=[whole()] * 3,
        out_shape=[sd(tokens.shape, F32), sd(weights.shape, BF), sd((16, width), F32)],
        scratch_shapes=[pltpu.VMEM((total, width), BF)] * 6,
        compiler_params=pltpu.CompilerParams(vmem_limit_bytes=63 << 20),
        name="attention_backward",
    )(lengths, tokens, weights, q, k, v, c, lse, dr1)

MESH = pl.DeviceIdType.MESH
F32, BF = jnp.float32, jnp.bfloat16
DMA = pltpu.SemaphoreType.DMA

def place():
    d, t = lax.axis_index("dp"), lax.axis_index("tensor")
    return d // 2, d % 2, t // 2, t % 2

def dev(z, x, y, c):
    return {"dp": z * 2 + x, "tensor": y * 2 + c}

def greet(z, x, y, c):
    b = pltpu.get_barrier_semaphore()
    for p in [((z + k) % 4, x, y, c) for k in (1, 2, 3)] + [(z, 1 - x, y, c), (z, x, 1 - y, c), (z, x, y, 1 - c)]:
        pl.semaphore_signal(b, inc=1, device_id=dev(*p), device_id_type=MESH)
    pl.semaphore_wait(b, 6)

def pick(ref, order, rows=None, **at):
    idx = tuple(at.get(ch, slice(None)) for ch in order)
    return ref.at[idx + ((rows,) if rows is not None else ())]

def send(src, dst, s, r, p):
    cp = pltpu.make_async_remote_copy(src, dst, s, r, device_id=dev(*p), device_id_type=MESH)
    cp.start()
    return cp

SHAPE = {"z": 4, "x": 2, "y": 2, "c": 2}

def gather_kernel(orders, half, *refs):
    nm = len(orders)
    ins, vec = refs[:nm], refs[nm]
    outs, vouts = refs[nm + 1:2 * nm + 1], refs[2 * nm + 1]
    loc, ssem, zs, xs, ys, cs, vs, vr = refs[2 * nm + 2:]
    z, x, y, c = place()
    greet(z, x, y, c)
    units = [(m, h) for m in range(nm) for h in range(2)]
    rows = lambda h: pl.ds(h * half, half)
    pend, locs, zc = [], [], {}
    for m in range(nm):
        cp = pltpu.make_async_copy(ins[m], pick(outs[m], orders[m], z=z, x=x, y=y, c=c), loc.at[m]); cp.start(); locs.append(cp)
    cp = pltpu.make_async_copy(vec, vouts.at[z, x], loc.at[nm]); cp.start(); locs.append(cp)
    vz = []
    for k in (1, 2, 3):
        cp = send(vec, vouts.at[z, x], vs.at[k - 1], vr.at[k - 1], ((z + k) % 4, x, y, c)); vz.append(cp); pend.append(cp)
    for u, (m, h) in enumerate(units):
        for k in (1, 2, 3):
            cp = send(ins[m].at[rows(h)], pick(outs[m], orders[m], rows(h), z=z, x=x, y=y, c=c), ssem.at[u, k - 1], zs.at[u, k - 1], ((z + k) % 4, x, y, c))
            zc[u, k] = cp; pend.append(cp)
    for cp in locs:
        cp.wait()
    for cp in vz:
        cp.wait_recv()
    vx = send(vouts.at[:, x], vouts.at[:, x], vs.at[3], vr.at[3], (z, 1 - x, y, c)); pend.append(vx)
    def st1(u):
        m, h = units[u]
        for k in (1, 2, 3):
            zc[u, k].wait_recv()
        src = pick(outs[m], orders[m], rows(h), x=x, y=y, c=c)
        p = (z, 1 - x, y, c) if h == 0 else (z, x, 1 - y, c)
        a = send(src, src, ssem.at[u, 3], xs.at[u], p)
        b = send(src, src, ssem.at[u, 4], cs.at[u, 0], (z, x, y, 1 - c))
        pend.extend((a, b))
        return a, b
    def st2(u, a):
        m, h = units[u]
        a.wait_recv()
        if h == 0:
            src, fresh, p = pick(outs[m], orders[m], rows(h), y=y, c=c), pick(outs[m], orders[m], rows(h), x=1 - x, y=y, c=c), (z, x, 1 - y, c)
        else:
            src, fresh, p = pick(outs[m], orders[m], rows(h), x=x, c=c), pick(outs[m], orders[m], rows(h), x=x, y=1 - y, c=c), (z, 1 - x, y, c)
        a2 = send(src, src, ssem.at[u, 5], ys.at[u], p)
        b2 = send(fresh, fresh, ssem.at[u, 6], cs.at[u, 1], (z, x, y, 1 - c))
        pend.extend((a2, b2))
        return a2, b2
    def st3(u, a2):
        m, h = units[u]
        a2.wait_recv()
        src = pick(outs[m], orders[m], rows(h), **({"y": 1 - y} if h == 0 else {"x": 1 - x}), c=c)
        b3 = send(src, src, ssem.at[u, 7], cs.at[u, 2], (z, x, y, 1 - c))
        pend.append(b3)
        return b3
    n = len(units)
    A, B, A2, B2, B3 = {}, {}, {}, {}, {}
    lag = 2
    for s in range(n + 2 * lag):
        if s < n:
            A[s], B[s] = st1(s)
        if 0 <= s - lag < n:
            A2[s - lag], B2[s - lag] = st2(s - lag, A[s - lag])
        if 0 <= s - 2 * lag < n:
            B3[s - 2 * lag] = st3(s - 2 * lag, A2[s - 2 * lag])
    vx.wait_recv()
    for u in range(n):
        for q in (B[u], B2[u], B3[u]):
            q.wait_recv()
    for cp in pend:
        cp.wait_send()

def gather(orders, shards, vec):
    nm = len(shards)
    rows, width = shards[0].shape
    nu = 2 * nm
    any_ = pl.BlockSpec(memory_space=pl.ANY)
    return pl.pallas_call(
        functools.partial(gather_kernel, orders, rows // 2),
        out_shape=[jax.ShapeDtypeStruct(tuple(SHAPE[ch] for ch in o) + (rows, width), s.dtype) for o, s in zip(orders, shards)] + [jax.ShapeDtypeStruct((4, 2) + vec.shape, vec.dtype)],
        in_specs=[any_] * (nm + 1), out_specs=[any_] * (nm + 1),
        scratch_shapes=[DMA((nm + 1,)), DMA((nu, 8)), DMA((nu, 3)), DMA((nu,)), DMA((nu,)), DMA((nu, 3)), DMA((4,)), DMA((4,))],
        compiler_params=pltpu.CompilerParams(collective_id=0, has_side_effects=True),
        name="gather_weights",
    )(*shards, vec)

def scatter_kernel(orders, half, *refs):
    nm = len(orders)
    ins, vec = refs[:nm], refs[nm]
    outs, vout = refs[nm + 1:2 * nm + 1], refs[2 * nm + 1]
    rest = refs[2 * nm + 2:]
    own, rc = rest[:nm], rest[nm:2 * nm]
    r1 = rest[2 * nm:4 * nm]
    r2, rz, vbuf, lsem, ssem, rsem, vs, vr = rest[4 * nm:]
    z, x, y, c = place()
    me = dict(z=z, x=x, y=y, c=c)
    greet(z, x, y, c)
    units = [(m, h) for m in range(nm) for h in range(2)]
    n = len(units)
    rows = lambda h: pl.ds(h * half, half)
    inner = [o.replace("c", "") for o in orders]
    pend = []
    core, xp, yp = (z, x, y, 1 - c), (z, 1 - x, y, c), (z, x, 1 - y, c)
    L, C0, C1, C2, C3 = {}, {}, {}, {}, {}
    for u, (m, h) in enumerate(units):
        C0[u] = send(pick(ins[m], orders[m], rows(h), c=1 - c), rc[m].at[h], ssem.at[u, 0], rsem.at[u, 0], core)
        L[u] = pltpu.make_async_copy(pick(ins[m], orders[m], rows(h), c=c), own[m].at[h], lsem.at[u])
        L[u].start()
        pend.append(C0[u])
    vbuf[0] = vec[...]
    V0 = send(vbuf.at[0], vbuf.at[1], vs.at[0], vr.at[0], core)

    def first(h):
        return "y" if h == 0 else "x"
    def second(h):
        return "x" if h == 0 else "y"
    def st1(u):
        m, h = units[u]
        C0[u].wait_recv()
        L[u].wait()
        o, r, dims = own[m].at[h], rc[m].at[h], inner[m]
        sh = [SHAPE[ch] for ch in dims]
        def body(i, _):
            at = (i // (sh[1] * sh[2]), (i // sh[2]) % sh[1], i % sh[2])
            o[at] = (o[at].astype(F32) + r[at].astype(F32)).astype(BF)
            return 0
        lax.fori_loop(0, sh[0] * sh[1] * sh[2], body, 0)
        f = first(h)
        C1[u] = send(pick(o, dims, **{f: 1 - me[f]}), r1[u], ssem.at[u, 1], rsem.at[u, 1], yp if h == 0 else xp)
        pend.append(C1[u])
    def st2(u):
        m, h = units[u]
        C1[u].wait_recv()
        f, s = first(h), second(h)
        o = pick(own[m].at[h], inner[m], **{f: me[f]})
        left = inner[m].replace(f, "")
        sh = [SHAPE[ch] for ch in left]
        def body(i, _):
            at = (i // sh[1], i % sh[1])
            o[at] = (o[at].astype(F32) + r1[u][at].astype(F32)).astype(BF)
            return 0
        lax.fori_loop(0, 8, body, 0)
        C2[u] = send(pick(o, left, **{s: 1 - me[s]}), r2.at[u], ssem.at[u, 2], rsem.at[u, 2], xp if h == 0 else yp)
        pend.append(C2[u])
    def st3(u):
        m, h = units[u]
        C2[u].wait_recv()
        o = pick(own[m].at[h], inner[m], x=x, y=y)
        def body(i, _):
            o[i] = (o[i].astype(F32) + r2[u, i].astype(F32)).astype(BF)
            return 0
        lax.fori_loop(0, 4, body, 0)
        for k in (1, 2, 3):
            C3[u, k] = send(o.at[(z + k) % 4], rz.at[u, k - 1], ssem.at[u, 2 + k], rsem.at[u, 2 + k], ((z + k) % 4, x, y, c))
            pend.append(C3[u, k])
    def st4(u):
        m, h = units[u]
        for k in (1, 2, 3):
            C3[u, k].wait_recv()
        o = pick(own[m].at[h], inner[m], x=x, y=y)
        outs[m][rows(h)] = ((o[z].astype(F32) + rz[u, 0].astype(F32)) + rz[u, 1].astype(F32)) + rz[u, 2].astype(F32)
    vstage = []
    def v1():
        V0.wait_recv()
        vbuf[0] = vbuf[0] + vbuf[1]
    steps = n + 3
    vq = {}
    lag = (0, 1, 2, 3)
    for s in range(n + 3):
        for k, st in enumerate((st1, st2, st3, st4)):
            u = s - k
            if 0 <= u < n:
                st(u)
        if s == 0:
            V0.wait_recv(); V0.wait_send()
            vbuf[0] = vbuf[0] + vbuf[1]
            vq["y"] = send(vbuf.at[0], vbuf.at[2], vs.at[1], vr.at[1], yp)
        if s == 1:
            vq["y"].wait_recv(); vq["y"].wait_send()
            vbuf[0] = vbuf[0] + vbuf[2]
            vq["x"] = send(vbuf.at[0], vbuf.at[3], vs.at[2], vr.at[2], xp)
        if s == 2:
            vq["x"].wait_recv(); vq["x"].wait_send()
            vbuf[4 + z] = vbuf[0] + vbuf[3]
            for k in (1, 2, 3):
                vq[k] = send(vbuf.at[4 + z], vbuf.at[4 + z], vs.at[2 + k], vr.at[2 + k], ((z + k) % 4, x, y, c))
        if s == 3:
            for k in (1, 2, 3):
                vq[k].wait_recv()
            vout[...] = ((vbuf[4] + vbuf[5]) + vbuf[6]) + vbuf[7]
            pend.extend(vq[k] for k in (1, 2, 3))
    for cp in pend:
        cp.wait_send()

def scatter(orders, grads, vec):
    nm = len(grads)
    rows, width = grads[0].shape[-2:]
    half = rows // 2
    nu = 2 * nm
    any_ = pl.BlockSpec(memory_space=pl.ANY)
    vm = pl.BlockSpec(memory_space=pltpu.VMEM)
    shp = lambda o: tuple(SHAPE[ch] for ch in o.replace("c", ""))
    st = [pltpu.VMEM((2,) + shp(o) + (half, width), BF) for o in orders]
    return pl.pallas_call(
        functools.partial(scatter_kernel, orders, half),
        out_shape=[jax.ShapeDtypeStruct((rows, width), F32)] * nm + [jax.ShapeDtypeStruct(vec.shape, F32)],
        in_specs=[any_] * nm + [vm], out_specs=[vm] * (nm + 1),
        scratch_shapes=st + st + [*[pltpu.VMEM((4, 2, half, width), BF) if (h == 0 or o == "zxyc") else pltpu.VMEM((2, 4, half, width), BF) for o in orders for h in range(2)], pltpu.VMEM((nu, 4, half, width), BF), pltpu.VMEM((nu, 3, half, width), BF), pltpu.VMEM((8,) + vec.shape, F32),
            DMA((nu,)), DMA((nu, 6)), DMA((nu, 6)), DMA((6,)), DMA((6,))],
        compiler_params=pltpu.CompilerParams(collective_id=1, has_side_effects=True, vmem_limit_bytes=56 << 20),
        name="scatter_sums",
    )(*grads, vec)


class Legs:
    def __init__(self, ssem, rsem):
        self.ssem, self.rsem, self.make, self.count = ssem, rsem, {}, 0

    def add(self, key, src, dst, peer):
        i = self.count
        self.count += 1
        self.make[key] = lambda: pltpu.make_async_remote_copy(
            src(), dst(), self.ssem.at[i], self.rsem.at[i], device_id=dev(*peer), device_id_type=MESH)

    def start(self, *keys):
        for k in keys:
            self.make[k]().start()

    def got(self, *keys):
        for k in keys:
            self.make[k]().wait_recv()

    def sent(self, *keys):
        for k in keys:
            self.make[k]().wait_send()

def add_spread(legs, key, view, place_now, h):
    z, x, y, c = place_now
    core, xp, yp = (z, x, y, 1 - c), (z, 1 - x, y, c), (z, x, 1 - y, c)
    def leg(name, peer, **at):
        legs.add((key, name), lambda: view(**at), lambda: view(**at), peer)
    leg("s1", xp if h == 0 else yp, x=x, y=y, c=c)
    leg("k1", core, x=x, y=y, c=c)
    if h == 0:
        leg("s2", yp, y=y, c=c)
        leg("k2", core, x=1 - x, y=y, c=c)
        leg("k3", core, y=1 - y, c=c)
    else:
        leg("s2", xp, x=x, c=c)
        leg("k2", core, x=x, y=1 - y, c=c)
        leg("k3", core, x=1 - x, c=c)

N_FORWARD_LEGS = 3 * 3 + 4 + 6 * 5 + 2 * 5 + 4 * 3 + 4 * 5

def forward_kernel(seg_rows, len_ref, tok, cot, am, um, dm, vp,
                   out_o, q_o, k_o, v_o, c_o, w_o, dr1_o, dup_o, ddn_o, lse_ref, dvec_ref,
                   wa, wu, wd, vec, tab, traw, craw, xs, cs, q, k, v, ct, cc, n1, inv, ab, hid, slo, dy, dyt, abt,
                   ssem, rsem, lsem):
    segs, rows, width = q_o.shape
    total = segs * rows
    heads = width // HEAD_DIM
    part = am.shape[0]
    z, x, y, c = here = place()
    peers_z = {i: ((z + i) % 4, x, y, c) for i in (1, 2, 3)}
    lt = pltpu.make_async_copy(tok, traw, lsem.at[0]); lt.start()
    lc = pltpu.make_async_copy(cot, craw, lsem.at[1]); lc.start()
    wa[z, x, y, c] = am[...].astype(BF)
    wu[y, c, z, x] = um[...].astype(BF)
    wd[y, c, z, x] = dm[...].astype(BF)
    vec[z, x] = vp[...]

    legs = Legs(ssem, rsem)
    pair_w = 2 * HEAD_DIM
    groups = width // (2 * pair_w)
    for g in range(groups):
        col = pl.ds(g * 2 * pair_w, 2 * pair_w)
        for i in (1, 2, 3):
            f = functools.partial(lambda col: wa.at[z, x, y, c, :, col], col)
            legs.add(("z", g, i), f, f, peers_z[i])
    for i in (1, 2, 3):
        legs.add(("vz", i), lambda: vec.at[z, x], lambda: vec.at[z, x], peers_z[i])
    legs.add("vx", lambda: vec.at[:, x], lambda: vec.at[:, x], (z, 1 - x, y, c))
    three = pl.ds(0, 3)
    def att_view(zz, col):
        return lambda **at: pick(wa, "zxycr", z=zz, **at).at[(Ellipsis,)] if False else wa.at[tuple([zz] + [at.get(ch, slice(None)) for ch in "xyc"] + [slice(None), col])]
    for g in range(groups):
        for h in range(2):
            add_spread(legs, ("a", g, h), att_view(three, pl.ds((2 * g + h) * pair_w, pair_w)), here, h)
    for h in range(2):
        add_spread(legs, ("o", h), att_view(3, pl.ds(h * (width // 2), width // 2)), here, h)
    half = part // 2
    for name, ref in (("u", wu), ("d", wd)):
        for h in range(2):
            rr = pl.ds(h * half, half)
            f = functools.partial(lambda ref, rr: ref.at[y, c, z, x, rr], ref, rr)
            for i in (1, 2, 3):
                legs.add((name, h, "z", i), f, f, peers_z[i])
            view = functools.partial(lambda ref, rr, **at: ref.at[tuple([at.get(ch, slice(None)) for ch in "yczx"] + [rr])], ref, rr)
            add_spread(legs, (name, h), view, here, h)

    def stage(units, n):
        for u in units:
            if n == 2:
                legs.got((u, "s1"))
                legs.start((u, "s2"), (u, "k2"))
            elif n == 3:
                legs.got((u, "s2"))
                legs.start((u, "k3"))
            elif n == 1:
                legs.start((u, "s1"), (u, "k1"))
            elif n == 4:
                legs.got((u, "k1"), (u, "k2"), (u, "k3"))
    A = lambda g: [("a", g, 0), ("a", g, 1)]
    O = [("o", 0), ("o", 1)]
    U, W = [("u", 0), ("u", 1)], [("d", 0), ("d", 1)]
    def zstart(name):
        for h in range(2):
            legs.start(*[(name, h, "z", i) for i in (1, 2, 3)])
    def zgot(name):
        for h in range(2):
            legs.got(*[(name, h, "z", i) for i in (1, 2, 3)])

    greet(*here)
    legs.start(*[("z", 0, i) for i in (1, 2, 3)])
    legs.start(*[("vz", i) for i in (1, 2, 3)])
    for g in range(1, groups):
        legs.start(*[("z", g, i) for i in (1, 2, 3)])
    lt.wait()
    for s in range(segs):
        xs[pl.ds(s * rows, seg_rows), :] = traw[s]
        xs[pl.ds(s * rows + seg_rows, rows - seg_rows), :] = jnp.zeros((rows - seg_rows, width), BF)
    legs.got(*[("z", 0, i) for i in (1, 2, 3)])
    stage(A(0), 1)
    lc.wait()
    for s in range(segs):
        cs[pl.ds(s * rows, seg_rows), :] = craw[s]
        cs[pl.ds(s * rows + seg_rows, rows - seg_rows), :] = jnp.zeros((rows - seg_rows, width), BF)
    legs.got(*[("z", 1, i) for i in (1, 2, 3)])
    stage(A(1), 1)
    stage(A(0), 2)
    legs.got(*[("vz", i) for i in (1, 2, 3)])
    legs.start("vx")
    legs.got(*[("z", 2, i) for i in (1, 2, 3)])
    stage(A(2), 1)
    zstart("u")
    stage(A(1), 2)
    stage(A(0), 3)
    legs.got("vx")
    lane_in = lax.broadcasted_iota(jnp.int32, (128, width), 0)
    lane_out = lax.broadcasted_iota(jnp.int32, (128, width), 1)
    acc = jnp.zeros((16, width), F32)
    for d in range(8):
        move = ((lane_out == lane_in + d * part) & (lane_in < part)).astype(BF)
        acc = acc + mm(vec[d // 2, d % 2], move)
    tab[...] = acc
    ticks = {
        1: lambda: (stage(A(2), 2), stage(A(1), 3)),
        2: lambda: (stage(O, 1), stage(A(2), 3)),
        3: lambda: (stage(O, 2), zgot("u"), stage(U, 1)),
        5: lambda: (stage(O, 3), stage(U, 2), zstart("d")),
        8: lambda: (zgot("d"), stage(W, 1)),
        9: lambda: stage(U, 3),
        11: lambda: stage(W, 2),
    }
    lane = lax.broadcasted_iota(jnp.int32, (rows, pair_w), 1)
    key_at = lax.broadcasted_iota(jnp.int32, (rows, 1), 0)
    zero = jnp.zeros((), BF)

    def body(it, carry):
        for n, f in ticks.items():
            pl.when(it == n)(lambda f=f: (f(), None)[1])
        for g in range(groups):
            pl.when(it == 4 * g)(lambda g=g: (stage(A(g), 4), None)[1])
        g = it // 4

        @pl.when(it % 4 == 0)
        def _():
            col = pl.ds(pl.multiple_of(g * 2 * pair_w, 2 * pair_w), 2 * pair_w)
            w3 = [wa[m, :, :, :, :, col].reshape(width, 2 * pair_w) for m in range(3)]
            xx = xs[...]
            q[:, col] = ((mm(xx, w3[0]) + tab[0:1, col]).astype(BF) * BF(HEAD_DIM ** -0.5)).astype(BF)
            k[:, col] = mm(xx, w3[1]).astype(BF)
            v[:, col] = (mm(xx, w3[2]) + tab[1:2, col]).astype(BF)

        s = (it // 2) % 2
        i = 2 * g + it % 2
        col = pl.ds(pl.multiple_of(i * pair_w, pair_w), pair_w)
        rr = pl.ds(pl.multiple_of(s * rows, 16), rows)
        live = len_ref[s] + MEM
        usable = (key_at < live) | ((key_at >= seg_rows - MEM) & (key_at < seg_rows))
        bias = jnp.where(usable, 0.0, -1e30).astype(F32)
        q2, k2, v2 = q[rr, col], k[rr, col], v[rr, col]
        vt = v2.T
        for h in range(2):
            mine = (lane < HEAD_DIM) if h == 0 else (lane >= HEAD_DIM)
            sc = mm(k2, jnp.where(mine, q2, zero), NT) + bias
            top = jnp.max(sc, axis=0, keepdims=True)
            e = jnp.exp(sc - top)
            tot = jnp.sum(e, axis=0, keepdims=True)
            p = (e * (1.0 / tot)).astype(BF)
            at = pl.ds(pl.multiple_of(i * pair_w + h * HEAD_DIM, HEAD_DIM), HEAD_DIM)
            ct[s, at, :] = mm(vt[h * HEAD_DIM:(h + 1) * HEAD_DIM], p).astype(BF)
            lse_ref[s, pl.ds(2 * i + h, 1), :] = top + jnp.log(tot)
        return carry
    lax.fori_loop(0, 4 * groups, body, 0)

    spill = [pltpu.make_async_copy(a.at[pl.ds(s * rows, rows)], o.at[s], lsem.at[2 + 2 * n + s]) for n, (a, o) in enumerate(((q, q_o), (k, k_o), (v, v_o))) for s in range(segs)]
    for cp in spill:
        cp.start()
    stage(O, 4)
    wcopy = pltpu.make_async_copy(wa, w_o, lsem.at[8]); wcopy.start()
    for s in range(segs):
        rr = pl.ds(s * rows, rows)
        cs_ = ct[s].T
        cc[rr, :] = cs_
        r = xs[rr, :].astype(F32) + mm(cs_, wa[3].reshape(width, width)) + tab[2:3, :]
        n, iv = norm_stats(r, width)
        n1[rr, :] = n
        inv[rr, :] = jnp.broadcast_to(iv, (rows, 128))
        ab[rr, :] = (n * tab[3:4, :] + tab[4:5, :]).astype(BF)
    ccopy = [pltpu.make_async_copy(cc.at[pl.ds(s * rows, rows)], c_o.at[s], lsem.at[9 + s]) for s in range(segs)]
    for cp in ccopy:
        cp.start()

    block = rows // 2
    nb = total // block
    chunks = 4
    def rb(i):
        return pl.ds(pl.multiple_of(i * block, 16), block)
    def up(j):
        return wu[j // 2, j % 2].reshape(width, width)
    def down(j):
        return wd[j // 2, j % 2].reshape(width, width)
    stage(U, 4)
    def fwd(i, carry):
        pl.when(i == 2)(lambda: (stage(W, 3), None)[1])
        a = ab[rb(i), :]
        for j in range(chunks):
            u = mm(a, up(j)) + tab[8 + j:9 + j, :]
            phi = 0.5 * (1.0 + lax.erf(u * inv_root_two))
            hid[j, rb(i), :] = (u * phi).astype(BF)
            slo[j, rb(i), :] = (phi + u * jnp.exp(-0.5 * u * u) * inv_root_tau).astype(BF)
        return carry
    lax.fori_loop(0, nb, fwd, 0)
    stage(W, 4)
    dvec_ref[...] = jnp.zeros_like(dvec_ref)
    def mid(i, carry):
        yy = tab[7:8, :]
        for j in range(chunks):
            yy = yy + mm(hid[j, rb(i), :], down(j), NT)
        nn = n1[rb(i), :]
        r2 = nn * tab[3:4, :] + tab[4:5, :] + yy
        n2, inv2 = norm_stats(r2, width)
        e = cs[rb(i), :].astype(F32)
        cs[rb(i), :] = (n2 * tab[5:6, :] + tab[6:7, :]).astype(BF)
        dvec_ref[5:6, :] += jnp.sum(e * n2, axis=0, keepdims=True)
        dvec_ref[6:7, :] += jnp.sum(e, axis=0, keepdims=True)
        dr2 = norm_back(e * tab[5:6, :], n2, inv2, width)
        g16 = dr2.astype(BF)
        dy[rb(i), :] = g16
        dvec_ref[7:8, :] += jnp.sum(g16.astype(F32), axis=0, keepdims=True)
        da = jnp.zeros((block, width), F32)
        for j in range(chunks):
            d16 = (mm(g16, down(j)) * slo[j, rb(i), :].astype(F32)).astype(BF)
            slo[j, rb(i), :] = d16
            dvec_ref[8 + j:9 + j, :] += jnp.sum(d16.astype(F32), axis=0, keepdims=True)
            da = da + mm(d16, up(j), NT)
        da = dr2 + da.astype(BF).astype(F32)
        dvec_ref[3:4, :] += jnp.sum(da * nn, axis=0, keepdims=True)
        dvec_ref[4:5, :] += jnp.sum(da, axis=0, keepdims=True)
        dr1 = norm_back(da * tab[3:4, :], nn, inv[rb(i), 0:1], width)
        n1[rb(i), :] = dr1
        dvec_ref[2:3, :] += jnp.sum(dr1.astype(BF).astype(F32), axis=0, keepdims=True)
        return carry
    lax.fori_loop(0, nb, mid, 0)
    dcopy = pltpu.make_async_copy(n1, dr1_o, lsem.at[0]); dcopy.start()
    for s in range(segs):
        craw[s] = cs[pl.ds(s * rows, seg_rows), :]
    ocopy = pltpu.make_async_copy(craw, out_o, lsem.at[1]); ocopy.start()
    dyt[...] = dy[...].T
    abt[...] = ab[...].T
    legs.sent(*legs.make)
    def grad_copies(j):
        return (pltpu.make_async_copy(wd.at[j // 2, j % 2], ddn_o.at[j // 2, j % 2], lsem.at[11 + 2 * (j % 2)]),
                pltpu.make_async_copy(wu.at[j // 2, j % 2], dup_o.at[j // 2, j % 2], lsem.at[12 + 2 * (j % 2)]))
    def grads(j, carry):
        shape = wd.shape[2:]
        @pl.when(j >= 2)
        def _():
            for cp in grad_copies(j - 2):
                cp.wait()
        wd[j // 2, j % 2] = mm(dyt[...], hid[j]).astype(BF).reshape(shape)
        wu[j // 2, j % 2] = mm(abt[...], slo[j]).astype(BF).reshape(shape)
        for cp in grad_copies(j):
            cp.start()
        return carry
    lax.fori_loop(0, chunks, grads, 0)
    for j in (2, 3):
        for cp in grad_copies(j):
            cp.wait()
    for cp in spill + [wcopy, dcopy, ocopy] + ccopy:
        cp.wait()

def forward(lengths, tokens, cotangent, att, up, down, piece):
    segs, seg_rows, width = tokens.shape
    part = att.shape[0]
    rows = -(-seg_rows // 16) * 16
    total = segs * rows
    hp = -(-(width // HEAD_DIM) // 8) * 8
    sd = jax.ShapeDtypeStruct
    any_, vm = pl.BlockSpec(memory_space=pl.ANY), whole()
    wshape, fshape = (4, 2, 2, 2, part, width), (2, 2, 4, 2, part, width)
    V = lambda *s, t=BF: pltpu.VMEM(s, t)
    return pl.pallas_call(
        functools.partial(forward_kernel, seg_rows),
        in_specs=[pl.BlockSpec(memory_space=pltpu.SMEM), any_, any_, vm, vm, vm, vm],
        out_specs=[any_] * 9 + [vm, vm],
        out_shape=[sd(cotangent.shape, BF)] + [sd((segs, rows, width), BF)] * 4 + [sd(wshape, BF), sd((total, width), F32), sd(fshape, BF), sd(fshape, BF), sd((segs, hp, rows), F32), sd((16, width), F32)],
        scratch_shapes=[V(*wshape), V(*fshape), V(*fshape), V(4, 2, 16, 128), V(16, width, t=F32), V(segs, seg_rows, width), V(segs, seg_rows, width),
                        V(total, width), V(total, width), V(total, width), V(total, width), V(total, width), V(segs, width, rows), V(total, width),
                        V(total, width, t=F32), V(total, 128, t=F32), V(total, width), V(4, total, width), V(4, total, width), V(total, width), V(width, total), V(width, total),
                        DMA((N_FORWARD_LEGS,)), DMA((N_FORWARD_LEGS,)), DMA((15,))],
        compiler_params=pltpu.CompilerParams(collective_id=0, has_side_effects=True, vmem_limit_bytes=63 << 20),
        name="forward_and_feed_forward_backward",
    )(lengths, tokens, cotangent, att, up, down, piece)

STEPS = 5
beta_first = 0.9
beta_second = 0.999
adam_epsilon = 1e-08
matrix_rate = 0.06
vector_rate = 0.2
weight_decay = 0.01
ORDERS = ("zxyc", "yczx", "yczx")


def adam(weight, moment_one, moment_two, gradient, step_rate, decay_rate):
    first_new = beta_first * moment_one + (1.0 - beta_first) * gradient
    second_new = beta_second * moment_two + (1.0 - beta_second) * gradient * gradient
    first_hat = first_new / (1.0 - beta_first**STEPS)
    second_hat = second_new / (1.0 - beta_second**STEPS)
    update = first_hat / (jnp.sqrt(second_hat) + adam_epsilon)
    return (weight - step_rate * (update + decay_rate * weight), first_new, second_new)


def shards(
    own_plan,
    tokens,
    segment_lengths,
    cotangent,
    attention_master,
    attention_mean,
    attention_square,
    up_master,
    up_mean,
    up_square,
    down_master,
    down_mean,
    down_square,
    vector_master,
    vector_mean,
    vector_square,
):
    width = tokens.shape[2]
    dp_count, tensor_count = lax.axis_size("dp"), lax.axis_size("tensor")
    part, columns = vector_master.shape
    spare = 16 - columns
    vec_low = vector_master.astype(BF).T
    if own_plan:
        piece = jnp.pad(vec_low, ((0, spare), (0, 128 - part)))
        block_output, q, k, v, c, w_all, dr1, d_up, d_down, lse, dvec_ffn = forward(
            segment_lengths, tokens, cotangent, attention_master, up_master, down_master, piece
        )
        w_all = w_all.reshape(4, width, width)
    else:
        low = [m.astype(BF) for m in (attention_master, up_master, down_master)]
        w_all = lax.all_gather(low[0], ("dp", "tensor"), axis=0, tiled=True)
        up_all, down_all = (lax.all_gather(m, ("tensor", "dp"), axis=0, tiled=True) for m in low[1:])
        rows = lax.all_gather(vec_low, "dp", axis=1, tiled=True).astype(F32)
        table = jnp.pad(rows, ((0, spare), (0, 0)))
        w_all = w_all.reshape(4, width, width)
        up_all = up_all.reshape(tensor_count, width, width)
        down_all = down_all.reshape(tensor_count, width, width)
        q, k, v, c, n1, inv, ab, lse = attn_fwd(segment_lengths, tokens, w_all, table)
        block_output, dr1, d_up, d_down, dvec_ffn = ffn(ab, n1, inv, cotangent, up_all, down_all, table)
    input_grad, d_attention, dvec_att = attn_bwd(segment_lengths, tokens, w_all, q, k, v, c, lse, dr1)
    d_vec = dvec_ffn + dvec_att

    if own_plan:
        cut = lambda g, order: g.reshape(tuple(SHAPE[ch] for ch in order) + (4 * width // (dp_count * tensor_count), width))
        grads = [cut(g, o) for g, o in zip((d_attention, d_up, d_down), ORDERS)]
        s_attention, s_up, s_down, s_vec = scatter(ORDERS, grads, d_vec)
        s_vec = lax.dynamic_slice_in_dim(s_vec, lax.axis_index("dp") * part, part, axis=1)
    else:
        flat = lambda g: g.astype(F32).reshape(-1, width)
        s_attention = lax.psum_scatter(flat(d_attention), ("dp", "tensor"), scatter_dimension=0, tiled=True)
        s_up, s_down = (lax.psum_scatter(flat(g), ("tensor", "dp"), scatter_dimension=0, tiled=True) for g in (d_up, d_down))
        s_vec = lax.psum(lax.psum_scatter(d_vec, "dp", scatter_dimension=1, tiled=True), "tensor")
    s_vec = s_vec[:columns].T

    attention_new = adam(attention_master, attention_mean, attention_square, s_attention, matrix_rate, weight_decay)
    up_new = adam(up_master, up_mean, up_square, s_up, matrix_rate, weight_decay)
    down_new = adam(down_master, down_mean, down_square, s_down, matrix_rate, weight_decay)
    vector_new = adam(vector_master, vector_mean, vector_square, s_vec, vector_rate, 0.0)
    return (block_output, input_grad, *attention_new, *up_new, *down_new, *vector_new)


def solution(mesh):
    rows, cols = P(("dp", "tensor")), P("dp", "tensor")
    own_plan = mesh.shape["dp"] == 8 and mesh.shape["tensor"] == 4
    return jax.shard_map(
        functools.partial(shards, own_plan),
        mesh=mesh,
        in_specs=(rows,) * 6 + (cols,) * 6 + (P("dp"),) * 3,
        out_specs=(rows,) * 5 + (cols,) * 6 + (P("dp"),) * 3,
        check_vma=False,
    )
```

```python
import functools

import jax
import jax.numpy as jnp
from jax import lax
from jax.experimental import pallas as pl
from jax.experimental.pallas import tpu as pltpu
from jax.sharding import PartitionSpec as P


HEAD_DIM = 64
MEM = 10
norm_epsilon = 1e-12
inv_root_two = 0.7071067811865476
inv_root_tau = 0.3989422804014327
F32, BF = jnp.float32, jnp.bfloat16
NT = (((1,), (1,)), ((), ()))
TN = (((0,), (0,)), ((), ()))
NN = (((1,), (0,)), ((), ()))

def mm(a, b, dims=NN):
    return lax.dot_general(a, b, dims, preferred_element_type=F32)

def whole(shape=None):
    return pl.BlockSpec(memory_space=pltpu.VMEM)

def norm_stats(signal, width):
    centre = signal - jnp.sum(signal, axis=-1, keepdims=True) * (1.0 / width)
    inverse = lax.rsqrt(jnp.sum(centre * centre, axis=-1, keepdims=True) * (1.0 / width) + norm_epsilon)
    return centre * inverse, inverse

def norm_back(up, scaled, inverse, width):
    return inverse * (up - jnp.sum(up, axis=-1, keepdims=True) * (1.0 / width)
                      - scaled * (jnp.sum(up * scaled, axis=-1, keepdims=True) * (1.0 / width)))

def attn_fwd_kernel(seg_rows, len_ref, x_ref, w_ref, tab_ref, q_ref, k_ref, v_ref, c_ref, n_ref, inv_ref, ab_ref, lse_ref, xs, ct):
    rows, width = xs.shape
    heads = width // HEAD_DIM
    xs[pl.ds(0, seg_rows), :] = x_ref[0]
    xs[pl.ds(seg_rows, rows - seg_rows), :] = jnp.zeros((rows - seg_rows, width), BF)
    x = xs[...]
    q_ref[0] = ((mm(x, w_ref[0]) + tab_ref[0:1, :]).astype(BF) * BF(HEAD_DIM ** -0.5)).astype(BF)
    k_ref[0] = mm(x, w_ref[1]).astype(BF)
    v_ref[0] = (mm(x, w_ref[2]) + tab_ref[1:2, :]).astype(BF)
    live = len_ref[pl.program_id(0)] + MEM
    key_at = lax.broadcasted_iota(jnp.int32, (rows, 1), 0)
    usable = (key_at < live) | ((key_at >= seg_rows - MEM) & (key_at < seg_rows))
    bias = jnp.where(usable, 0.0, -1e30).astype(F32)
    lane = lax.broadcasted_iota(jnp.int32, (rows, 2 * HEAD_DIM), 1)
    zero = jnp.zeros((), BF)

    def pair(i, carry):
        at = pl.ds(pl.multiple_of(i * 2 * HEAD_DIM, 2 * HEAD_DIM), 2 * HEAD_DIM)
        q2, k2, v2 = q_ref[0, :, at], k_ref[0, :, at], v_ref[0, :, at]
        vt = v2.T
        for h in range(2):
            mine = (lane < HEAD_DIM) if h == 0 else (lane >= HEAD_DIM)
            qh = jnp.where(mine, q2, zero)
            s = mm(k2, qh, NT) + bias
            top = jnp.max(s, axis=0, keepdims=True)
            e = jnp.exp(s - top)
            tot = jnp.sum(e, axis=0, keepdims=True)
            p = (e * (1.0 / tot)).astype(BF)
            ct[pl.ds(pl.multiple_of(i * 2 * HEAD_DIM + h * HEAD_DIM, HEAD_DIM), HEAD_DIM), :] = mm(vt[h * HEAD_DIM:(h + 1) * HEAD_DIM], p)
            lse_ref[0, pl.ds(2 * i + h, 1), :] = top + jnp.log(tot)
        return carry
    lax.fori_loop(0, heads // 2, pair, 0)
    c = ct[...].T.astype(BF)
    c_ref[0] = c
    r = x.astype(F32) + mm(c, w_ref[3]) + tab_ref[2:3, :]
    n, inv = norm_stats(r, width)
    n_ref[0] = n
    inv_ref[0] = jnp.broadcast_to(inv, (rows, 128))
    ab_ref[0] = (n * tab_ref[3:4, :] + tab_ref[4:5, :]).astype(BF)

def attn_fwd(lengths, tokens, weights, table):
    segs, seg_rows, width = tokens.shape
    rows = -(-seg_rows // 16) * 16
    heads = width // HEAD_DIM
    hp = -(-heads // 8) * 8
    seg = lambda *s: pl.BlockSpec((1,) + s, lambda i, L: (i,) + (0,) * len(s))
    full = lambda *s: pl.BlockSpec(s, lambda i, L: (0,) * len(s), pipeline_mode=pl.Buffered(1))
    sd = jax.ShapeDtypeStruct
    return pl.pallas_call(
        functools.partial(attn_fwd_kernel, seg_rows),
        grid_spec=pltpu.PrefetchScalarGridSpec(
            num_scalar_prefetch=1, grid=(segs,),
            in_specs=[seg(seg_rows, width), full(*weights.shape), full(*table.shape)],
            out_specs=[seg(rows, width)] * 5 + [seg(rows, 128), seg(rows, width), seg(hp, rows)],
            scratch_shapes=[pltpu.VMEM((rows, width), BF), pltpu.VMEM((width, rows), F32)]),
        out_shape=[sd((segs, rows, width), BF)] * 4 + [sd((segs, rows, width), F32), sd((segs, rows, 128), F32), sd((segs, rows, width), BF), sd((segs, hp, rows), F32)],
        compiler_params=pltpu.CompilerParams(vmem_limit_bytes=56 << 20),
        name="attention_forward",
    )(lengths, tokens, weights, table)

def ffn_kernel(seg_rows, block, ab_ref, n1_ref, inv_ref, cot_ref, up_ref, down_ref, tab_ref,
               out_ref, dr1_ref, dup_ref, ddown_ref, dvec_ref, hid, slope, dy, du):
    segs, rows, width = n1_ref.shape
    total = segs * rows
    chunks = up_ref.shape[0]
    per = rows // block
    nb = total // block
    def rb(i):
        return pl.ds(pl.multiple_of(i * block, block), block)
    y = dr1_ref
    def fwd(i, carry):
        a = ab_ref[rb(i), :]
        acc = jnp.zeros((block, width), F32)
        for j in range(chunks):
            u = mm(a, up_ref[j]) + tab_ref[8 + j:9 + j, :]
            phi = 0.5 * (1.0 + lax.erf(u * inv_root_two))
            h = (u * phi).astype(BF)
            hid[j, rb(i), :] = h
            slope[j, rb(i), :] = phi + u * jnp.exp(-0.5 * u * u) * inv_root_tau
            acc = acc + mm(h, down_ref[j], NT)
        y[rb(i), :] = acc
        return carry
    lax.fori_loop(0, nb, fwd, 0)
    dvec_ref[...] = jnp.zeros_like(dvec_ref)
    for s in range(segs):
        at = pl.ds(s * rows, rows)
        n1 = n1_ref[s]
        r2 = n1 * tab_ref[3:4, :] + tab_ref[4:5, :] + (y[at, :] + tab_ref[7:8, :])
        n2, inv2 = norm_stats(r2, width)
        out_ref[s] = (n2 * tab_ref[5:6, :] + tab_ref[6:7, :])[:seg_rows].astype(BF)
        live = lax.broadcasted_iota(jnp.int32, (rows, 1), 0) < seg_rows
        e = jnp.concatenate([cot_ref[s].astype(F32), jnp.zeros((rows - seg_rows, width), F32)], axis=0)
        dvec_ref[5:6, :] += jnp.sum(e * n2, axis=0, keepdims=True)
        dvec_ref[6:7, :] += jnp.sum(e, axis=0, keepdims=True)
        dr2 = norm_back(e * tab_ref[5:6, :], n2, inv2, width)
        d16 = dr2.astype(BF)
        y[at, :] = dr2
        dy[at, :] = d16
        dvec_ref[7:8, :] += jnp.sum(d16.astype(F32), axis=0, keepdims=True)
    dyt = dy[...].T
    abt = ab_ref[...].T
    for j in range(chunks):
        def back(i, carry):
            g = dy[rb(i), :]
            d = (mm(g, down_ref[j]) * slope[j, rb(i), :]).astype(BF)
            du[rb(i), :] = d
            return carry + jnp.sum(d.astype(F32), axis=0, keepdims=True)
        dvec_ref[8 + j:9 + j, :] = lax.fori_loop(0, nb, back, jnp.zeros((1, width), F32))
        ddown_ref[j] = mm(dyt, hid[j]).astype(BF)
        dup_ref[j] = mm(abt, du[...]).astype(BF)
        def inner(i, carry):
            part = mm(du[rb(i), :], up_ref[j], NT)
            slope[0, rb(i), :] = part if j == 0 else slope[0, rb(i), :] + part
            return carry
        lax.fori_loop(0, nb, inner, 0)
    for s in range(segs):
        at = pl.ds(s * rows, rows)
        da = y[at, :] + slope[0, at, :].astype(BF).astype(F32)
        n1 = n1_ref[s]
        dvec_ref[3:4, :] += jnp.sum(da * n1, axis=0, keepdims=True)
        dvec_ref[4:5, :] += jnp.sum(da, axis=0, keepdims=True)
        dr1 = norm_back(da * tab_ref[3:4, :], n1, inv_ref[s][:, 0:1], width)
        dr1_ref[at, :] = dr1
        dvec_ref[2:3, :] += jnp.sum(dr1.astype(BF).astype(F32), axis=0, keepdims=True)

def ffn(ab, n1, inv, cot, up, down, table):
    segs, rows, width = n1.shape
    seg_rows = cot.shape[1]
    total = segs * rows
    chunks = up.shape[0]
    sd = jax.ShapeDtypeStruct
    return pl.pallas_call(
        functools.partial(ffn_kernel, seg_rows, rows // 2),
        in_specs=[whole()] * 7, out_specs=[whole()] * 5,
        out_shape=[sd(cot.shape, BF), sd((total, width), F32), sd(up.shape, BF), sd(down.shape, BF), sd((16, width), F32)],
        scratch_shapes=[pltpu.VMEM((chunks, total, width), BF), pltpu.VMEM((chunks, total, width), F32), pltpu.VMEM((total, width), BF), pltpu.VMEM((total, width), BF)],
        compiler_params=pltpu.CompilerParams(vmem_limit_bytes=63 << 20),
        name="feed_forward",
    )(ab.reshape(total, width), n1, inv, cot, up, down, table)

def attn_bwd_kernel(seg_rows, len_ref, x_ref, w_ref, q_ref, k_ref, v_ref, c_ref, lse_ref, dr1_ref,
                    ig_ref, dw_ref, dvec_ref, dao, dc, dq, dk, dv, xs):
    segs, rows, width = q_ref.shape
    total = segs * rows
    heads = width // HEAD_DIM
    for s in range(segs):
        xs[pl.ds(s * rows, seg_rows), :] = x_ref[s]
        xs[pl.ds(s * rows + seg_rows, rows - seg_rows), :] = jnp.zeros((rows - seg_rows, width), BF)
    dao[...] = dr1_ref[...].astype(BF)
    dw_ref[3] = mm(c_ref[...].reshape(total, width).T, dao[...]).astype(BF)
    dc[...] = mm(dao[...], w_ref[3], NT).astype(BF)
    key_at = lax.broadcasted_iota(jnp.int32, (rows, 1), 0)
    lane = lax.broadcasted_iota(jnp.int32, (rows, 2 * HEAD_DIM), 1)
    zero = jnp.zeros((), BF)
    for s in range(segs):
        live = len_ref[s] + MEM
        usable = (key_at < live) | ((key_at >= seg_rows - MEM) & (key_at < seg_rows))
        bias = jnp.where(usable, 0.0, -1e30).astype(F32)
        at_rows = pl.ds(s * rows, rows)
        def pair(i, carry):
            at = pl.ds(pl.multiple_of(i * 2 * HEAD_DIM, 2 * HEAD_DIM), 2 * HEAD_DIM)
            q2, k2, v2 = q_ref[s, :, at], k_ref[s, :, at], v_ref[s, :, at]
            g2 = dc[at_rows, at]
            kt = k2.T
            dvp = jnp.zeros((rows, 2 * HEAD_DIM), F32)
            dkp = jnp.zeros((rows, 2 * HEAD_DIM), F32)
            dqt = []
            for h in range(2):
                mine = (lane < HEAD_DIM) if h == 0 else (lane >= HEAD_DIM)
                qh = jnp.where(mine, q2, zero)
                gh = jnp.where(mine, g2, zero)
                p = jnp.exp((mm(k2, qh, NT) + bias) - lse_ref[s, pl.ds(2 * i + h, 1), :])
                dp = mm(v2, gh, NT)
                dvp = dvp + mm(p.astype(BF), gh)
                ds = (p * (dp - jnp.sum(p * dp, axis=0, keepdims=True))).astype(BF)
                dkp = dkp + mm(ds, qh)
                dqt.append(mm(kt[h * HEAD_DIM:(h + 1) * HEAD_DIM], ds))
            dv[at_rows, at] = dvp.astype(BF)
            dk[at_rows, at] = dkp.astype(BF)
            dq[at_rows, at] = (jnp.concatenate(dqt, axis=0).T * (HEAD_DIM ** -0.5)).astype(BF)
            return carry
        lax.fori_loop(0, heads // 2, pair, 0)
    xt = xs[...].T
    dvec_ref[...] = jnp.zeros_like(dvec_ref)
    for j, g in enumerate((dq, dk, dv)):
        dw_ref[j] = mm(xt, g[...]).astype(BF)
    dvec_ref[0:1, :] = jnp.sum(dq[...].astype(F32), axis=0, keepdims=True)
    dvec_ref[1:2, :] = jnp.sum(dv[...].astype(F32), axis=0, keepdims=True)
    for s in range(segs):
        at = pl.ds(s * rows, rows)
        r = dr1_ref[at, :] + mm(dq[at, :], w_ref[0], NT) + mm(dk[at, :], w_ref[1], NT) + mm(dv[at, :], w_ref[2], NT)
        ig_ref[s] = r[:seg_rows]

def attn_bwd(lengths, tokens, weights, q, k, v, c, lse, dr1):
    segs, seg_rows, width = tokens.shape
    rows = q.shape[1]
    total = segs * rows
    sd = jax.ShapeDtypeStruct
    return pl.pallas_call(
        functools.partial(attn_bwd_kernel, seg_rows),
        in_specs=[pl.BlockSpec(memory_space=pltpu.SMEM)] + [whole()] * 8, out_specs=[whole()] * 3,
        out_shape=[sd(tokens.shape, F32), sd(weights.shape, BF), sd((16, width), F32)],
        scratch_shapes=[pltpu.VMEM((total, width), BF)] * 6,
        compiler_params=pltpu.CompilerParams(vmem_limit_bytes=63 << 20),
        name="attention_backward",
    )(lengths, tokens, weights, q, k, v, c, lse, dr1)

MESH = pl.DeviceIdType.MESH
F32, BF = jnp.float32, jnp.bfloat16
DMA = pltpu.SemaphoreType.DMA

def place():
    d, t = lax.axis_index("dp"), lax.axis_index("tensor")
    return d // 2, d % 2, t // 2, t % 2

def dev(z, x, y, c):
    return {"dp": z * 2 + x, "tensor": y * 2 + c}

def greet(z, x, y, c):
    b = pltpu.get_barrier_semaphore()
    for p in [((z + k) % 4, x, y, c) for k in (1, 2, 3)] + [(z, 1 - x, y, c), (z, x, 1 - y, c), (z, x, y, 1 - c)]:
        pl.semaphore_signal(b, inc=1, device_id=dev(*p), device_id_type=MESH)
    pl.semaphore_wait(b, 6)

def pick(ref, order, rows=None, **at):
    idx = tuple(at.get(ch, slice(None)) for ch in order)
    return ref.at[idx + ((rows,) if rows is not None else ())]

def send(src, dst, s, r, p):
    cp = pltpu.make_async_remote_copy(src, dst, s, r, device_id=dev(*p), device_id_type=MESH)
    cp.start()
    return cp

SHAPE = {"z": 4, "x": 2, "y": 2, "c": 2}


class Legs:
    def __init__(self, ssem, rsem):
        self.ssem, self.rsem, self.make, self.count = ssem, rsem, {}, 0

    def add(self, key, src, dst, peer):
        i = self.count
        self.count += 1
        self.make[key] = lambda: pltpu.make_async_remote_copy(
            src(), dst(), self.ssem.at[i], self.rsem.at[i], device_id=dev(*peer), device_id_type=MESH)

    def start(self, *keys):
        for k in keys:
            self.make[k]().start()

    def got(self, *keys):
        for k in keys:
            self.make[k]().wait_recv()

    def sent(self, *keys):
        for k in keys:
            self.make[k]().wait_send()

def add_spread(legs, key, view, place_now, h):
    z, x, y, c = place_now
    core, xp, yp = (z, x, y, 1 - c), (z, 1 - x, y, c), (z, x, 1 - y, c)
    def leg(name, peer, **at):
        legs.add((key, name), lambda: view(**at), lambda: view(**at), peer)
    leg("s1", xp if h == 0 else yp, x=x, y=y, c=c)
    leg("k1", core, x=x, y=y, c=c)
    if h == 0:
        leg("s2", yp, y=y, c=c)
        leg("k2", core, x=1 - x, y=y, c=c)
        leg("k3", core, y=1 - y, c=c)
    else:
        leg("s2", xp, x=x, c=c)
        leg("k2", core, x=x, y=1 - y, c=c)
        leg("k3", core, x=1 - x, c=c)

N_FORWARD_LEGS = 3 * 3 + 4 + 6 * 5 + 2 * 5 + 4 * 3 + 4 * 5

def forward_kernel(seg_rows, len_ref, tok, cot, am, um, dm, vp,
                   out_o, q_o, k_o, v_o, c_o, w_o, dr1_o, dup_o, ddn_o, lse_ref, dvec_ref,
                   wa, wu, wd, vec, tab, traw, craw, xs, cs, q, k, v, ct, cc, n1, inv, ab, hid, slo, dy, dyt, abt,
                   ssem, rsem, lsem):
    segs, rows, width = q_o.shape
    total = segs * rows
    heads = width // HEAD_DIM
    part = am.shape[0]
    z, x, y, c = here = place()
    peers_z = {i: ((z + i) % 4, x, y, c) for i in (1, 2, 3)}
    lt = pltpu.make_async_copy(tok, traw, lsem.at[0]); lt.start()
    lc = pltpu.make_async_copy(cot, craw, lsem.at[1]); lc.start()
    wa[z, x, y, c] = am[...].astype(BF)
    wu[y, c, z, x] = um[...].astype(BF)
    wd[y, c, z, x] = dm[...].astype(BF)
    vec[z, x] = vp[...]

    legs = Legs(ssem, rsem)
    pair_w = 2 * HEAD_DIM
    groups = width // (2 * pair_w)
    for g in range(groups):
        col = pl.ds(g * 2 * pair_w, 2 * pair_w)
        for i in (1, 2, 3):
            f = functools.partial(lambda col: wa.at[z, x, y, c, :, col], col)
            legs.add(("z", g, i), f, f, peers_z[i])
    for i in (1, 2, 3):
        legs.add(("vz", i), lambda: vec.at[z, x], lambda: vec.at[z, x], peers_z[i])
    legs.add("vx", lambda: vec.at[:, x], lambda: vec.at[:, x], (z, 1 - x, y, c))
    three = pl.ds(0, 3)
    def att_view(zz, col):
        return lambda **at: pick(wa, "zxycr", z=zz, **at).at[(Ellipsis,)] if False else wa.at[tuple([zz] + [at.get(ch, slice(None)) for ch in "xyc"] + [slice(None), col])]
    for g in range(groups):
        for h in range(2):
            add_spread(legs, ("a", g, h), att_view(three, pl.ds((2 * g + h) * pair_w, pair_w)), here, h)
    for h in range(2):
        add_spread(legs, ("o", h), att_view(3, pl.ds(h * (width // 2), width // 2)), here, h)
    half = part // 2
    for name, ref in (("u", wu), ("d", wd)):
        for h in range(2):
            rr = pl.ds(h * half, half)
            f = functools.partial(lambda ref, rr: ref.at[y, c, z, x, rr], ref, rr)
            for i in (1, 2, 3):
                legs.add((name, h, "z", i), f, f, peers_z[i])
            view = functools.partial(lambda ref, rr, **at: ref.at[tuple([at.get(ch, slice(None)) for ch in "yczx"] + [rr])], ref, rr)
            add_spread(legs, (name, h), view, here, h)

    def stage(units, n):
        for u in units:
            if n == 2:
                legs.got((u, "s1"))
                legs.start((u, "s2"), (u, "k2"))
            elif n == 3:
                legs.got((u, "s2"))
                legs.start((u, "k3"))
            elif n == 1:
                legs.start((u, "s1"), (u, "k1"))
            elif n == 4:
                legs.got((u, "k1"), (u, "k2"), (u, "k3"))
    A = lambda g: [("a", g, 0), ("a", g, 1)]
    O = [("o", 0), ("o", 1)]
    U, W = [("u", 0), ("u", 1)], [("d", 0), ("d", 1)]
    def zstart(name):
        for h in range(2):
            legs.start(*[(name, h, "z", i) for i in (1, 2, 3)])
    def zgot(name):
        for h in range(2):
            legs.got(*[(name, h, "z", i) for i in (1, 2, 3)])

    greet(*here)
    legs.start(*[("z", 0, i) for i in (1, 2, 3)])
    legs.start(*[("vz", i) for i in (1, 2, 3)])
    for g in range(1, groups):
        legs.start(*[("z", g, i) for i in (1, 2, 3)])
    lt.wait()
    for s in range(segs):
        xs[pl.ds(s * rows, seg_rows), :] = traw[s]
        xs[pl.ds(s * rows + seg_rows, rows - seg_rows), :] = jnp.zeros((rows - seg_rows, width), BF)
    legs.got(*[("z", 0, i) for i in (1, 2, 3)])
    stage(A(0), 1)
    lc.wait()
    for s in range(segs):
        cs[pl.ds(s * rows, seg_rows), :] = craw[s]
        cs[pl.ds(s * rows + seg_rows, rows - seg_rows), :] = jnp.zeros((rows - seg_rows, width), BF)
    legs.got(*[("z", 1, i) for i in (1, 2, 3)])
    stage(A(1), 1)
    stage(A(0), 2)
    legs.got(*[("vz", i) for i in (1, 2, 3)])
    legs.start("vx")
    legs.got(*[("z", 2, i) for i in (1, 2, 3)])
    stage(A(2), 1)
    zstart("u")
    stage(A(1), 2)
    stage(A(0), 3)
    legs.got("vx")
    lane_in = lax.broadcasted_iota(jnp.int32, (128, width), 0)
    lane_out = lax.broadcasted_iota(jnp.int32, (128, width), 1)
    acc = jnp.zeros((16, width), F32)
    for d in range(8):
        move = ((lane_out == lane_in + d * part) & (lane_in < part)).astype(BF)
        acc = acc + mm(vec[d // 2, d % 2], move)
    tab[...] = acc
    ticks = {
        1: lambda: (stage(A(2), 2), stage(A(1), 3)),
        2: lambda: (stage(O, 1), stage(A(2), 3)),
        3: lambda: (stage(O, 2), zgot("u"), stage(U, 1)),
        5: lambda: (stage(O, 3), stage(U, 2), zstart("d")),
        8: lambda: (zgot("d"), stage(W, 1)),
        9: lambda: stage(U, 3),
        11: lambda: stage(W, 2),
    }
    lane = lax.broadcasted_iota(jnp.int32, (rows, pair_w), 1)
    key_at = lax.broadcasted_iota(jnp.int32, (rows, 1), 0)
    zero = jnp.zeros((), BF)

    def body(it, carry):
        for n, f in ticks.items():
            pl.when(it == n)(lambda f=f: (f(), None)[1])
        for g in range(groups):
            pl.when(it == 4 * g)(lambda g=g: (stage(A(g), 4), None)[1])
        g = it // 4

        @pl.when(it % 4 == 0)
        def _():
            col = pl.ds(pl.multiple_of(g * 2 * pair_w, 2 * pair_w), 2 * pair_w)
            w3 = [wa[m, :, :, :, :, col].reshape(width, 2 * pair_w) for m in range(3)]
            xx = xs[...]
            q[:, col] = ((mm(xx, w3[0]) + tab[0:1, col]).astype(BF) * BF(HEAD_DIM ** -0.5)).astype(BF)
            k[:, col] = mm(xx, w3[1]).astype(BF)
            v[:, col] = (mm(xx, w3[2]) + tab[1:2, col]).astype(BF)

        s = (it // 2) % 2
        i = 2 * g + it % 2
        col = pl.ds(pl.multiple_of(i * pair_w, pair_w), pair_w)
        rr = pl.ds(pl.multiple_of(s * rows, 16), rows)
        live = len_ref[s] + MEM
        usable = (key_at < live) | ((key_at >= seg_rows - MEM) & (key_at < seg_rows))
        bias = jnp.where(usable, 0.0, -1e30).astype(F32)
        q2, k2, v2 = q[rr, col], k[rr, col], v[rr, col]
        vt = v2.T
        for h in range(2):
            mine = (lane < HEAD_DIM) if h == 0 else (lane >= HEAD_DIM)
            sc = mm(k2, jnp.where(mine, q2, zero), NT) + bias
            top = jnp.max(sc, axis=0, keepdims=True)
            e = jnp.exp(sc - top)
            tot = jnp.sum(e, axis=0, keepdims=True)
            p = (e * (1.0 / tot)).astype(BF)
            at = pl.ds(pl.multiple_of(i * pair_w + h * HEAD_DIM, HEAD_DIM), HEAD_DIM)
            ct[s, at, :] = mm(vt[h * HEAD_DIM:(h + 1) * HEAD_DIM], p).astype(BF)
            lse_ref[s, pl.ds(2 * i + h, 1), :] = top + jnp.log(tot)
        return carry
    lax.fori_loop(0, 4 * groups, body, 0)

    spill = [pltpu.make_async_copy(a.at[pl.ds(s * rows, rows)], o.at[s], lsem.at[2 + 2 * n + s]) for n, (a, o) in enumerate(((q, q_o), (k, k_o), (v, v_o))) for s in range(segs)]
    for cp in spill:
        cp.start()
    stage(O, 4)
    wcopy = pltpu.make_async_copy(wa, w_o, lsem.at[8]); wcopy.start()
    for s in range(segs):
        rr = pl.ds(s * rows, rows)
        cs_ = ct[s].T
        cc[rr, :] = cs_
        r = xs[rr, :].astype(F32) + mm(cs_, wa[3].reshape(width, width)) + tab[2:3, :]
        n, iv = norm_stats(r, width)
        n1[rr, :] = n
        inv[rr, :] = jnp.broadcast_to(iv, (rows, 128))
        ab[rr, :] = (n * tab[3:4, :] + tab[4:5, :]).astype(BF)
    ccopy = [pltpu.make_async_copy(cc.at[pl.ds(s * rows, rows)], c_o.at[s], lsem.at[9 + s]) for s in range(segs)]
    for cp in ccopy:
        cp.start()

    block = rows // 2
    nb = total // block
    chunks = 4
    def rb(i):
        return pl.ds(pl.multiple_of(i * block, 16), block)
    def up(j):
        return wu[j // 2, j % 2].reshape(width, width)
    def down(j):
        return wd[j // 2, j % 2].reshape(width, width)
    stage(U, 4)
    def fwd(i, carry):
        pl.when(i == 2)(lambda: (stage(W, 3), None)[1])
        a = ab[rb(i), :]
        for j in range(chunks):
            u = mm(a, up(j)) + tab[8 + j:9 + j, :]
            phi = 0.5 * (1.0 + lax.erf(u * inv_root_two))
            hid[j, rb(i), :] = (u * phi).astype(BF)
            slo[j, rb(i), :] = (phi + u * jnp.exp(-0.5 * u * u) * inv_root_tau).astype(BF)
        return carry
    lax.fori_loop(0, nb, fwd, 0)
    stage(W, 4)
    dvec_ref[...] = jnp.zeros_like(dvec_ref)
    def mid(i, carry):
        yy = tab[7:8, :]
        for j in range(chunks):
            yy = yy + mm(hid[j, rb(i), :], down(j), NT)
        nn = n1[rb(i), :]
        r2 = nn * tab[3:4, :] + tab[4:5, :] + yy
        n2, inv2 = norm_stats(r2, width)
        e = cs[rb(i), :].astype(F32)
        cs[rb(i), :] = (n2 * tab[5:6, :] + tab[6:7, :]).astype(BF)
        dvec_ref[5:6, :] += jnp.sum(e * n2, axis=0, keepdims=True)
        dvec_ref[6:7, :] += jnp.sum(e, axis=0, keepdims=True)
        dr2 = norm_back(e * tab[5:6, :], n2, inv2, width)
        g16 = dr2.astype(BF)
        dy[rb(i), :] = g16
        dvec_ref[7:8, :] += jnp.sum(g16.astype(F32), axis=0, keepdims=True)
        da = jnp.zeros((block, width), F32)
        for j in range(chunks):
            d16 = (mm(g16, down(j)) * slo[j, rb(i), :].astype(F32)).astype(BF)
            slo[j, rb(i), :] = d16
            dvec_ref[8 + j:9 + j, :] += jnp.sum(d16.astype(F32), axis=0, keepdims=True)
            da = da + mm(d16, up(j), NT)
        da = dr2 + da.astype(BF).astype(F32)
        dvec_ref[3:4, :] += jnp.sum(da * nn, axis=0, keepdims=True)
        dvec_ref[4:5, :] += jnp.sum(da, axis=0, keepdims=True)
        dr1 = norm_back(da * tab[3:4, :], nn, inv[rb(i), 0:1], width)
        n1[rb(i), :] = dr1
        dvec_ref[2:3, :] += jnp.sum(dr1.astype(BF).astype(F32), axis=0, keepdims=True)
        return carry
    lax.fori_loop(0, nb, mid, 0)
    dcopy = pltpu.make_async_copy(n1, dr1_o, lsem.at[0]); dcopy.start()
    for s in range(segs):
        craw[s] = cs[pl.ds(s * rows, seg_rows), :]
    ocopy = pltpu.make_async_copy(craw, out_o, lsem.at[1]); ocopy.start()
    dyt[...] = dy[...].T
    abt[...] = ab[...].T
    legs.sent(*legs.make)
    def grad_copies(j):
        return (pltpu.make_async_copy(wd.at[j // 2, j % 2], ddn_o.at[j // 2, j % 2], lsem.at[11 + 2 * (j % 2)]),
                pltpu.make_async_copy(wu.at[j // 2, j % 2], dup_o.at[j // 2, j % 2], lsem.at[12 + 2 * (j % 2)]))
    def grads(j, carry):
        shape = wd.shape[2:]
        @pl.when(j >= 2)
        def _():
            for cp in grad_copies(j - 2):
                cp.wait()
        wd[j // 2, j % 2] = mm(dyt[...], hid[j]).astype(BF).reshape(shape)
        wu[j // 2, j % 2] = mm(abt[...], slo[j]).astype(BF).reshape(shape)
        for cp in grad_copies(j):
            cp.start()
        return carry
    lax.fori_loop(0, chunks, grads, 0)
    for j in (2, 3):
        for cp in grad_copies(j):
            cp.wait()
    for cp in spill + [wcopy, dcopy, ocopy] + ccopy:
        cp.wait()

def forward(lengths, tokens, cotangent, att, up, down, piece):
    segs, seg_rows, width = tokens.shape
    part = att.shape[0]
    rows = -(-seg_rows // 16) * 16
    total = segs * rows
    hp = -(-(width // HEAD_DIM) // 8) * 8
    sd = jax.ShapeDtypeStruct
    any_, vm = pl.BlockSpec(memory_space=pl.ANY), whole()
    wshape, fshape = (4, 2, 2, 2, part, width), (2, 2, 4, 2, part, width)
    V = lambda *s, t=BF: pltpu.VMEM(s, t)
    return pl.pallas_call(
        functools.partial(forward_kernel, seg_rows),
        in_specs=[pl.BlockSpec(memory_space=pltpu.SMEM), any_, any_, vm, vm, vm, vm],
        out_specs=[any_] * 9 + [vm, vm],
        out_shape=[sd(cotangent.shape, BF)] + [sd((segs, rows, width), BF)] * 4 + [sd(wshape, BF), sd((total, width), F32), sd(fshape, BF), sd(fshape, BF), sd((segs, hp, rows), F32), sd((16, width), F32)],
        scratch_shapes=[V(*wshape), V(*fshape), V(*fshape), V(4, 2, 16, 128), V(16, width, t=F32), V(segs, seg_rows, width), V(segs, seg_rows, width),
                        V(total, width), V(total, width), V(total, width), V(total, width), V(total, width), V(segs, width, rows), V(total, width),
                        V(total, width, t=F32), V(total, 128, t=F32), V(total, width), V(4, total, width), V(4, total, width), V(total, width), V(width, total), V(width, total),
                        DMA((N_FORWARD_LEGS,)), DMA((N_FORWARD_LEGS,)), DMA((15,))],
        compiler_params=pltpu.CompilerParams(collective_id=0, has_side_effects=True, vmem_limit_bytes=63 << 20),
        name="forward_and_feed_forward_backward",
    )(lengths, tokens, cotangent, att, up, down, piece)

N_BACK_LEGS = 4 * 6 + 2 * 6 + 6 * 6 + 6


def backward_kernel(seg_rows, len_ref, tok, w_i, q_i, k_i, v_i, c_i, dr1_i, dup, ddn, lse_ref, dvec_in,
                    ig_o, ga_ref, gu_ref, gd_ref, gv_ref,
                    wa, q, k, v, cc, r1f, traw, xs, xt, dao, own_u, own_d, rc_u, rc_d, h1_u0, h1_u1, h1_d0, h1_d1, h2_f, rz_f, rc_a, h1_a, h2_a, rz_a, rc_o, h1_o, h2_o, rz_o, vbuf,
                    ssem, rsem, lsem):
    segs, rows, width = q_i.shape
    total = segs * rows
    heads = width // HEAD_DIM
    pair_w = 2 * HEAD_DIM
    groups = width // (2 * pair_w)
    part = ga_ref.shape[0]
    half = part // 2
    z, x, y, c = here = place()
    me = dict(z=z, x=x, y=y, c=c)
    core, xp, yp = (z, x, y, 1 - c), (z, 1 - x, y, c), (z, x, 1 - y, c)
    zp = {i: ((z + i) % 4, x, y, c) for i in (1, 2, 3)}
    h1_u, h1_d = (h1_u0, h1_u1), (h1_d0, h1_d1)
    legs = Legs(ssem, rsem)
    first, second = {0: "y", 1: "x"}, {0: "x", 1: "y"}
    peer = {"x": xp, "y": yp}

    load = {}
    def local(name, src, dst, i):
        load[name] = pltpu.make_async_copy(src, dst, lsem.at[i])
        load[name].start()
    local("dr1", dr1_i, r1f, 0)
    local("w", w_i, wa, 1)
    for s in range(segs):
        rr = pl.ds(s * rows, rows)
        local(("c", s), c_i.at[s], cc.at[rr], 2 + s)
        local(("v", s), v_i.at[s], v.at[rr], 4 + s)
        local(("k", s), k_i.at[s], k.at[rr], 6 + s)
        local(("q", s), q_i.at[s], q.at[rr], 8 + s)
    local("t", tok, traw, 10)

    ff = [("u", dup, own_u, rc_u, h1_u), ("d", ddn, own_d, rc_d, h1_d)]
    hop = {}
    for n, (name, g, own, rc, h1) in enumerate(ff):
        for h in range(2):
            rr = pl.ds(h * half, half)
            u = 2 * n + h
            f, s = first[h], second[h]
            o = own.at[h]
            legs.add((name, h, 0), functools.partial(lambda g, rr: g.at[:, 1 - c, :, :, rr], g, rr), functools.partial(lambda rc, h: rc.at[h], rc, h), core)
            local((name, h), g.at[:, c, :, :, rr], o, 11 + u)
            legs.add((name, h, 1), functools.partial(lambda o, f: pick(o, "yzx", **{f: 1 - me[f]}), o, f), functools.partial(lambda h1, h: h1[h], h1, h), peer[f])
            legs.add((name, h, 2), functools.partial(lambda o, f, s: pick(o, "yzx", **{f: me[f], s: 1 - me[s]}), o, f, s), functools.partial(lambda u: h2_f.at[u], u), peer[s])
            for i in (1, 2, 3):
                legs.add((name, h, 2 + i), functools.partial(lambda o, i: o.at[y, (z + i) % 4, x], o, i), functools.partial(lambda u, i: rz_f.at[u, i - 1], u, i), zp[i])

    def ff_stage(name, h, n):
        own, rc, h1 = (own_u, rc_u, h1_u) if name == "u" else (own_d, rc_d, h1_d)
        u = 2 * (name == "d") + h
        o, f, s = own.at[h], first[h], second[h]
        if n == 0:
            legs.got((name, h, 0))
            load[name, h].wait()
            def body(i, _):
                at = (i // 8, (i // 2) % 4, i % 2)
                o[at] = (o[at].astype(F32) + rc[(h,) + at].astype(F32)).astype(BF)
                return 0
            lax.fori_loop(0, 16, body, 0)
            legs.start((name, h, 1))
        elif n == 1:
            legs.got((name, h, 1))
            left = "yzx".replace(f, "")
            sh = [SHAPE[ch] for ch in left]
            o = pick(o, "yzx", **{f: me[f]})
            def body(i, _):
                at = (i // sh[1], i % sh[1])
                o[at] = (o[at].astype(F32) + h1[h][at].astype(F32)).astype(BF)
                return 0
            lax.fori_loop(0, 8, body, 0)
            legs.start((name, h, 2))
        elif n == 2:
            legs.got((name, h, 2))
            def body(i, _):
                o[y, i, x] = (o[y, i, x].astype(F32) + h2_f[u, i].astype(F32)).astype(BF)
                return 0
            lax.fori_loop(0, 4, body, 0)
            legs.start(*[(name, h, 2 + i) for i in (1, 2, 3)])
        else:
            legs.got(*[(name, h, 2 + i) for i in (1, 2, 3)])
            out = gu_ref if name == "u" else gd_ref
            out[pl.ds(h * half, half)] = ((o[y, z, x].astype(F32) + rz_f[u, 0].astype(F32)) + rz_f[u, 1].astype(F32)) + rz_f[u, 2].astype(F32)

    three = pl.ds(0, 3)
    def att(zz, col, **at):
        return wa.at[tuple([zz] + [at.get(ch, slice(None)) for ch in "xyc"] + [slice(None), col])]
    def add_att(key, zz, col, rc, h1, h2, rz, h):
        f, s = first[h], second[h]
        legs.add((key, 0), lambda: att(zz, col, c=1 - c), lambda: rc, core)
        legs.add((key, 1), lambda: att(zz, col, c=c, **{f: 1 - me[f]}), lambda: h1, peer[f])
        legs.add((key, 2), lambda: att(zz, col, c=c, **{f: me[f], s: 1 - me[s]}), lambda: h2, peer[s])
        for i in (1, 2, 3):
            legs.add((key, 2 + i), functools.partial(lambda i: att((z + i) % 4, col, c=c, x=x, y=y), i), functools.partial(lambda i: rz.at[i - 1], i), zp[i])
    units = {}
    for g in range(groups):
        for h in range(2):
            u = 2 * g + h
            col = pl.ds(u * pair_w, pair_w)
            units["a", g, h] = (range(3), col, rc_a.at[u], h1_a.at[u], h2_a.at[u], rz_a.at[u], h)
            add_att(("a", g, h), three, col, *units["a", g, h][2:])
    for h in range(2):
        col = pl.ds(h * (width // 2), width // 2)
        units["o", h] = ((3,), col, rc_o.at[h], h1_o.at[h], h2_o.at[h], rz_o.at[h], h)
        add_att(("o", h), 3, col, *units["o", h][2:])

    def att_stage(key, n):
        zs, col, rc, h1, h2, rz, h = units[key]
        f, s = first[h], second[h]
        one = len(zs) == 1
        base = zs[0]
        def sub(ref, i, *rest):
            at = tuple(rest) if one else (i,) + tuple(rest)
            return ref[at] if at else ref[...]
        if n == 0:
            legs.start((key, 0))
            return
        if n == 1:
            legs.got((key, 0))
            def body(i, _):
                m, a, b = base + i // 4, (i // 2) % 2, i % 2
                t = (m, a, b, c, slice(None), col)
                wa[t] = (wa[t].astype(F32) + sub(rc, i // 4, a, b).astype(F32)).astype(BF)
                return 0
            lax.fori_loop(0, 4 * len(zs), body, 0)
            legs.start((key, 1))
        elif n == 2:
            legs.got((key, 1))
            def body(i, _):
                m, a = base + i // 2, i % 2
                t = (m, a, y, c, slice(None), col) if f == "y" else (m, x, a, c, slice(None), col)
                wa[t] = (wa[t].astype(F32) + sub(h1, i // 2, a).astype(F32)).astype(BF)
                return 0
            lax.fori_loop(0, 2 * len(zs), body, 0)
            legs.start((key, 2))
        elif n == 3:
            legs.got((key, 2))
            def body(i, _):
                t = (base + i, x, y, c, slice(None), col)
                wa[t] = (wa[t].astype(F32) + sub(h2, i).astype(F32)).astype(BF)
                return 0
            lax.fori_loop(0, len(zs), body, 0)
            for i in (1, 2, 3):
                to = (z + i) % 4
                pl.when((to == 3) if one else (to < 3))(functools.partial(lambda i: (legs.start((key, 2 + i)), None)[1], i))
        else:
            @pl.when((z == 3) if one else (z < 3))
            def _():
                legs.got(*[(key, 2 + i) for i in (1, 2, 3)])
                ga_ref[:, col] = ((wa[z, x, y, c, :, col].astype(F32) + rz[0].astype(F32)) + rz[1].astype(F32)) + rz[2].astype(F32)

    def att_sent(key):
        one = key[0] == "o"
        legs.sent((key, 0), (key, 1), (key, 2))
        for i in (1, 2, 3):
            to = (z + i) % 4
            pl.when((to == 3) if one else (to < 3))(functools.partial(lambda i: (legs.sent((key, 2 + i)), None)[1], i))

    legs.add("v0", lambda: vbuf.at[0], lambda: vbuf.at[1], core)
    legs.add("v1", lambda: vbuf.at[2], lambda: vbuf.at[3], yp)
    legs.add("v2", lambda: vbuf.at[4], lambda: vbuf.at[5], xp)
    for i in (1, 2, 3):
        legs.add(("v3", i), lambda: vbuf.at[6 + z], lambda: vbuf.at[6 + z], zp[i])

    greet(*here)
    for h in range(2):
        for name in ("u", "d"):
            legs.start((name, h, 0))
    load["dr1"].wait()
    dao[...] = r1f[...].astype(BF)
    for s in range(segs):
        load["c", s].wait()
    load["w"].wait()
    dwo = mm(cc[...].T, dao[...]).astype(BF)
    dc = mm(dao[...], wa[3].reshape(width, width), NT).astype(BF)
    cc[...] = dc
    wa[3] = dwo.reshape(wa.shape[1:])
    for h in range(2):
        att_stage(("o", h), 0)
    ff_stage("u", 0, 0)
    ff_stage("u", 1, 0)
    load["t"].wait()
    for s in range(segs):
        xs[pl.ds(s * rows, seg_rows), :] = traw[s]
        xs[pl.ds(s * rows + seg_rows, rows - seg_rows), :] = jnp.zeros((rows - seg_rows, width), BF)
    xt[...] = xs[...].T
    for s in range(segs):
        for n in "qkv":
            load[n, s].wait()
    vbuf[0] = dvec_in[...]

    def ffs(*what):
        return lambda: [ff_stage(*w) for w in what]
    def atts(*what):
        return lambda: [att_stage(*w) for w in what]
    ticks = {
        1: ffs(("u", 0, 1), ("u", 1, 1), ("d", 0, 0), ("d", 1, 0)),
        3: ffs(("u", 0, 2), ("u", 1, 2)),
        4: ffs(("d", 0, 1), ("d", 1, 1)),
        5: ffs(("u", 0, 3), ("u", 1, 3)),
        6: atts((("o", 0), 1), (("o", 1), 1)),
        7: ffs(("d", 0, 2), ("d", 1, 2)),
        8: atts((("o", 0), 2), (("o", 1), 2), (("a", 0, 0), 1), (("a", 0, 1), 1)),
        9: ffs(("d", 0, 3), ("d", 1, 3)),
        10: atts((("o", 0), 3), (("o", 1), 3), (("a", 0, 0), 2), (("a", 0, 1), 2)),
        11: atts((("a", 0, 0), 3), (("a", 0, 1), 3), (("a", 1, 0), 1), (("a", 1, 1), 1)),
    }
    lane = lax.broadcasted_iota(jnp.int32, (rows, pair_w), 1)
    key_at = lax.broadcasted_iota(jnp.int32, (rows, 1), 0)
    zero = jnp.zeros((), BF)

    def body(it, carry):
        for n, f in ticks.items():
            pl.when(it == n)(lambda f=f: (f(), None)[1])
        g = it // 4
        s = (it // 2) % 2
        i = 2 * g + it % 2
        col = pl.ds(pl.multiple_of(i * pair_w, pair_w), pair_w)
        rr = pl.ds(pl.multiple_of(s * rows, 16), rows)
        live = len_ref[s] + MEM
        usable = (key_at < live) | ((key_at >= seg_rows - MEM) & (key_at < seg_rows))
        bias = jnp.where(usable, 0.0, -1e30).astype(F32)
        q2, k2, v2, g2 = q[rr, col], k[rr, col], v[rr, col], cc[rr, col]
        kt = k2.T
        dvp = jnp.zeros((rows, pair_w), F32)
        dkp = jnp.zeros((rows, pair_w), F32)
        dqt = []
        for h in range(2):
            mine = (lane < HEAD_DIM) if h == 0 else (lane >= HEAD_DIM)
            qh = jnp.where(mine, q2, zero)
            gh = jnp.where(mine, g2, zero)
            p = jnp.exp((mm(k2, qh, NT) + bias) - lse_ref[s, pl.ds(2 * i + h, 1), :])
            dp = mm(v2, gh, NT)
            dvp = dvp + mm(p.astype(BF), gh)
            ds = (p * (dp - jnp.sum(p * dp, axis=0, keepdims=True))).astype(BF)
            dkp = dkp + mm(ds, qh)
            dqt.append(mm(kt[h * HEAD_DIM:(h + 1) * HEAD_DIM], ds))
        v[rr, col] = dvp.astype(BF)
        k[rr, col] = dkp.astype(BF)
        q[rr, col] = (jnp.concatenate(dqt, axis=0).T * (HEAD_DIM ** -0.5)).astype(BF)

        @pl.when(it % 4 == 3)
        def _():
            gcol = pl.ds(pl.multiple_of(g * 2 * pair_w, 2 * pair_w), 2 * pair_w)
            for m, ref in enumerate((q, k, v)):
                d = ref[:, gcol]
                r1f[...] += mm(d, wa[m, :, :, :, :, gcol].reshape(width, 2 * pair_w), NT)
                wa[m, :, :, :, :, gcol] = mm(xt[...], d).astype(BF).reshape(2, 2, 2, part, 2 * pair_w)
            for gg in range(groups):
                pl.when(g == gg)(functools.partial(lambda gg: ([att_stage(("a", gg, h), 0) for h in range(2)], None)[1], gg))
        return carry
    lax.fori_loop(0, 4 * groups, body, 0)

    vbuf[0, 0:1, :] = jnp.sum(q[...].astype(F32), axis=0, keepdims=True)
    vbuf[0, 1:2, :] = jnp.sum(v[...].astype(F32), axis=0, keepdims=True)
    legs.start("v0")
    def a_all(g, n):
        for h in range(2):
            att_stage(("a", g, h), n)
    a_all(1, 2)
    a_all(2, 1)
    legs.got("v0")
    vbuf[2] = vbuf[0] + vbuf[1]
    legs.start("v1")
    for h in range(2):
        att_stage(("o", h), 4)
    a_all(1, 3)
    a_all(2, 2)
    legs.got("v1")
    vbuf[4] = vbuf[2] + vbuf[3]
    legs.start("v2")
    a_all(0, 4)
    a_all(2, 3)
    legs.got("v2")
    vbuf[6 + z] = vbuf[4] + vbuf[5]
    legs.start(*[("v3", i) for i in (1, 2, 3)])
    for s in range(segs):
        ig_o[s] = r1f[pl.ds(s * rows, seg_rows), :]
    a_all(1, 4)
    legs.got(*[("v3", i) for i in (1, 2, 3)])
    gv_ref[...] = ((vbuf[6] + vbuf[7]) + vbuf[8]) + vbuf[9]
    a_all(2, 4)
    for key in legs.make:
        if isinstance(key, tuple) and isinstance(key[0], tuple):
            continue
        legs.sent(key)
    for key in units:
        att_sent(key)


def backward(lengths, tokens, w, q, k, v, c, dr1, dup, ddn, lse, dvec):
    segs, seg_rows, width = tokens.shape
    rows = q.shape[1]
    total = segs * rows
    part = w.shape[-2]
    half = part // 2
    pw = 2 * HEAD_DIM
    sd = jax.ShapeDtypeStruct
    any_, vm = pl.BlockSpec(memory_space=pl.ANY), whole()
    V = lambda *s, t=BF: pltpu.VMEM(s, t)
    nu = width // pw
    scratch = [V(*w.shape), V(total, width), V(total, width), V(total, width), V(total, width), V(total, width, t=F32), V(segs, seg_rows, width), V(total, width), V(width, total), V(total, width)]
    scratch += [V(2, 2, 4, 2, half, width)] * 4 + [V(4, 2, half, width), V(2, 4, half, width)] * 2 + [V(4, 4, half, width), V(4, 3, half, width)]
    scratch += [V(nu, 3, 2, 2, part, pw), V(nu, 3, 2, part, pw), V(nu, 3, part, pw), V(nu, 3, part, pw)]
    scratch += [V(2, 2, 2, part, width // 2), V(2, 2, part, width // 2), V(2, part, width // 2), V(2, 3, part, width // 2), V(10, 16, width, t=F32)]
    return pl.pallas_call(
        functools.partial(backward_kernel, seg_rows),
        in_specs=[pl.BlockSpec(memory_space=pltpu.SMEM)] + [any_] * 9 + [vm, vm],
        out_specs=[vm] * 5,
        out_shape=[sd(tokens.shape, F32)] + [sd((part, width), F32)] * 3 + [sd((16, width), F32)],
        scratch_shapes=scratch + [DMA((N_BACK_LEGS,)), DMA((N_BACK_LEGS,)), DMA((15,))],
        compiler_params=pltpu.CompilerParams(collective_id=1, has_side_effects=True, vmem_limit_bytes=63 << 20),
        name="attention_backward_and_sums",
    )(lengths, tokens, w, q, k, v, c, dr1, dup, ddn, lse, dvec)

STEPS = 5
beta_first = 0.9
beta_second = 0.999
adam_epsilon = 1e-08
matrix_rate = 0.06
vector_rate = 0.2
weight_decay = 0.01
ORDERS = ("zxyc", "yczx", "yczx")


def adam(weight, moment_one, moment_two, gradient, step_rate, decay_rate):
    first_new = beta_first * moment_one + (1.0 - beta_first) * gradient
    second_new = beta_second * moment_two + (1.0 - beta_second) * gradient * gradient
    first_hat = first_new / (1.0 - beta_first**STEPS)
    second_hat = second_new / (1.0 - beta_second**STEPS)
    update = first_hat / (jnp.sqrt(second_hat) + adam_epsilon)
    return (weight - step_rate * (update + decay_rate * weight), first_new, second_new)


def shards(
    own_plan,
    tokens,
    segment_lengths,
    cotangent,
    attention_master,
    attention_mean,
    attention_square,
    up_master,
    up_mean,
    up_square,
    down_master,
    down_mean,
    down_square,
    vector_master,
    vector_mean,
    vector_square,
):
    width = tokens.shape[2]
    dp_count, tensor_count = lax.axis_size("dp"), lax.axis_size("tensor")
    part, columns = vector_master.shape
    spare = 16 - columns
    vec_low = vector_master.astype(BF).T
    if own_plan:
        piece = jnp.pad(vec_low, ((0, spare), (0, 128 - part)))
        block_output, q, k, v, c, w_all, dr1, d_up, d_down, lse, dvec_ffn = forward(
            segment_lengths, tokens, cotangent, attention_master, up_master, down_master, piece
        )
    else:
        low = [m.astype(BF) for m in (attention_master, up_master, down_master)]
        w_all = lax.all_gather(low[0], ("dp", "tensor"), axis=0, tiled=True)
        up_all, down_all = (lax.all_gather(m, ("tensor", "dp"), axis=0, tiled=True) for m in low[1:])
        rows = lax.all_gather(vec_low, "dp", axis=1, tiled=True).astype(F32)
        table = jnp.pad(rows, ((0, spare), (0, 0)))
        w_all = w_all.reshape(4, width, width)
        up_all = up_all.reshape(tensor_count, width, width)
        down_all = down_all.reshape(tensor_count, width, width)
        q, k, v, c, n1, inv, ab, lse = attn_fwd(segment_lengths, tokens, w_all, table)
        block_output, dr1, d_up, d_down, dvec_ffn = ffn(ab, n1, inv, cotangent, up_all, down_all, table)
    if own_plan:
        input_grad, s_attention, s_up, s_down, s_vec = backward(
            segment_lengths, tokens, w_all, q, k, v, c, dr1, d_up, d_down, lse, dvec_ffn
        )
        s_vec = lax.dynamic_slice_in_dim(s_vec, lax.axis_index("dp") * part, part, axis=1)
    else:
        input_grad, d_attention, dvec_att = attn_bwd(segment_lengths, tokens, w_all, q, k, v, c, lse, dr1)
        d_vec = dvec_ffn + dvec_att
        flat = lambda g: g.astype(F32).reshape(-1, width)
        s_attention = lax.psum_scatter(flat(d_attention), ("dp", "tensor"), scatter_dimension=0, tiled=True)
        s_up, s_down = (lax.psum_scatter(flat(g), ("tensor", "dp"), scatter_dimension=0, tiled=True) for g in (d_up, d_down))
        s_vec = lax.psum(lax.psum_scatter(d_vec, "dp", scatter_dimension=1, tiled=True), "tensor")
    s_vec = s_vec[:columns].T

    attention_new = adam(attention_master, attention_mean, attention_square, s_attention, matrix_rate, weight_decay)
    up_new = adam(up_master, up_mean, up_square, s_up, matrix_rate, weight_decay)
    down_new = adam(down_master, down_mean, down_square, s_down, matrix_rate, weight_decay)
    vector_new = adam(vector_master, vector_mean, vector_square, s_vec, vector_rate, 0.0)
    return (block_output, input_grad, *attention_new, *up_new, *down_new, *vector_new)


def solution(mesh):
    rows, cols = P(("dp", "tensor")), P("dp", "tensor")
    own_plan = mesh.shape["dp"] == 8 and mesh.shape["tensor"] == 4
    return jax.shard_map(
        functools.partial(shards, own_plan),
        mesh=mesh,
        in_specs=(rows,) * 6 + (cols,) * 6 + (P("dp"),) * 3,
        out_specs=(rows,) * 5 + (cols,) * 6 + (P("dp"),) * 3,
        check_vma=False,
    )
```

```python
import functools

import jax
import jax.numpy as jnp
from jax import lax
from jax.experimental import pallas as pl
from jax.experimental.pallas import tpu as pltpu
from jax.sharding import PartitionSpec as P


HEAD_DIM = 64
MEM = 10
norm_epsilon = 1e-12
inv_root_two = 0.7071067811865476
inv_root_tau = 0.3989422804014327
F32, BF = jnp.float32, jnp.bfloat16
NT = (((1,), (1,)), ((), ()))
TN = (((0,), (0,)), ((), ()))
NN = (((1,), (0,)), ((), ()))

def mm(a, b, dims=NN):
    return lax.dot_general(a, b, dims, preferred_element_type=F32)

def whole(shape=None):
    return pl.BlockSpec(memory_space=pltpu.VMEM)

def norm_stats(signal, width):
    centre = signal - jnp.sum(signal, axis=-1, keepdims=True) * (1.0 / width)
    inverse = lax.rsqrt(jnp.sum(centre * centre, axis=-1, keepdims=True) * (1.0 / width) + norm_epsilon)
    return centre * inverse, inverse

def norm_back(up, scaled, inverse, width):
    return inverse * (up - jnp.sum(up, axis=-1, keepdims=True) * (1.0 / width)
                      - scaled * (jnp.sum(up * scaled, axis=-1, keepdims=True) * (1.0 / width)))

def attn_fwd_kernel(seg_rows, len_ref, x_ref, w_ref, tab_ref, q_ref, k_ref, v_ref, c_ref, n_ref, inv_ref, ab_ref, lse_ref, xs, ct):
    rows, width = xs.shape
    heads = width // HEAD_DIM
    xs[pl.ds(0, seg_rows), :] = x_ref[0]
    xs[pl.ds(seg_rows, rows - seg_rows), :] = jnp.zeros((rows - seg_rows, width), BF)
    x = xs[...]
    q_ref[0] = ((mm(x, w_ref[0]) + tab_ref[0:1, :]).astype(BF) * BF(HEAD_DIM ** -0.5)).astype(BF)
    k_ref[0] = mm(x, w_ref[1]).astype(BF)
    v_ref[0] = (mm(x, w_ref[2]) + tab_ref[1:2, :]).astype(BF)
    live = len_ref[pl.program_id(0)] + MEM
    key_at = lax.broadcasted_iota(jnp.int32, (rows, 1), 0)
    usable = (key_at < live) | ((key_at >= seg_rows - MEM) & (key_at < seg_rows))
    bias = jnp.where(usable, 0.0, -1e30).astype(F32)
    lane = lax.broadcasted_iota(jnp.int32, (rows, 2 * HEAD_DIM), 1)
    zero = jnp.zeros((), BF)

    def pair(i, carry):
        at = pl.ds(pl.multiple_of(i * 2 * HEAD_DIM, 2 * HEAD_DIM), 2 * HEAD_DIM)
        q2, k2, v2 = q_ref[0, :, at], k_ref[0, :, at], v_ref[0, :, at]
        vt = v2.T
        for h in range(2):
            mine = (lane < HEAD_DIM) if h == 0 else (lane >= HEAD_DIM)
            qh = jnp.where(mine, q2, zero)
            s = mm(k2, qh, NT) + bias
            top = jnp.max(s, axis=0, keepdims=True)
            e = jnp.exp(s - top)
            tot = jnp.sum(e, axis=0, keepdims=True)
            p = (e * (1.0 / tot)).astype(BF)
            ct[pl.ds(pl.multiple_of(i * 2 * HEAD_DIM + h * HEAD_DIM, HEAD_DIM), HEAD_DIM), :] = mm(vt[h * HEAD_DIM:(h + 1) * HEAD_DIM], p)
            lse_ref[0, pl.ds(2 * i + h, 1), :] = top + jnp.log(tot)
        return carry
    lax.fori_loop(0, heads // 2, pair, 0)
    c = ct[...].T.astype(BF)
    c_ref[0] = c
    r = x.astype(F32) + mm(c, w_ref[3]) + tab_ref[2:3, :]
    n, inv = norm_stats(r, width)
    n_ref[0] = n
    inv_ref[0] = jnp.broadcast_to(inv, (rows, 128))
    ab_ref[0] = (n * tab_ref[3:4, :] + tab_ref[4:5, :]).astype(BF)

def attn_fwd(lengths, tokens, weights, table):
    segs, seg_rows, width = tokens.shape
    rows = -(-seg_rows // 16) * 16
    heads = width // HEAD_DIM
    hp = -(-heads // 8) * 8
    seg = lambda *s: pl.BlockSpec((1,) + s, lambda i, L: (i,) + (0,) * len(s))
    full = lambda *s: pl.BlockSpec(s, lambda i, L: (0,) * len(s), pipeline_mode=pl.Buffered(1))
    sd = jax.ShapeDtypeStruct
    return pl.pallas_call(
        functools.partial(attn_fwd_kernel, seg_rows),
        grid_spec=pltpu.PrefetchScalarGridSpec(
            num_scalar_prefetch=1, grid=(segs,),
            in_specs=[seg(seg_rows, width), full(*weights.shape), full(*table.shape)],
            out_specs=[seg(rows, width)] * 5 + [seg(rows, 128), seg(rows, width), seg(hp, rows)],
            scratch_shapes=[pltpu.VMEM((rows, width), BF), pltpu.VMEM((width, rows), F32)]),
        out_shape=[sd((segs, rows, width), BF)] * 4 + [sd((segs, rows, width), F32), sd((segs, rows, 128), F32), sd((segs, rows, width), BF), sd((segs, hp, rows), F32)],
        compiler_params=pltpu.CompilerParams(vmem_limit_bytes=56 << 20),
        name="attention_forward",
    )(lengths, tokens, weights, table)

def ffn_kernel(seg_rows, block, ab_ref, n1_ref, inv_ref, cot_ref, up_ref, down_ref, tab_ref,
               out_ref, dr1_ref, dup_ref, ddown_ref, dvec_ref, hid, slope, dy, du):
    segs, rows, width = n1_ref.shape
    total = segs * rows
    chunks = up_ref.shape[0]
    per = rows // block
    nb = total // block
    def rb(i):
        return pl.ds(pl.multiple_of(i * block, block), block)
    y = dr1_ref
    def fwd(i, carry):
        a = ab_ref[rb(i), :]
        acc = jnp.zeros((block, width), F32)
        for j in range(chunks):
            u = mm(a, up_ref[j]) + tab_ref[8 + j:9 + j, :]
            phi = 0.5 * (1.0 + lax.erf(u * inv_root_two))
            h = (u * phi).astype(BF)
            hid[j, rb(i), :] = h
            slope[j, rb(i), :] = phi + u * jnp.exp(-0.5 * u * u) * inv_root_tau
            acc = acc + mm(h, down_ref[j], NT)
        y[rb(i), :] = acc
        return carry
    lax.fori_loop(0, nb, fwd, 0)
    dvec_ref[...] = jnp.zeros_like(dvec_ref)
    for s in range(segs):
        at = pl.ds(s * rows, rows)
        n1 = n1_ref[s]
        r2 = n1 * tab_ref[3:4, :] + tab_ref[4:5, :] + (y[at, :] + tab_ref[7:8, :])
        n2, inv2 = norm_stats(r2, width)
        out_ref[s] = (n2 * tab_ref[5:6, :] + tab_ref[6:7, :])[:seg_rows].astype(BF)
        live = lax.broadcasted_iota(jnp.int32, (rows, 1), 0) < seg_rows
        e = jnp.concatenate([cot_ref[s].astype(F32), jnp.zeros((rows - seg_rows, width), F32)], axis=0)
        dvec_ref[5:6, :] += jnp.sum(e * n2, axis=0, keepdims=True)
        dvec_ref[6:7, :] += jnp.sum(e, axis=0, keepdims=True)
        dr2 = norm_back(e * tab_ref[5:6, :], n2, inv2, width)
        d16 = dr2.astype(BF)
        y[at, :] = dr2
        dy[at, :] = d16
        dvec_ref[7:8, :] += jnp.sum(d16.astype(F32), axis=0, keepdims=True)
    dyt = dy[...].T
    abt = ab_ref[...].T
    for j in range(chunks):
        def back(i, carry):
            g = dy[rb(i), :]
            d = (mm(g, down_ref[j]) * slope[j, rb(i), :]).astype(BF)
            du[rb(i), :] = d
            return carry + jnp.sum(d.astype(F32), axis=0, keepdims=True)
        dvec_ref[8 + j:9 + j, :] = lax.fori_loop(0, nb, back, jnp.zeros((1, width), F32))
        ddown_ref[j] = mm(dyt, hid[j]).astype(BF)
        dup_ref[j] = mm(abt, du[...]).astype(BF)
        def inner(i, carry):
            part = mm(du[rb(i), :], up_ref[j], NT)
            slope[0, rb(i), :] = part if j == 0 else slope[0, rb(i), :] + part
            return carry
        lax.fori_loop(0, nb, inner, 0)
    for s in range(segs):
        at = pl.ds(s * rows, rows)
        da = y[at, :] + slope[0, at, :].astype(BF).astype(F32)
        n1 = n1_ref[s]
        dvec_ref[3:4, :] += jnp.sum(da * n1, axis=0, keepdims=True)
        dvec_ref[4:5, :] += jnp.sum(da, axis=0, keepdims=True)
        dr1 = norm_back(da * tab_ref[3:4, :], n1, inv_ref[s][:, 0:1], width)
        dr1_ref[at, :] = dr1
        dvec_ref[2:3, :] += jnp.sum(dr1.astype(BF).astype(F32), axis=0, keepdims=True)

def ffn(ab, n1, inv, cot, up, down, table):
    segs, rows, width = n1.shape
    seg_rows = cot.shape[1]
    total = segs * rows
    chunks = up.shape[0]
    sd = jax.ShapeDtypeStruct
    return pl.pallas_call(
        functools.partial(ffn_kernel, seg_rows, rows // 2),
        in_specs=[whole()] * 7, out_specs=[whole()] * 5,
        out_shape=[sd(cot.shape, BF), sd((total, width), F32), sd(up.shape, BF), sd(down.shape, BF), sd((16, width), F32)],
        scratch_shapes=[pltpu.VMEM((chunks, total, width), BF), pltpu.VMEM((chunks, total, width), F32), pltpu.VMEM((total, width), BF), pltpu.VMEM((total, width), BF)],
        compiler_params=pltpu.CompilerParams(vmem_limit_bytes=63 << 20),
        name="feed_forward",
    )(ab.reshape(total, width), n1, inv, cot, up, down, table)

def attn_bwd_kernel(seg_rows, len_ref, x_ref, w_ref, q_ref, k_ref, v_ref, c_ref, lse_ref, dr1_ref,
                    ig_ref, dw_ref, dvec_ref, dao, dc, dq, dk, dv, xs):
    segs, rows, width = q_ref.shape
    total = segs * rows
    heads = width // HEAD_DIM
    for s in range(segs):
        xs[pl.ds(s * rows, seg_rows), :] = x_ref[s]
        xs[pl.ds(s * rows + seg_rows, rows - seg_rows), :] = jnp.zeros((rows - seg_rows, width), BF)
    dao[...] = dr1_ref[...].astype(BF)
    dw_ref[3] = mm(c_ref[...].reshape(total, width).T, dao[...]).astype(BF)
    dc[...] = mm(dao[...], w_ref[3], NT).astype(BF)
    key_at = lax.broadcasted_iota(jnp.int32, (rows, 1), 0)
    lane = lax.broadcasted_iota(jnp.int32, (rows, 2 * HEAD_DIM), 1)
    zero = jnp.zeros((), BF)
    for s in range(segs):
        live = len_ref[s] + MEM
        usable = (key_at < live) | ((key_at >= seg_rows - MEM) & (key_at < seg_rows))
        bias = jnp.where(usable, 0.0, -1e30).astype(F32)
        at_rows = pl.ds(s * rows, rows)
        def pair(i, carry):
            at = pl.ds(pl.multiple_of(i * 2 * HEAD_DIM, 2 * HEAD_DIM), 2 * HEAD_DIM)
            q2, k2, v2 = q_ref[s, :, at], k_ref[s, :, at], v_ref[s, :, at]
            g2 = dc[at_rows, at]
            kt = k2.T
            dvp = jnp.zeros((rows, 2 * HEAD_DIM), F32)
            dkp = jnp.zeros((rows, 2 * HEAD_DIM), F32)
            dqt = []
            for h in range(2):
                mine = (lane < HEAD_DIM) if h == 0 else (lane >= HEAD_DIM)
                qh = jnp.where(mine, q2, zero)
                gh = jnp.where(mine, g2, zero)
                p = jnp.exp((mm(k2, qh, NT) + bias) - lse_ref[s, pl.ds(2 * i + h, 1), :])
                dp = mm(v2, gh, NT)
                dvp = dvp + mm(p.astype(BF), gh)
                ds = (p * (dp - jnp.sum(p * dp, axis=0, keepdims=True))).astype(BF)
                dkp = dkp + mm(ds, qh)
                dqt.append(mm(kt[h * HEAD_DIM:(h + 1) * HEAD_DIM], ds))
            dv[at_rows, at] = dvp.astype(BF)
            dk[at_rows, at] = dkp.astype(BF)
            dq[at_rows, at] = (jnp.concatenate(dqt, axis=0).T * (HEAD_DIM ** -0.5)).astype(BF)
            return carry
        lax.fori_loop(0, heads // 2, pair, 0)
    xt = xs[...].T
    dvec_ref[...] = jnp.zeros_like(dvec_ref)
    for j, g in enumerate((dq, dk, dv)):
        dw_ref[j] = mm(xt, g[...]).astype(BF)
    dvec_ref[0:1, :] = jnp.sum(dq[...].astype(F32), axis=0, keepdims=True)
    dvec_ref[1:2, :] = jnp.sum(dv[...].astype(F32), axis=0, keepdims=True)
    for s in range(segs):
        at = pl.ds(s * rows, rows)
        r = dr1_ref[at, :] + mm(dq[at, :], w_ref[0], NT) + mm(dk[at, :], w_ref[1], NT) + mm(dv[at, :], w_ref[2], NT)
        ig_ref[s] = r[:seg_rows]

def attn_bwd(lengths, tokens, weights, q, k, v, c, lse, dr1):
    segs, seg_rows, width = tokens.shape
    rows = q.shape[1]
    total = segs * rows
    sd = jax.ShapeDtypeStruct
    return pl.pallas_call(
        functools.partial(attn_bwd_kernel, seg_rows),
        in_specs=[pl.BlockSpec(memory_space=pltpu.SMEM)] + [whole()] * 8, out_specs=[whole()] * 3,
        out_shape=[sd(tokens.shape, F32), sd(weights.shape, BF), sd((16, width), F32)],
        scratch_shapes=[pltpu.VMEM((total, width), BF)] * 6,
        compiler_params=pltpu.CompilerParams(vmem_limit_bytes=63 << 20),
        name="attention_backward",
    )(lengths, tokens, weights, q, k, v, c, lse, dr1)

MESH = pl.DeviceIdType.MESH
DMA = pltpu.SemaphoreType.DMA
SHAPE = {"z": 4, "x": 2, "y": 2, "c": 2}
ATT, FFN = "zxyc", "yczx"
ROUTES = ("zxy", "zyx", "xzy", "zyx", "zxy", "yzx")


def place():
    d, t = lax.axis_index("dp"), lax.axis_index("tensor")
    return d // 2, d % 2, t // 2, t % 2


def dev(z, x, y, c):
    return {"dp": z * 2 + x, "tensor": y * 2 + c}


def partners(z, x, y, c):
    return {"x": (z, 1 - x, y, c), "y": (z, x, 1 - y, c), "c": (z, x, y, 1 - c), **{i: ((z + i) % 4, x, y, c) for i in (1, 2, 3)}}


def greet(*here):
    b = pltpu.get_barrier_semaphore()
    for p in partners(*here).values():
        pl.semaphore_signal(b, inc=1, device_id=dev(*p), device_id_type=MESH)
    pl.semaphore_wait(b, 6)


class Legs:
    def __init__(self, here, ssem, rsem):
        self.here, self.peer = dict(zip("zxyc", here)), partners(*here)
        self.ssem, self.rsem, self.make = ssem, rsem, {}

    def add(self, key, src, dst, peer):
        i = len(self.make)
        self.make[key] = lambda: pltpu.make_async_remote_copy(
            src(), dst(), self.ssem.at[i], self.rsem.at[i], device_id=dev(*self.peer[peer]), device_id_type=MESH)

    def start(self, *keys):
        for k in keys:
            self.make[k]().start()

    def got(self, *keys):
        for k in keys:
            self.make[k]().wait_recv()

    def sent(self):
        for m in self.make.values():
            m().wait_send()


def view_of(ref, order, cols):
    return lambda at, rows: ref.at[tuple(at.get(ch, slice(None)) for ch in order) + (rows, cols)]


class GatherUnit:
    def __init__(self, legs, key, view, r0, nr, route):
        self.legs, self.key, self.steps = legs, key, [([], [])]
        me = legs.here
        c = {"c": me["c"]}
        full = pl.ds(r0, nr)

        def leg(name, peer, at):
            f = functools.partial(view, at, full)
            legs.add((key, name), f, f, peer)
            self.steps[-1][1].append((key, name))

        for n, d in enumerate(route + "c"):
            fixed = {**c, **{e: me[e] for e in route[n:]}}
            names = [(d, i) for i in (1, 2, 3)] if d == "z" else [(d, d)]
            for name in names:
                leg(name, name[1], fixed)
            self.steps.append(([(key, name) for name in names], []))

    def go(self, n):
        self.legs.got(*self.steps[n][0])
        self.legs.start(*self.steps[n][1])


class SumUnit:
    @staticmethod
    def buffers(order, nr, nc, route):
        inner = order.replace("c", "")
        out, gone = [], ""
        for d in "c" + route:
            gone += d
            out += [tuple(SHAPE[ch] for ch in inner if ch not in gone) + (nr, nc)] * (3 if d == "z" else 1)
        return out

    def __init__(self, legs, key, given, own, bufs, r0, nr, order, route, finish, ready=None):
        self.legs, self.key, self.own, self.finish, self.ready = legs, key, own, finish, ready
        self.inner = order.replace("c", "")
        self.rows = pl.ds(r0, nr)
        me, bufs, done = legs.here, list(bufs), {"c": legs.here["c"]}
        self.work = []
        for d in "c" + route:
            names = [(d, i) for i in (1, 2, 3)] if d == "z" else [(d, d)]
            got = []
            for name in names:
                to = (me["z"] + name[1]) % 4 if d == "z" else 1 - me[d]
                b = bufs.pop(0)
                got.append(b)
                legs.add((key, name), functools.partial(given if d == "c" else own, {**done, d: to}, self.rows), functools.partial(lambda b: b, b), name[1])
            done = {**done, d: me[d]}
            self.work.append(([(key, name) for name in names], dict(done), got))

    def begin(self):
        self.legs.start(*self.work[0][0])

    def go(self, n):
        names, at, bufs = self.work[n]
        self.legs.got(*names)
        if n == 0 and self.ready is not None:
            self.ready()
        free = [ch for ch in self.inner if ch not in at]

        def total(ref, cut):
            t = ref[...].astype(jnp.float32)
            for b in bufs:
                t = t + cut(b).astype(jnp.float32)
            return t
        if n == len(self.work) - 1:
            self.finish(self.rows, total(self.own(at, self.rows), lambda b: b[...]))
            return
        ch = free[0]

        def body(i, carry):
            ref = self.own({**at, ch: i}, self.rows)
            ref[...] = total(ref, lambda b: b[i]).astype(jnp.bfloat16)
            return carry
        lax.fori_loop(0, SHAPE[ch], body, 0)
        self.legs.start(*self.work[n + 1][0])


N_FORWARD_LEGS = 18 * 6 + 4
GATHER_FIRST = ((0, 0),), ((0, 1), (1, 0)), ((0, 2), (2, 0)), ((0, 3), (1, 1), (3, 0), (4, 0), (5, 0))
GATHER_SLOTS = {
    0: ((1, 2), (2, 1)),
    4: ((1, 3), (2, 2), (3, 1)),
    6: ((4, 1),),
    8: ((1, 4), (5, 1), (6, 0)),
    10: ((2, 3), (3, 2), (7, 0)),
    12: ((4, 2), (8, 0)),
    14: ((5, 2), (6, 1)),
    16: ((2, 4), (3, 3), (7, 1)),
    18: ((4, 3), (6, 2), (8, 1)),
    20: ((5, 3), (7, 2)),
    24: ((6, 3), (8, 2)),
    28: ((7, 3),),
    32: ((8, 3),),
}


def forward_kernel(seg_rows, len_ref, tok, cot, am, um, dm, vp,
                   out_o, q_o, k_o, v_o, c_o, w_o, dr1_o, dup_o, ddn_o, lse_ref, dvec_ref,
                   wa, wu, wd, vec, tab, traw, craw, xs, cs, q, k, v, ct, cc, n1, inv, ab, hid, slo, dy, dyt, abt,
                   ssem, rsem, lsem):
    segs, rows, width = q_o.shape
    total = segs * rows
    heads = width // HEAD_DIM
    part = am.shape[0]
    z, x, y, c = here = place()
    lt = pltpu.make_async_copy(tok, traw, lsem.at[0]); lt.start()
    lc = pltpu.make_async_copy(cot, craw, lsem.at[1]); lc.start()
    wa[z, x, y, c] = am[...].astype(BF)
    wu[y, c, z, x] = um[...].astype(BF)
    wd[y, c, z, x] = dm[...].astype(BF)
    vec[z, x] = vp[...]

    legs = Legs(here, ssem, rsem)
    pair_w = 2 * HEAD_DIM
    groups = width // (2 * pair_w)
    units = []
    for name, ref, order in (("a", wa, ATT), ("u", wu, FFN), ("d", wd, FFN)):
        for h in range(2 * groups):
            units.append(GatherUnit(legs, (name, h), view_of(ref, order, pl.ds(h * pair_w, pair_w)), 0, part, ROUTES[h]))
    here_vec = lambda: vec.at[z, x]
    for i in (1, 2, 3):
        legs.add(("v", i), here_vec, here_vec, i)
    legs.add("vx", lambda: vec.at[:, x], lambda: vec.at[:, x], "x")

    def advance(what):
        for i, n in what:
            for unit in units[2 * i:2 * i + 2]:
                unit.go(n)

    greet(*here)
    advance(GATHER_FIRST[0])
    legs.start(*[("v", i) for i in (1, 2, 3)])
    lt.wait()
    for s in range(segs):
        xs[pl.ds(s * rows, seg_rows), :] = traw[s]
        xs[pl.ds(s * rows + seg_rows, rows - seg_rows), :] = jnp.zeros((rows - seg_rows, width), BF)
    advance(GATHER_FIRST[1])
    legs.got(*[("v", i) for i in (1, 2, 3)])
    legs.start("vx")
    advance(GATHER_FIRST[2])
    lc.wait()
    for s in range(segs):
        cs[pl.ds(s * rows, seg_rows), :] = craw[s]
        cs[pl.ds(s * rows + seg_rows, rows - seg_rows), :] = jnp.zeros((rows - seg_rows, width), BF)
    advance(GATHER_FIRST[3])
    legs.got("vx")
    lane_in = lax.broadcasted_iota(jnp.int32, (128, width), 0)
    lane_out = lax.broadcasted_iota(jnp.int32, (128, width), 1)
    acc = jnp.zeros((16, width), F32)
    for d in range(8):
        move = ((lane_out == lane_in + d * part) & (lane_in < part)).astype(BF)
        acc = acc + mm(vec[d // 2, d % 2], move)
    tab[...] = acc
    advance(((0, 4),))
    lane = lax.broadcasted_iota(jnp.int32, (rows, pair_w), 1)
    key_at = lax.broadcasted_iota(jnp.int32, (rows, 1), 0)
    zero = jnp.zeros((), BF)

    def body(it, carry):
        for n in range(0, 8 * groups, 2):
            if n in GATHER_SLOTS:
                pl.when(2 * it == n)(functools.partial(lambda n: advance(GATHER_SLOTS[n]), n))
        g = it // 4

        @pl.when(it % 4 == 0)
        def _():
            col = pl.ds(pl.multiple_of(g * 2 * pair_w, 2 * pair_w), 2 * pair_w)
            w3 = [wa[m, :, :, :, :, col].reshape(width, 2 * pair_w) for m in range(3)]
            xx = xs[...]
            q[:, col] = ((mm(xx, w3[0]) + tab[0:1, col]).astype(BF) * BF(HEAD_DIM ** -0.5)).astype(BF)
            k[:, col] = mm(xx, w3[1]).astype(BF)
            v[:, col] = (mm(xx, w3[2]) + tab[1:2, col]).astype(BF)

        s = (it // 2) % 2
        i = 2 * g + it % 2
        col = pl.ds(pl.multiple_of(i * pair_w, pair_w), pair_w)
        rr = pl.ds(pl.multiple_of(s * rows, 16), rows)
        live = len_ref[s] + MEM
        usable = (key_at < live) | ((key_at >= seg_rows - MEM) & (key_at < seg_rows))
        bias = jnp.where(usable, 0.0, -1e30).astype(F32)
        q2, k2, v2 = q[rr, col], k[rr, col], v[rr, col]
        vt = v2.T
        for h in range(2):
            mine = (lane < HEAD_DIM) if h == 0 else (lane >= HEAD_DIM)
            if h == 1:
                for n in range(1, 8 * groups, 2):
                    if n in GATHER_SLOTS:
                        pl.when(2 * it + 1 == n)(functools.partial(lambda n: advance(GATHER_SLOTS[n]), n))
            sc = mm(k2, jnp.where(mine, q2, zero), NT) + bias
            top = jnp.max(sc, axis=0, keepdims=True)
            e = jnp.exp(sc - top)
            tot = jnp.sum(e, axis=0, keepdims=True)
            p = (e * (1.0 / tot)).astype(BF)
            at = pl.ds(pl.multiple_of(i * pair_w + h * HEAD_DIM, HEAD_DIM), HEAD_DIM)
            ct[s, at, :] = mm(vt[h * HEAD_DIM:(h + 1) * HEAD_DIM], p).astype(BF)
            lse_ref[s, pl.ds(2 * i + h, 1), :] = top + jnp.log(tot)
        return carry
    lax.fori_loop(0, 4 * groups, body, 0)

    spill = [pltpu.make_async_copy(a.at[pl.ds(s * rows, rows)], o.at[s], lsem.at[2 + 2 * n + s]) for n, (a, o) in enumerate(((q, q_o), (k, k_o), (v, v_o))) for s in range(segs)]
    for cp in spill:
        cp.start()
    wcopy = pltpu.make_async_copy(wa, w_o, lsem.at[8]); wcopy.start()
    for s in range(segs):
        rr = pl.ds(s * rows, rows)
        cs_ = ct[s].T
        cc[rr, :] = cs_
        r = xs[rr, :].astype(F32) + mm(cs_, wa[3].reshape(width, width)) + tab[2:3, :]
        n, iv = norm_stats(r, width)
        n1[rr, :] = n
        inv[rr, :] = jnp.broadcast_to(iv, (rows, 128))
        ab[rr, :] = (n * tab[3:4, :] + tab[4:5, :]).astype(BF)
    ccopy = [pltpu.make_async_copy(cc.at[pl.ds(s * rows, rows)], c_o.at[s], lsem.at[9 + s]) for s in range(segs)]
    for cp in ccopy:
        cp.start()

    block = rows // 2
    nb = total // block
    chunks = 4
    def rb(i):
        return pl.ds(pl.multiple_of(i * block, 16), block)
    def up(j):
        return wu[j // 2, j % 2].reshape(width, width)
    def down(j):
        return wd[j // 2, j % 2].reshape(width, width)
    advance(((3, 4), (4, 4), (5, 4)))

    def fwd(i, carry):
        a = ab[rb(i), :]
        for j in range(chunks):
            for n in range(nb):
                if 8 * groups + 4 * n + j in GATHER_SLOTS:
                    pl.when(i == n)(functools.partial(lambda n: advance(GATHER_SLOTS[n]), 8 * groups + 4 * n + j))
            u = mm(a, up(j)) + tab[8 + j:9 + j, :]
            phi = 0.5 * (1.0 + lax.erf(u * inv_root_two))
            hid[j, rb(i), :] = (u * phi).astype(BF)
            slo[j, rb(i), :] = (phi + u * jnp.exp(-0.5 * u * u) * inv_root_tau).astype(BF)
        return carry
    lax.fori_loop(0, nb, fwd, 0)
    advance(((6, 4), (7, 4), (8, 4)))
    dvec_ref[...] = jnp.zeros_like(dvec_ref)
    def mid(i, carry):
        yy = tab[7:8, :]
        for j in range(chunks):
            yy = yy + mm(hid[j, rb(i), :], down(j), NT)
        nn = n1[rb(i), :]
        r2 = nn * tab[3:4, :] + tab[4:5, :] + yy
        n2, inv2 = norm_stats(r2, width)
        e = cs[rb(i), :].astype(F32)
        cs[rb(i), :] = (n2 * tab[5:6, :] + tab[6:7, :]).astype(BF)
        dvec_ref[5:6, :] += jnp.sum(e * n2, axis=0, keepdims=True)
        dvec_ref[6:7, :] += jnp.sum(e, axis=0, keepdims=True)
        dr2 = norm_back(e * tab[5:6, :], n2, inv2, width)
        g16 = dr2.astype(BF)
        dy[rb(i), :] = g16
        dvec_ref[7:8, :] += jnp.sum(g16.astype(F32), axis=0, keepdims=True)
        da = jnp.zeros((block, width), F32)
        for j in range(chunks):
            d16 = (mm(g16, down(j)) * slo[j, rb(i), :].astype(F32)).astype(BF)
            slo[j, rb(i), :] = d16
            dvec_ref[8 + j:9 + j, :] += jnp.sum(d16.astype(F32), axis=0, keepdims=True)
            da = da + mm(d16, up(j), NT)
        da = dr2 + da.astype(BF).astype(F32)
        dvec_ref[3:4, :] += jnp.sum(da * nn, axis=0, keepdims=True)
        dvec_ref[4:5, :] += jnp.sum(da, axis=0, keepdims=True)
        dr1 = norm_back(da * tab[3:4, :], nn, inv[rb(i), 0:1], width)
        n1[rb(i), :] = dr1
        dvec_ref[2:3, :] += jnp.sum(dr1.astype(BF).astype(F32), axis=0, keepdims=True)
        return carry
    lax.fori_loop(0, nb, mid, 0)
    dcopy = pltpu.make_async_copy(n1, dr1_o, lsem.at[0]); dcopy.start()
    for s in range(segs):
        craw[s] = cs[pl.ds(s * rows, seg_rows), :]
    ocopy = pltpu.make_async_copy(craw, out_o, lsem.at[1]); ocopy.start()
    dyt[...] = dy[...].T
    abt[...] = ab[...].T
    legs.sent()
    def grad_copies(j):
        return (pltpu.make_async_copy(wd.at[j // 2, j % 2], ddn_o.at[j // 2, j % 2], lsem.at[11 + 2 * (j % 2)]),
                pltpu.make_async_copy(wu.at[j // 2, j % 2], dup_o.at[j // 2, j % 2], lsem.at[12 + 2 * (j % 2)]))
    def grads(j, carry):
        shape = wd.shape[2:]
        @pl.when(j >= 2)
        def _():
            for cp in grad_copies(j - 2):
                cp.wait()
        wd[j // 2, j % 2] = mm(dyt[...], hid[j]).astype(BF).reshape(shape)
        wu[j // 2, j % 2] = mm(abt[...], slo[j]).astype(BF).reshape(shape)
        for cp in grad_copies(j):
            cp.start()
        return carry
    lax.fori_loop(0, chunks, grads, 0)
    for j in (2, 3):
        for cp in grad_copies(j):
            cp.wait()
    for cp in spill + [wcopy, dcopy, ocopy] + ccopy:
        cp.wait()

def forward(lengths, tokens, cotangent, att, up, down, piece):
    segs, seg_rows, width = tokens.shape
    part = att.shape[0]
    rows = -(-seg_rows // 16) * 16
    total = segs * rows
    hp = -(-(width // HEAD_DIM) // 8) * 8
    sd = jax.ShapeDtypeStruct
    any_, vm = pl.BlockSpec(memory_space=pl.ANY), whole()
    wshape, fshape = (4, 2, 2, 2, part, width), (2, 2, 4, 2, part, width)
    V = lambda *s, t=BF: pltpu.VMEM(s, t)
    return pl.pallas_call(
        functools.partial(forward_kernel, seg_rows),
        in_specs=[pl.BlockSpec(memory_space=pltpu.SMEM), any_, any_, vm, vm, vm, vm],
        out_specs=[any_] * 9 + [vm, vm],
        out_shape=[sd(cotangent.shape, BF)] + [sd((segs, rows, width), BF)] * 4 + [sd(wshape, BF), sd((total, width), F32), sd(fshape, BF), sd(fshape, BF), sd((segs, hp, rows), F32), sd((16, width), F32)],
        scratch_shapes=[V(*wshape), V(*fshape), V(*fshape), V(4, 2, 16, 128), V(16, width, t=F32), V(segs, seg_rows, width), V(segs, seg_rows, width),
                        V(total, width), V(total, width), V(total, width), V(total, width), V(total, width), V(segs, width, rows), V(total, width),
                        V(total, width, t=F32), V(total, 128, t=F32), V(total, width), V(4, total, width), V(4, total, width), V(total, width), V(width, total), V(width, total),
                        DMA((N_FORWARD_LEGS,)), DMA((N_FORWARD_LEGS,)), DMA((15,))],
        compiler_params=pltpu.CompilerParams(collective_id=0, has_side_effects=True, vmem_limit_bytes=63 << 20),
        name="forward_and_feed_forward_backward",
    )(lengths, tokens, cotangent, att, up, down, piece)

N_BACK_LEGS = 18 * 6 + 6
SUM_SLOTS = ((0, 4, 8, 12),) * 3 + ((4, 10, 16, 22),) * 3 + ((10, 16, 22, 24), (18, 22, 25, 27), (24, 26, 28, 30))


def sum_plan(width):
    pw = 2 * HEAD_DIM
    return [((name, h), h * pw, pw, order, ROUTES[h][::-1]) for name, order in (("u", FFN), ("d", FFN), ("a", ATT)) for h in range(width // pw)]


def backward_kernel(seg_rows, n_bufs, len_ref, tok, w_i, q_i, k_i, v_i, c_i, dr1_i, dup, ddn, lse_ref, dvec_in,
                    ig_o, ga_ref, gu_ref, gd_ref, gv_ref,
                    wa, ga, q, k, v, cc, r1f, traw, xt, dao, own_u, own_d, vbuf, *rest):
    bufs, (ssem, rsem, lsem) = list(rest[:n_bufs]), rest[n_bufs:]
    segs, rows, width = q_i.shape
    total = segs * rows
    heads = width // HEAD_DIM
    pair_w = 2 * HEAD_DIM
    groups = width // (2 * pair_w)
    part = ga_ref.shape[0]
    z, x, y, c = here = place()
    legs = Legs(here, ssem, rsem)

    load = {}
    def local(name, src, dst, i):
        load[name] = pltpu.make_async_copy(src, dst, lsem.at[i])
        load[name].start()
    local("dr1", dr1_i, r1f, 0)
    local("w", w_i, wa, 1)
    for s in range(segs):
        rr = pl.ds(s * rows, rows)
        local(("c", s), c_i.at[s], cc.at[rr], 2 + s)
        local(("v", s), v_i.at[s], v.at[rr], 4 + s)
        local(("k", s), k_i.at[s], k.at[rr], 6 + s)
        local(("q", s), q_i.at[s], q.at[rr], 8 + s)
    local("t", tok, traw, 10)

    local("u", dup.at[:, c], own_u, 11)
    local("d", ddn.at[:, c], own_d, 12)
    loaded = set()
    def need(name):
        if name not in loaded:
            loaded.add(name)
            load[name].wait()

    units = {}
    for key, c0, nc, order, route in sum_plan(width):
        mine = bufs[:6]
        del bufs[:6]
        col = pl.ds(c0, nc)
        if key[0] == "a":
            given = own = view_of(ga, ATT, col)
            out, ready = ga_ref, None
        else:
            given = view_of(dup if key[0] == "u" else ddn, FFN, col)
            own = view_of(own_u if key[0] == "u" else own_d, "yzx", col)
            out, ready = (gu_ref, gd_ref)[key[0] == "d"], functools.partial(need, key[0])
        def finish(rr, total, out=out, col=col):
            out[rr, col] = total
        units[key] = SumUnit(legs, key, given, own, mine, 0, part, order, route, finish, ready)
    F = lambda i: [("ud"[i // groups], 2 * (i % groups) + h) for h in range(2)]
    A = lambda g: [("a", 2 * g), ("a", 2 * g + 1)]
    def begin(keys):
        for key in keys:
            units[key].begin()
    def stage(keys, n):
        for key in keys:
            units[key].go(n)

    legs.add("v0", lambda: vbuf.at[0], lambda: vbuf.at[1], "c")
    legs.add("v1", lambda: vbuf.at[2], lambda: vbuf.at[3], "y")
    legs.add("v2", lambda: vbuf.at[4], lambda: vbuf.at[5], "x")
    for i in (1, 2, 3):
        legs.add(("v", i), lambda: vbuf.at[6 + z], lambda: vbuf.at[6 + z], i)

    greet(*here)
    for i in range(2 * groups):
        begin(F(i))
    load["dr1"].wait()
    dao[...] = r1f[...].astype(BF)
    for s in range(segs):
        load["c", s].wait()
    load["w"].wait()
    ga[3] = mm(cc[...].T, dao[...]).astype(BF).reshape(ga.shape[1:])
    cc[...] = mm(dao[...], wa[3].reshape(width, width), NT).astype(BF)
    load["t"].wait()
    for s in range(segs):
        dao[pl.ds(s * rows, seg_rows), :] = traw[s]
        dao[pl.ds(s * rows + seg_rows, rows - seg_rows), :] = jnp.zeros((rows - seg_rows, width), BF)
    xt[...] = dao[...].T
    for s in range(segs):
        for n in "qkv":
            load[n, s].wait()
    need("u")
    need("d")
    vbuf[0] = dvec_in[...]
    ticks = {}
    for i, slots in enumerate(SUM_SLOTS):
        for n, at in enumerate(slots):
            ticks.setdefault(at, []).append((F(i) if i < 2 * groups else A(i - 2 * groups), n))
    def tail(n):
        for w in ticks.get(n, ()):
            stage(*w)
    lane = lax.broadcasted_iota(jnp.int32, (rows, pair_w), 1)
    key_at = lax.broadcasted_iota(jnp.int32, (rows, 1), 0)
    zero = jnp.zeros((), BF)

    def body(it, carry):
        def tick(h):
            for n, what in ticks.items():
                if n % 2 == h and n < 8 * groups:
                    pl.when(it == n // 2)(functools.partial(lambda what: ([stage(*w) for w in what], None)[1], what))
        tick(0)
        g = it // 4
        s = (it // 2) % 2
        i = 2 * g + it % 2
        col = pl.ds(pl.multiple_of(i * pair_w, pair_w), pair_w)
        rr = pl.ds(pl.multiple_of(s * rows, 16), rows)
        live = len_ref[s] + MEM
        usable = (key_at < live) | ((key_at >= seg_rows - MEM) & (key_at < seg_rows))
        bias = jnp.where(usable, 0.0, -1e30).astype(F32)
        q2, k2, v2, g2 = q[rr, col], k[rr, col], v[rr, col], cc[rr, col]
        kt = k2.T
        dvp = jnp.zeros((rows, pair_w), F32)
        dkp = jnp.zeros((rows, pair_w), F32)
        dqt = []
        for h in range(2):
            if h == 1:
                tick(1)
            mine = (lane < HEAD_DIM) if h == 0 else (lane >= HEAD_DIM)
            qh = jnp.where(mine, q2, zero)
            gh = jnp.where(mine, g2, zero)
            p = jnp.exp((mm(k2, qh, NT) + bias) - lse_ref[s, pl.ds(2 * i + h, 1), :])
            dp = mm(v2, gh, NT)
            dvp = dvp + mm(p.astype(BF), gh)
            ds = (p * (dp - jnp.sum(p * dp, axis=0, keepdims=True))).astype(BF)
            dkp = dkp + mm(ds, qh)
            dqt.append(mm(kt[h * HEAD_DIM:(h + 1) * HEAD_DIM], ds))
        v[rr, col] = dvp.astype(BF)
        k[rr, col] = dkp.astype(BF)
        q[rr, col] = (jnp.concatenate(dqt, axis=0).T * (HEAD_DIM ** -0.5)).astype(BF)

        @pl.when(it % 4 == 3)
        def _():
            gcol = pl.ds(pl.multiple_of(g * 2 * pair_w, 2 * pair_w), 2 * pair_w)
            for m, ref in enumerate((q, k, v)):
                ga[m, :, :, :, :, gcol] = mm(xt[...], ref[:, gcol]).astype(BF).reshape(2, 2, 2, part, 2 * pair_w)
            for gg in range(groups):
                pl.when(g == gg)(functools.partial(lambda gg: (begin(A(gg)), None)[1], gg))
        return carry
    lax.fori_loop(0, 4 * groups, body, 0)

    def rest_of_rows(s):
        at = pl.ds(s * rows, rows)
        r = r1f[at, :]
        for m, ref in enumerate((q, k, v)):
            r = r + mm(ref[at, :], wa[m].reshape(width, width), NT)
        ig_o[s] = r[:seg_rows]
    vbuf[0, 0:1, :] = jnp.sum(q[...].astype(F32), axis=0, keepdims=True)
    vbuf[0, 1:2, :] = jnp.sum(v[...].astype(F32), axis=0, keepdims=True)
    legs.start("v0")
    tail(24)
    tail(25)
    legs.got("v0")
    vbuf[2] = vbuf[0] + vbuf[1]
    legs.start("v1")
    rest_of_rows(0)
    tail(26)
    tail(27)
    legs.got("v1")
    vbuf[4] = vbuf[2] + vbuf[3]
    legs.start("v2")
    rest_of_rows(1)
    tail(28)
    tail(29)
    legs.got("v2")
    vbuf[6 + z] = vbuf[4] + vbuf[5]
    legs.start(*[("v", i) for i in (1, 2, 3)])
    tail(30)
    legs.got(*[("v", i) for i in (1, 2, 3)])
    gv_ref[...] = ((vbuf[6] + vbuf[7]) + vbuf[8]) + vbuf[9]
    legs.sent()


def backward(lengths, tokens, w, q, k, v, c, dr1, dup, ddn, lse, dvec):
    segs, seg_rows, width = tokens.shape
    rows = q.shape[1]
    total = segs * rows
    part = w.shape[-2]
    sd = jax.ShapeDtypeStruct
    any_, vm = pl.BlockSpec(memory_space=pl.ANY), whole()
    V = lambda *s, t=BF: pltpu.VMEM(s, t)
    scratch = [V(*w.shape), V(*w.shape)] + [V(total, width)] * 4 + [V(total, width, t=F32), V(segs, seg_rows, width), V(width, total), V(total, width)]
    scratch += [V(2, 4, 2, part, width)] * 2 + [V(10, 16, width, t=F32)]
    bufs = [V(*s) for _, _, nc, order, route in sum_plan(width) for s in SumUnit.buffers(order, part, nc, route)]
    return pl.pallas_call(
        functools.partial(backward_kernel, seg_rows, len(bufs)),
        in_specs=[pl.BlockSpec(memory_space=pltpu.SMEM)] + [any_] * 9 + [vm, vm],
        out_specs=[vm] * 5,
        out_shape=[sd(tokens.shape, F32)] + [sd((part, width), F32)] * 3 + [sd((16, width), F32)],
        scratch_shapes=scratch + bufs + [DMA((N_BACK_LEGS,)), DMA((N_BACK_LEGS,)), DMA((15,))],
        compiler_params=pltpu.CompilerParams(collective_id=1, has_side_effects=True, vmem_limit_bytes=63 << 20),
        name="attention_backward_and_sums",
    )(lengths, tokens, w, q, k, v, c, dr1, dup, ddn, lse, dvec)

STEPS = 5
beta_first = 0.9
beta_second = 0.999
adam_epsilon = 1e-08
matrix_rate = 0.06
vector_rate = 0.2
weight_decay = 0.01
ORDERS = ("zxyc", "yczx", "yczx")


def adam(weight, moment_one, moment_two, gradient, step_rate, decay_rate):
    first_new = beta_first * moment_one + (1.0 - beta_first) * gradient
    second_new = beta_second * moment_two + (1.0 - beta_second) * gradient * gradient
    first_hat = first_new / (1.0 - beta_first**STEPS)
    second_hat = second_new / (1.0 - beta_second**STEPS)
    update = first_hat / (jnp.sqrt(second_hat) + adam_epsilon)
    return (weight - step_rate * (update + decay_rate * weight), first_new, second_new)


def shards(
    own_plan,
    tokens,
    segment_lengths,
    cotangent,
    attention_master,
    attention_mean,
    attention_square,
    up_master,
    up_mean,
    up_square,
    down_master,
    down_mean,
    down_square,
    vector_master,
    vector_mean,
    vector_square,
):
    width = tokens.shape[2]
    dp_count, tensor_count = lax.axis_size("dp"), lax.axis_size("tensor")
    part, columns = vector_master.shape
    spare = 16 - columns
    vec_low = vector_master.astype(BF).T
    if own_plan:
        piece = jnp.pad(vec_low, ((0, spare), (0, 128 - part)))
        block_output, q, k, v, c, w_all, dr1, d_up, d_down, lse, dvec_ffn = forward(
            segment_lengths, tokens, cotangent, attention_master, up_master, down_master, piece
        )
    else:
        low = [m.astype(BF) for m in (attention_master, up_master, down_master)]
        w_all = lax.all_gather(low[0], ("dp", "tensor"), axis=0, tiled=True)
        up_all, down_all = (lax.all_gather(m, ("tensor", "dp"), axis=0, tiled=True) for m in low[1:])
        rows = lax.all_gather(vec_low, "dp", axis=1, tiled=True).astype(F32)
        table = jnp.pad(rows, ((0, spare), (0, 0)))
        w_all = w_all.reshape(4, width, width)
        up_all = up_all.reshape(tensor_count, width, width)
        down_all = down_all.reshape(tensor_count, width, width)
        q, k, v, c, n1, inv, ab, lse = attn_fwd(segment_lengths, tokens, w_all, table)
        block_output, dr1, d_up, d_down, dvec_ffn = ffn(ab, n1, inv, cotangent, up_all, down_all, table)
    if own_plan:
        input_grad, s_attention, s_up, s_down, s_vec = backward(
            segment_lengths, tokens, w_all, q, k, v, c, dr1, d_up, d_down, lse, dvec_ffn
        )
        s_vec = lax.dynamic_slice_in_dim(s_vec, lax.axis_index("dp") * part, part, axis=1)
    else:
        input_grad, d_attention, dvec_att = attn_bwd(segment_lengths, tokens, w_all, q, k, v, c, lse, dr1)
        d_vec = dvec_ffn + dvec_att
        flat = lambda g: g.astype(F32).reshape(-1, width)
        s_attention = lax.psum_scatter(flat(d_attention), ("dp", "tensor"), scatter_dimension=0, tiled=True)
        s_up, s_down = (lax.psum_scatter(flat(g), ("tensor", "dp"), scatter_dimension=0, tiled=True) for g in (d_up, d_down))
        s_vec = lax.psum(lax.psum_scatter(d_vec, "dp", scatter_dimension=1, tiled=True), "tensor")
    s_vec = s_vec[:columns].T

    attention_new = adam(attention_master, attention_mean, attention_square, s_attention, matrix_rate, weight_decay)
    up_new = adam(up_master, up_mean, up_square, s_up, matrix_rate, weight_decay)
    down_new = adam(down_master, down_mean, down_square, s_down, matrix_rate, weight_decay)
    vector_new = adam(vector_master, vector_mean, vector_square, s_vec, vector_rate, 0.0)
    return (block_output, input_grad, *attention_new, *up_new, *down_new, *vector_new)


def solution(mesh):
    rows, cols = P(("dp", "tensor")), P("dp", "tensor")
    own_plan = mesh.shape["dp"] == 8 and mesh.shape["tensor"] == 4
    return jax.shard_map(
        functools.partial(shards, own_plan),
        mesh=mesh,
        in_specs=(rows,) * 6 + (cols,) * 6 + (P("dp"),) * 3,
        out_specs=(rows,) * 5 + (cols,) * 6 + (P("dp"),) * 3,
        check_vma=False,
    )
```

```python
import functools

import jax
import jax.numpy as jnp
from jax import lax
from jax.experimental import pallas as pl
from jax.experimental.pallas import tpu as pltpu
from jax.sharding import PartitionSpec as P


HEAD_DIM = 64
MEM = 10
norm_epsilon = 1e-12
inv_root_two = 0.7071067811865476
inv_root_tau = 0.3989422804014327
F32, BF = jnp.float32, jnp.bfloat16
NT = (((1,), (1,)), ((), ()))
TN = (((0,), (0,)), ((), ()))
NN = (((1,), (0,)), ((), ()))

def mm(a, b, dims=NN):
    return lax.dot_general(a, b, dims, preferred_element_type=F32)

def whole(shape=None):
    return pl.BlockSpec(memory_space=pltpu.VMEM)

def norm_stats(signal, width):
    centre = signal - jnp.sum(signal, axis=-1, keepdims=True) * (1.0 / width)
    inverse = lax.rsqrt(jnp.sum(centre * centre, axis=-1, keepdims=True) * (1.0 / width) + norm_epsilon)
    return centre * inverse, inverse

def norm_back(up, scaled, inverse, width):
    return inverse * (up - jnp.sum(up, axis=-1, keepdims=True) * (1.0 / width)
                      - scaled * (jnp.sum(up * scaled, axis=-1, keepdims=True) * (1.0 / width)))

def attn_fwd_kernel(seg_rows, len_ref, x_ref, w_ref, tab_ref, q_ref, k_ref, v_ref, c_ref, n_ref, inv_ref, ab_ref, lse_ref, xs, ct):
    rows, width = xs.shape
    heads = width // HEAD_DIM
    xs[pl.ds(0, seg_rows), :] = x_ref[0]
    xs[pl.ds(seg_rows, rows - seg_rows), :] = jnp.zeros((rows - seg_rows, width), BF)
    x = xs[...]
    q_ref[0] = ((mm(x, w_ref[0]) + tab_ref[0:1, :]).astype(BF) * BF(HEAD_DIM ** -0.5)).astype(BF)
    k_ref[0] = mm(x, w_ref[1]).astype(BF)
    v_ref[0] = (mm(x, w_ref[2]) + tab_ref[1:2, :]).astype(BF)
    live = len_ref[pl.program_id(0)] + MEM
    key_at = lax.broadcasted_iota(jnp.int32, (rows, 1), 0)
    usable = (key_at < live) | ((key_at >= seg_rows - MEM) & (key_at < seg_rows))
    bias = jnp.where(usable, 0.0, -1e30).astype(F32)
    lane = lax.broadcasted_iota(jnp.int32, (rows, 2 * HEAD_DIM), 1)
    zero = jnp.zeros((), BF)

    def pair(i, carry):
        at = pl.ds(pl.multiple_of(i * 2 * HEAD_DIM, 2 * HEAD_DIM), 2 * HEAD_DIM)
        q2, k2, v2 = q_ref[0, :, at], k_ref[0, :, at], v_ref[0, :, at]
        vt = v2.T
        for h in range(2):
            mine = (lane < HEAD_DIM) if h == 0 else (lane >= HEAD_DIM)
            qh = jnp.where(mine, q2, zero)
            s = mm(k2, qh, NT) + bias
            top = jnp.max(s, axis=0, keepdims=True)
            e = jnp.exp(s - top)
            tot = jnp.sum(e, axis=0, keepdims=True)
            p = (e * (1.0 / tot)).astype(BF)
            ct[pl.ds(pl.multiple_of(i * 2 * HEAD_DIM + h * HEAD_DIM, HEAD_DIM), HEAD_DIM), :] = mm(vt[h * HEAD_DIM:(h + 1) * HEAD_DIM], p)
            lse_ref[0, pl.ds(2 * i + h, 1), :] = top + jnp.log(tot)
        return carry
    lax.fori_loop(0, heads // 2, pair, 0)
    c = ct[...].T.astype(BF)
    c_ref[0] = c
    r = x.astype(F32) + mm(c, w_ref[3]) + tab_ref[2:3, :]
    n, inv = norm_stats(r, width)
    n_ref[0] = n
    inv_ref[0] = jnp.broadcast_to(inv, (rows, 128))
    ab_ref[0] = (n * tab_ref[3:4, :] + tab_ref[4:5, :]).astype(BF)

def attn_fwd(lengths, tokens, weights, table):
    segs, seg_rows, width = tokens.shape
    rows = -(-seg_rows // 16) * 16
    heads = width // HEAD_DIM
    hp = -(-heads // 8) * 8
    seg = lambda *s: pl.BlockSpec((1,) + s, lambda i, L: (i,) + (0,) * len(s))
    full = lambda *s: pl.BlockSpec(s, lambda i, L: (0,) * len(s), pipeline_mode=pl.Buffered(1))
    sd = jax.ShapeDtypeStruct
    return pl.pallas_call(
        functools.partial(attn_fwd_kernel, seg_rows),
        grid_spec=pltpu.PrefetchScalarGridSpec(
            num_scalar_prefetch=1, grid=(segs,),
            in_specs=[seg(seg_rows, width), full(*weights.shape), full(*table.shape)],
            out_specs=[seg(rows, width)] * 5 + [seg(rows, 128), seg(rows, width), seg(hp, rows)],
            scratch_shapes=[pltpu.VMEM((rows, width), BF), pltpu.VMEM((width, rows), F32)]),
        out_shape=[sd((segs, rows, width), BF)] * 4 + [sd((segs, rows, width), F32), sd((segs, rows, 128), F32), sd((segs, rows, width), BF), sd((segs, hp, rows), F32)],
        compiler_params=pltpu.CompilerParams(vmem_limit_bytes=56 << 20),
        name="attention_forward",
    )(lengths, tokens, weights, table)

def ffn_kernel(seg_rows, block, ab_ref, n1_ref, inv_ref, cot_ref, up_ref, down_ref, tab_ref,
               out_ref, dr1_ref, dup_ref, ddown_ref, dvec_ref, hid, slope, dy, du):
    segs, rows, width = n1_ref.shape
    total = segs * rows
    chunks = up_ref.shape[0]
    per = rows // block
    nb = total // block
    def rb(i):
        return pl.ds(pl.multiple_of(i * block, block), block)
    y = dr1_ref
    def fwd(i, carry):
        a = ab_ref[rb(i), :]
        acc = jnp.zeros((block, width), F32)
        for j in range(chunks):
            u = mm(a, up_ref[j]) + tab_ref[8 + j:9 + j, :]
            phi = 0.5 * (1.0 + lax.erf(u * inv_root_two))
            h = (u * phi).astype(BF)
            hid[j, rb(i), :] = h
            slope[j, rb(i), :] = phi + u * jnp.exp(-0.5 * u * u) * inv_root_tau
            acc = acc + mm(h, down_ref[j], NT)
        y[rb(i), :] = acc
        return carry
    lax.fori_loop(0, nb, fwd, 0)
    dvec_ref[...] = jnp.zeros_like(dvec_ref)
    for s in range(segs):
        at = pl.ds(s * rows, rows)
        n1 = n1_ref[s]
        r2 = n1 * tab_ref[3:4, :] + tab_ref[4:5, :] + (y[at, :] + tab_ref[7:8, :])
        n2, inv2 = norm_stats(r2, width)
        out_ref[s] = (n2 * tab_ref[5:6, :] + tab_ref[6:7, :])[:seg_rows].astype(BF)
        live = lax.broadcasted_iota(jnp.int32, (rows, 1), 0) < seg_rows
        e = jnp.concatenate([cot_ref[s].astype(F32), jnp.zeros((rows - seg_rows, width), F32)], axis=0)
        dvec_ref[5:6, :] += jnp.sum(e * n2, axis=0, keepdims=True)
        dvec_ref[6:7, :] += jnp.sum(e, axis=0, keepdims=True)
        dr2 = norm_back(e * tab_ref[5:6, :], n2, inv2, width)
        d16 = dr2.astype(BF)
        y[at, :] = dr2
        dy[at, :] = d16
        dvec_ref[7:8, :] += jnp.sum(d16.astype(F32), axis=0, keepdims=True)
    dyt = dy[...].T
    abt = ab_ref[...].T
    for j in range(chunks):
        def back(i, carry):
            g = dy[rb(i), :]
            d = (mm(g, down_ref[j]) * slope[j, rb(i), :]).astype(BF)
            du[rb(i), :] = d
            return carry + jnp.sum(d.astype(F32), axis=0, keepdims=True)
        dvec_ref[8 + j:9 + j, :] = lax.fori_loop(0, nb, back, jnp.zeros((1, width), F32))
        ddown_ref[j] = mm(dyt, hid[j]).astype(BF)
        dup_ref[j] = mm(abt, du[...]).astype(BF)
        def inner(i, carry):
            part = mm(du[rb(i), :], up_ref[j], NT)
            slope[0, rb(i), :] = part if j == 0 else slope[0, rb(i), :] + part
            return carry
        lax.fori_loop(0, nb, inner, 0)
    for s in range(segs):
        at = pl.ds(s * rows, rows)
        da = y[at, :] + slope[0, at, :].astype(BF).astype(F32)
        n1 = n1_ref[s]
        dvec_ref[3:4, :] += jnp.sum(da * n1, axis=0, keepdims=True)
        dvec_ref[4:5, :] += jnp.sum(da, axis=0, keepdims=True)
        dr1 = norm_back(da * tab_ref[3:4, :], n1, inv_ref[s][:, 0:1], width)
        dr1_ref[at, :] = dr1
        dvec_ref[2:3, :] += jnp.sum(dr1.astype(BF).astype(F32), axis=0, keepdims=True)

def ffn(ab, n1, inv, cot, up, down, table):
    segs, rows, width = n1.shape
    seg_rows = cot.shape[1]
    total = segs * rows
    chunks = up.shape[0]
    sd = jax.ShapeDtypeStruct
    return pl.pallas_call(
        functools.partial(ffn_kernel, seg_rows, rows // 2),
        in_specs=[whole()] * 7, out_specs=[whole()] * 5,
        out_shape=[sd(cot.shape, BF), sd((total, width), F32), sd(up.shape, BF), sd(down.shape, BF), sd((16, width), F32)],
        scratch_shapes=[pltpu.VMEM((chunks, total, width), BF), pltpu.VMEM((chunks, total, width), F32), pltpu.VMEM((total, width), BF), pltpu.VMEM((total, width), BF)],
        compiler_params=pltpu.CompilerParams(vmem_limit_bytes=63 << 20),
        name="feed_forward",
    )(ab.reshape(total, width), n1, inv, cot, up, down, table)

def attn_bwd_kernel(seg_rows, len_ref, x_ref, w_ref, q_ref, k_ref, v_ref, c_ref, lse_ref, dr1_ref,
                    ig_ref, dw_ref, dvec_ref, dao, dc, dq, dk, dv, xs):
    segs, rows, width = q_ref.shape
    total = segs * rows
    heads = width // HEAD_DIM
    for s in range(segs):
        xs[pl.ds(s * rows, seg_rows), :] = x_ref[s]
        xs[pl.ds(s * rows + seg_rows, rows - seg_rows), :] = jnp.zeros((rows - seg_rows, width), BF)
    dao[...] = dr1_ref[...].astype(BF)
    dw_ref[3] = mm(c_ref[...].reshape(total, width).T, dao[...]).astype(BF)
    dc[...] = mm(dao[...], w_ref[3], NT).astype(BF)
    key_at = lax.broadcasted_iota(jnp.int32, (rows, 1), 0)
    lane = lax.broadcasted_iota(jnp.int32, (rows, 2 * HEAD_DIM), 1)
    zero = jnp.zeros((), BF)
    for s in range(segs):
        live = len_ref[s] + MEM
        usable = (key_at < live) | ((key_at >= seg_rows - MEM) & (key_at < seg_rows))
        bias = jnp.where(usable, 0.0, -1e30).astype(F32)
        at_rows = pl.ds(s * rows, rows)
        def pair(i, carry):
            at = pl.ds(pl.multiple_of(i * 2 * HEAD_DIM, 2 * HEAD_DIM), 2 * HEAD_DIM)
            q2, k2, v2 = q_ref[s, :, at], k_ref[s, :, at], v_ref[s, :, at]
            g2 = dc[at_rows, at]
            kt = k2.T
            dvp = jnp.zeros((rows, 2 * HEAD_DIM), F32)
            dkp = jnp.zeros((rows, 2 * HEAD_DIM), F32)
            dqt = []
            for h in range(2):
                mine = (lane < HEAD_DIM) if h == 0 else (lane >= HEAD_DIM)
                qh = jnp.where(mine, q2, zero)
                gh = jnp.where(mine, g2, zero)
                p = jnp.exp((mm(k2, qh, NT) + bias) - lse_ref[s, pl.ds(2 * i + h, 1), :])
                dp = mm(v2, gh, NT)
                dvp = dvp + mm(p.astype(BF), gh)
                ds = (p * (dp - jnp.sum(p * dp, axis=0, keepdims=True))).astype(BF)
                dkp = dkp + mm(ds, qh)
                dqt.append(mm(kt[h * HEAD_DIM:(h + 1) * HEAD_DIM], ds))
            dv[at_rows, at] = dvp.astype(BF)
            dk[at_rows, at] = dkp.astype(BF)
            dq[at_rows, at] = (jnp.concatenate(dqt, axis=0).T * (HEAD_DIM ** -0.5)).astype(BF)
            return carry
        lax.fori_loop(0, heads // 2, pair, 0)
    xt = xs[...].T
    dvec_ref[...] = jnp.zeros_like(dvec_ref)
    for j, g in enumerate((dq, dk, dv)):
        dw_ref[j] = mm(xt, g[...]).astype(BF)
    dvec_ref[0:1, :] = jnp.sum(dq[...].astype(F32), axis=0, keepdims=True)
    dvec_ref[1:2, :] = jnp.sum(dv[...].astype(F32), axis=0, keepdims=True)
    for s in range(segs):
        at = pl.ds(s * rows, rows)
        r = dr1_ref[at, :] + mm(dq[at, :], w_ref[0], NT) + mm(dk[at, :], w_ref[1], NT) + mm(dv[at, :], w_ref[2], NT)
        ig_ref[s] = r[:seg_rows]

def attn_bwd(lengths, tokens, weights, q, k, v, c, lse, dr1):
    segs, seg_rows, width = tokens.shape
    rows = q.shape[1]
    total = segs * rows
    sd = jax.ShapeDtypeStruct
    return pl.pallas_call(
        functools.partial(attn_bwd_kernel, seg_rows),
        in_specs=[pl.BlockSpec(memory_space=pltpu.SMEM)] + [whole()] * 8, out_specs=[whole()] * 3,
        out_shape=[sd(tokens.shape, F32), sd(weights.shape, BF), sd((16, width), F32)],
        scratch_shapes=[pltpu.VMEM((total, width), BF)] * 6,
        compiler_params=pltpu.CompilerParams(vmem_limit_bytes=63 << 20),
        name="attention_backward",
    )(lengths, tokens, weights, q, k, v, c, lse, dr1)

MESH = pl.DeviceIdType.MESH
DMA = pltpu.SemaphoreType.DMA
SHAPE = {"z": 4, "x": 2, "y": 2, "c": 2}
ATT, FFN = "zxyc", "yczx"
ROUTES = ("zxy", "zyx", "xzy", "zyx", "zxy", "yzx")


def place():
    d, t = lax.axis_index("dp"), lax.axis_index("tensor")
    return d // 2, d % 2, t // 2, t % 2


def dev(z, x, y, c):
    return {"dp": z * 2 + x, "tensor": y * 2 + c}


def partners(z, x, y, c):
    return {"x": (z, 1 - x, y, c), "y": (z, x, 1 - y, c), "c": (z, x, y, 1 - c), **{i: ((z + i) % 4, x, y, c) for i in (1, 2, 3)}}


def greet(*here):
    b = pltpu.get_barrier_semaphore()
    for p in partners(*here).values():
        pl.semaphore_signal(b, inc=1, device_id=dev(*p), device_id_type=MESH)
    pl.semaphore_wait(b, 6)


class Legs:
    def __init__(self, here, ssem, rsem):
        self.here, self.peer = dict(zip("zxyc", here)), partners(*here)
        self.ssem, self.rsem, self.make = ssem, rsem, {}

    def add(self, key, src, dst, peer):
        i = len(self.make)
        self.make[key] = lambda: pltpu.make_async_remote_copy(
            src(), dst(), self.ssem.at[i], self.rsem.at[i], device_id=dev(*self.peer[peer]), device_id_type=MESH)

    def start(self, *keys):
        for k in keys:
            self.make[k]().start()

    def got(self, *keys):
        for k in keys:
            self.make[k]().wait_recv()

    def sent(self):
        for m in self.make.values():
            m().wait_send()


def view_of(ref, order, cols):
    return lambda at, rows: ref.at[tuple(at.get(ch, slice(None)) for ch in order) + (rows, cols)]


class GatherUnit:
    def __init__(self, legs, key, view, r0, nr, route):
        self.legs, self.key, self.steps = legs, key, [([], [])]
        me = legs.here
        c = {"c": me["c"]}
        full = pl.ds(r0, nr)

        def leg(name, peer, at):
            f = functools.partial(view, at, full)
            legs.add((key, name), f, f, peer)
            self.steps[-1][1].append((key, name))

        for n, d in enumerate(route + "c"):
            fixed = {**c, **{e: me[e] for e in route[n:]}}
            names = [(d, i) for i in (1, 2, 3)] if d == "z" else [(d, d)]
            for name in names:
                leg(name, name[1], fixed)
            self.steps.append(([(key, name) for name in names], []))

    def go(self, n):
        self.legs.got(*self.steps[n][0])
        self.legs.start(*self.steps[n][1])


class SumUnit:
    @staticmethod
    def buffers(order, nr, nc, route):
        inner = order.replace("c", "")
        out, gone = [], ""
        for d in "c" + route:
            gone += d
            out += [tuple(SHAPE[ch] for ch in inner if ch not in gone) + (nr, nc)] * (3 if d == "z" else 1)
        return out

    def __init__(self, legs, key, given, own, bufs, r0, nr, order, route, finish, ready=None):
        self.legs, self.key, self.own, self.finish, self.ready = legs, key, own, finish, ready
        self.inner = order.replace("c", "")
        self.rows = pl.ds(r0, nr)
        me, bufs, done = legs.here, list(bufs), {"c": legs.here["c"]}
        self.work = []
        for d in "c" + route:
            names = [(d, i) for i in (1, 2, 3)] if d == "z" else [(d, d)]
            got = []
            for name in names:
                to = (me["z"] + name[1]) % 4 if d == "z" else 1 - me[d]
                b = bufs.pop(0)
                got.append(b)
                legs.add((key, name), functools.partial(given if d == "c" else own, {**done, d: to}, self.rows), functools.partial(lambda b: b, b), name[1])
            done = {**done, d: me[d]}
            self.work.append(([(key, name) for name in names], dict(done), got))

    def begin(self):
        self.legs.start(*self.work[0][0])

    def go(self, n):
        names, at, bufs = self.work[n]
        self.legs.got(*names)
        if n == 0 and self.ready is not None:
            self.ready()
        free = [ch for ch in self.inner if ch not in at]

        def total(ref, cut):
            t = ref[...].astype(jnp.float32)
            for b in bufs:
                t = t + cut(b).astype(jnp.float32)
            return t
        if n == len(self.work) - 1:
            self.finish(self.rows, total(self.own(at, self.rows), lambda b: b[...]))
            return
        ch = free[0]

        def body(i, carry):
            ref = self.own({**at, ch: i}, self.rows)
            ref[...] = total(ref, lambda b: b[i]).astype(jnp.bfloat16)
            return carry
        lax.fori_loop(0, SHAPE[ch], body, 0)
        self.legs.start(*self.work[n + 1][0])


N_FORWARD_LEGS = 18 * 6 + 4
GATHER_FIRST = (((0, 0), (1, 0)), ((0, 1), (2, 0)), ((0, 2), (1, 1), (3, 0), (4, 0)), ((0, 3), (2, 1), (1, 2), (5, 0)))
GATHER_SLOTS = {
    0: ((2, 2), (3, 1), (4, 1), (5, 1)),
    4: ((1, 3), (6, 0), (7, 0), (8, 0)),
    6: ((2, 3), (3, 2), (4, 2), (5, 2)),
    8: ((1, 4),),
    14: ((6, 1), (7, 1), (8, 1)),
    16: ((2, 4), (3, 3), (4, 3), (5, 3)),
    18: ((6, 2), (7, 2), (8, 2)),
    28: ((6, 3), (7, 3), (8, 3)),
}


def forward_kernel(seg_rows, len_ref, tok, cot, am, um, dm, vp,
                   out_o, q_o, k_o, v_o, c_o, x_o, w_o, dr1_o, dup_o, ddn_o, lse_ref, dvec_ref,
                   wa, wu, wd, vec, tab, traw, craw, xs, cs, q, k, v, ct, cc, n1, inv, ab, hid, slo, dy, dyt, abt,
                   ssem, rsem, lsem):
    segs, rows, width = q_o.shape
    total = segs * rows
    heads = width // HEAD_DIM
    part = am.shape[0]
    z, x, y, c = here = place()
    lt = pltpu.make_async_copy(tok, traw, lsem.at[0]); lt.start()
    lc = pltpu.make_async_copy(cot, craw, lsem.at[1]); lc.start()
    wa[z, x, y, c] = am[...].astype(BF)
    wu[y, c, z, x] = um[...].astype(BF)
    wd[y, c, z, x] = dm[...].astype(BF)
    vec[z, x] = vp[...]

    legs = Legs(here, ssem, rsem)
    pair_w = 2 * HEAD_DIM
    groups = width // (2 * pair_w)
    units = []
    for name, ref, order in (("a", wa, ATT), ("u", wu, FFN), ("d", wd, FFN)):
        for h in range(2 * groups):
            units.append(GatherUnit(legs, (name, h), view_of(ref, order, pl.ds(h * pair_w, pair_w)), 0, part, ROUTES[h]))
    here_vec = lambda: vec.at[z, x]
    for i in (1, 2, 3):
        legs.add(("v", i), here_vec, here_vec, i)
    legs.add("vx", lambda: vec.at[:, x], lambda: vec.at[:, x], "x")

    def advance(what):
        for i, n in what:
            for unit in units[2 * i:2 * i + 2]:
                unit.go(n)

    greet(*here)
    advance(GATHER_FIRST[0])
    legs.start(*[("v", i) for i in (1, 2, 3)])
    lt.wait()

    def pad_rows(to, raw, s):
        to[pl.ds(s * rows, seg_rows), :] = raw[:, s, :]
        to[pl.ds(s * rows + seg_rows, rows - seg_rows), :] = jnp.zeros((rows - seg_rows, width), BF)

    pad_rows(xs, traw, 0)
    advance(GATHER_FIRST[1])
    for s in range(1, segs):
        pad_rows(xs, traw, s)
    legs.got(*[("v", i) for i in (1, 2, 3)])
    legs.start("vx")
    advance(GATHER_FIRST[2])
    lc.wait()
    for s in range(segs):
        pad_rows(cs, craw, s)
    advance(GATHER_FIRST[3])
    legs.got("vx")
    lane_in = lax.broadcasted_iota(jnp.int32, (128, width), 0)
    lane_out = lax.broadcasted_iota(jnp.int32, (128, width), 1)
    acc = jnp.zeros((16, width), F32)
    for d in range(8):
        move = ((lane_out == lane_in + d * part) & (lane_in < part)).astype(BF)
        acc = acc + mm(vec[d // 2, d % 2], move)
    tab[...] = acc
    advance(((0, 4),))
    lane = lax.broadcasted_iota(jnp.int32, (rows, pair_w), 1)
    key_at = lax.broadcasted_iota(jnp.int32, (rows, 1), 0)
    zero = jnp.zeros((), BF)

    def body(it, carry):
        for n in range(0, 8 * groups, 2):
            if n in GATHER_SLOTS:
                pl.when(2 * it == n)(functools.partial(lambda n: advance(GATHER_SLOTS[n]), n))
        g = it // 4

        @pl.when(it % 4 == 0)
        def _():
            col = pl.ds(pl.multiple_of(g * 2 * pair_w, 2 * pair_w), 2 * pair_w)
            w3 = [wa[m, :, :, :, :, col].reshape(width, 2 * pair_w) for m in range(3)]
            xx = xs[...]
            q[:, col] = ((mm(xx, w3[0]) + tab[0:1, col]).astype(BF) * BF(HEAD_DIM ** -0.5)).astype(BF)
            k[:, col] = mm(xx, w3[1]).astype(BF)
            v[:, col] = (mm(xx, w3[2]) + tab[1:2, col]).astype(BF)

        s = (it // 2) % 2
        i = 2 * g + it % 2
        col = pl.ds(pl.multiple_of(i * pair_w, pair_w), pair_w)
        rr = pl.ds(pl.multiple_of(s * rows, 16), rows)
        live = len_ref[s] + MEM
        usable = (key_at < live) | ((key_at >= seg_rows - MEM) & (key_at < seg_rows))
        bias = jnp.where(usable, 0.0, -1e30).astype(F32)
        q2, k2, v2 = q[rr, col], k[rr, col], v[rr, col]
        vt = v2.T
        for h in range(2):
            mine = (lane < HEAD_DIM) if h == 0 else (lane >= HEAD_DIM)
            if h == 1:
                for n in range(1, 8 * groups, 2):
                    if n in GATHER_SLOTS:
                        pl.when(2 * it + 1 == n)(functools.partial(lambda n: advance(GATHER_SLOTS[n]), n))
            sc = mm(k2, jnp.where(mine, q2, zero), NT) + bias
            top = jnp.max(sc, axis=0, keepdims=True)
            e = jnp.exp(sc - top)
            tot = jnp.sum(e, axis=0, keepdims=True)
            p = (e * (1.0 / tot)).astype(BF)
            at = pl.ds(pl.multiple_of(i * pair_w + h * HEAD_DIM, HEAD_DIM), HEAD_DIM)
            ct[s, at, :] = mm(vt[h * HEAD_DIM:(h + 1) * HEAD_DIM], p).astype(BF)
            lse_ref[s, pl.ds(2 * i + h, 1), :] = top + jnp.log(tot)
        return carry
    lax.fori_loop(0, 4 * groups, body, 0)

    spill = [pltpu.make_async_copy(a.at[pl.ds(s * rows, rows)], o.at[s], lsem.at[2 + 2 * n + s]) for n, (a, o) in enumerate(((q, q_o), (k, k_o), (v, v_o))) for s in range(segs)]
    for cp in spill:
        cp.start()
    wcopy = pltpu.make_async_copy(wa, w_o, lsem.at[8]); wcopy.start()
    xcopy = pltpu.make_async_copy(xs, x_o, lsem.at[15]); xcopy.start()
    for s in range(segs):
        rr = pl.ds(s * rows, rows)
        cs_ = ct[s].T
        cc[rr, :] = cs_
        r = xs[rr, :].astype(F32) + mm(cs_, wa[3].reshape(width, width)) + tab[2:3, :]
        n, iv = norm_stats(r, width)
        n1[rr, :] = n
        inv[rr, :] = jnp.broadcast_to(iv, (rows, 128))
        ab[rr, :] = (n * tab[3:4, :] + tab[4:5, :]).astype(BF)
    ccopy = [pltpu.make_async_copy(cc.at[pl.ds(s * rows, rows)], c_o.at[s], lsem.at[9 + s]) for s in range(segs)]
    for cp in ccopy:
        cp.start()

    block = rows // 2
    nb = total // block
    chunks = 4
    def rb(i):
        return pl.ds(pl.multiple_of(i * block, 16), block)
    def up(j):
        return wu[j // 2, j % 2].reshape(width, width)
    def down(j):
        return wd[j // 2, j % 2].reshape(width, width)
    advance(((3, 4), (4, 4), (5, 4)))

    def fwd(i, carry):
        a = ab[rb(i), :]
        for j in range(chunks):
            for n in range(nb):
                if 8 * groups + 4 * n + j in GATHER_SLOTS:
                    pl.when(i == n)(functools.partial(lambda n: advance(GATHER_SLOTS[n]), 8 * groups + 4 * n + j))
            u = mm(a, up(j)) + tab[8 + j:9 + j, :]
            phi = 0.5 * (1.0 + lax.erf(u * inv_root_two))
            hid[j, rb(i), :] = (u * phi).astype(BF)
            slo[j, rb(i), :] = (phi + u * jnp.exp(-0.5 * u * u) * inv_root_tau).astype(BF)
        return carry
    lax.fori_loop(0, nb, fwd, 0)
    abt[...] = ab[...].T
    advance(((6, 4), (7, 4), (8, 4)))
    dvec_ref[...] = jnp.zeros_like(dvec_ref)
    def mid(i, carry):
        yy = tab[7:8, :]
        for j in range(chunks):
            yy = yy + mm(hid[j, rb(i), :], down(j), NT)
        nn = n1[rb(i), :]
        r2 = nn * tab[3:4, :] + tab[4:5, :] + yy
        n2, inv2 = norm_stats(r2, width)
        e = cs[rb(i), :].astype(F32)
        cs[rb(i), :] = (n2 * tab[5:6, :] + tab[6:7, :]).astype(BF)
        dvec_ref[5:6, :] += jnp.sum(e * n2, axis=0, keepdims=True)
        dvec_ref[6:7, :] += jnp.sum(e, axis=0, keepdims=True)
        dr2 = norm_back(e * tab[5:6, :], n2, inv2, width)
        g16 = dr2.astype(BF)
        dy[rb(i), :] = g16
        dvec_ref[7:8, :] += jnp.sum(g16.astype(F32), axis=0, keepdims=True)
        da = jnp.zeros((block, width), F32)
        for j in range(chunks):
            d16 = (mm(g16, down(j)) * slo[j, rb(i), :].astype(F32)).astype(BF)
            slo[j, rb(i), :] = d16
            dvec_ref[8 + j:9 + j, :] += jnp.sum(d16.astype(F32), axis=0, keepdims=True)
            da = da + mm(d16, up(j), NT)
        da = dr2 + da.astype(BF).astype(F32)
        dvec_ref[3:4, :] += jnp.sum(da * nn, axis=0, keepdims=True)
        dvec_ref[4:5, :] += jnp.sum(da, axis=0, keepdims=True)
        dr1 = norm_back(da * tab[3:4, :], nn, inv[rb(i), 0:1], width)
        n1[rb(i), :] = dr1
        dvec_ref[2:3, :] += jnp.sum(dr1.astype(BF).astype(F32), axis=0, keepdims=True)
        return carry
    lax.fori_loop(0, nb, mid, 0)
    dcopy = pltpu.make_async_copy(n1, dr1_o, lsem.at[0]); dcopy.start()
    for s in range(segs):
        craw[:, s, :] = cs[pl.ds(s * rows, seg_rows), :]
    ocopy = pltpu.make_async_copy(craw, out_o, lsem.at[1]); ocopy.start()
    dyt[...] = dy[...].T
    legs.sent()
    def grad_copies(j):
        return (pltpu.make_async_copy(wd.at[j // 2, j % 2], ddn_o.at[j // 2, j % 2], lsem.at[11 + 2 * (j % 2)]),
                pltpu.make_async_copy(wu.at[j // 2, j % 2], dup_o.at[j // 2, j % 2], lsem.at[12 + 2 * (j % 2)]))
    def grads(j, carry):
        shape = wd.shape[2:]
        @pl.when(j >= 2)
        def _():
            for cp in grad_copies(j - 2):
                cp.wait()
        wd[j // 2, j % 2] = mm(dyt[...], hid[j]).astype(BF).reshape(shape)
        wu[j // 2, j % 2] = mm(abt[...], slo[j]).astype(BF).reshape(shape)
        for cp in grad_copies(j):
            cp.start()
        return carry
    lax.fori_loop(0, chunks, grads, 0)
    for j in (2, 3):
        for cp in grad_copies(j):
            cp.wait()
    for cp in spill + [wcopy, xcopy, dcopy, ocopy] + ccopy:
        cp.wait()

def forward(lengths, tokens, cotangent, att, up, down, piece):
    seg_rows, segs, width = tokens.shape
    part = att.shape[0]
    rows = -(-seg_rows // 16) * 16
    total = segs * rows
    hp = -(-(width // HEAD_DIM) // 8) * 8
    sd = jax.ShapeDtypeStruct
    any_, vm = pl.BlockSpec(memory_space=pl.ANY), whole()
    wshape, fshape = (4, 2, 2, 2, part, width), (2, 2, 4, 2, part, width)
    V = lambda *s, t=BF: pltpu.VMEM(s, t)
    return pl.pallas_call(
        functools.partial(forward_kernel, seg_rows),
        in_specs=[pl.BlockSpec(memory_space=pltpu.SMEM), any_, any_, vm, vm, vm, vm],
        out_specs=[any_] * 10 + [vm, vm],
        out_shape=[sd(cotangent.shape, BF)] + [sd((segs, rows, width), BF)] * 4 + [sd((total, width), BF), sd(wshape, BF), sd((total, width), F32), sd(fshape, BF), sd(fshape, BF), sd((segs, hp, rows), F32), sd((16, width), F32)],
        scratch_shapes=[V(*wshape), V(*fshape), V(*fshape), V(4, 2, 16, 128), V(16, width, t=F32), V(seg_rows, segs, width), V(seg_rows, segs, width),
                        V(total, width), V(total, width), V(total, width), V(total, width), V(total, width), V(segs, width, rows), V(total, width),
                        V(total, width, t=F32), V(total, 128, t=F32), V(total, width), V(4, total, width), V(4, total, width), V(total, width), V(width, total), V(width, total),
                        DMA((N_FORWARD_LEGS,)), DMA((N_FORWARD_LEGS,)), DMA((16,))],
        compiler_params=pltpu.CompilerParams(collective_id=0, has_side_effects=True, vmem_limit_bytes=63 << 20),
        name="forward_and_feed_forward_backward",
    )(lengths, tokens, cotangent, att, up, down, piece)

N_BACK_LEGS = 18 * 6 + 6
SUM_SLOTS = ((0, 4, 8, 12),) * 3 + ((4, 10, 16, 22),) * 3 + ((10, 16, 22, 24), (18, 22, 25, 27), (24, 26, 28, 30))


def sum_plan(width):
    pw = 2 * HEAD_DIM
    return [((name, h), h * pw, pw, order, ROUTES[h][::-1]) for name, order in (("u", FFN), ("d", FFN), ("a", ATT)) for h in range(width // pw)]


def backward_kernel(seg_rows, n_bufs, len_ref, x_i, w_i, q_i, k_i, v_i, c_i, dr1_i, dup, ddn, lse_ref, dvec_in,
                    ig_o, ga_ref, gu_ref, gd_ref, gv_ref,
                    wa, ga, q, k, v, cc, r1f, xs, xt, dao, own_u, own_d, vbuf, *rest):
    bufs, (ssem, rsem, lsem) = list(rest[:n_bufs]), rest[n_bufs:]
    segs, rows, width = q_i.shape
    total = segs * rows
    heads = width // HEAD_DIM
    pair_w = 2 * HEAD_DIM
    groups = width // (2 * pair_w)
    part = ga_ref.shape[0]
    z, x, y, c = here = place()
    legs = Legs(here, ssem, rsem)

    load = {}
    def local(name, src, dst, i):
        load[name] = pltpu.make_async_copy(src, dst, lsem.at[i])
        load[name].start()
    local("dr1", dr1_i, r1f, 0)
    local("w", w_i, wa, 1)
    for s in range(segs):
        rr = pl.ds(s * rows, rows)
        local(("c", s), c_i.at[s], cc.at[rr], 2 + s)
        local(("v", s), v_i.at[s], v.at[rr], 4 + s)
        local(("k", s), k_i.at[s], k.at[rr], 6 + s)
        local(("q", s), q_i.at[s], q.at[rr], 8 + s)
    local("t", x_i, xs, 10)

    local("u", dup.at[:, c], own_u, 11)
    local("d", ddn.at[:, c], own_d, 12)
    loaded = set()
    def need(name):
        if name not in loaded:
            loaded.add(name)
            load[name].wait()

    units = {}
    for key, c0, nc, order, route in sum_plan(width):
        mine = bufs[:6]
        del bufs[:6]
        col = pl.ds(c0, nc)
        if key[0] == "a":
            given = own = view_of(ga, ATT, col)
            out, ready = ga_ref, None
        else:
            given = view_of(dup if key[0] == "u" else ddn, FFN, col)
            own = view_of(own_u if key[0] == "u" else own_d, "yzx", col)
            out, ready = (gu_ref, gd_ref)[key[0] == "d"], functools.partial(need, key[0])
        def finish(rr, total, out=out, col=col):
            out[rr, col] = total
        units[key] = SumUnit(legs, key, given, own, mine, 0, part, order, route, finish, ready)
    F = lambda i: [("ud"[i // groups], 2 * (i % groups) + h) for h in range(2)]
    A = lambda g: [("a", 2 * g), ("a", 2 * g + 1)]
    def begin(keys):
        for key in keys:
            units[key].begin()
    def stage(keys, n):
        for key in keys:
            units[key].go(n)

    legs.add("v0", lambda: vbuf.at[0], lambda: vbuf.at[1], "c")
    legs.add("v1", lambda: vbuf.at[2], lambda: vbuf.at[3], "y")
    legs.add("v2", lambda: vbuf.at[4], lambda: vbuf.at[5], "x")
    for i in (1, 2, 3):
        legs.add(("v", i), lambda: vbuf.at[6 + z], lambda: vbuf.at[6 + z], i)

    greet(*here)
    for i in range(2 * groups):
        begin(F(i))
    load["dr1"].wait()
    dao[...] = r1f[...].astype(BF)
    for s in range(segs):
        load["c", s].wait()
    load["w"].wait()
    ga[3] = mm(cc[...].T, dao[...]).astype(BF).reshape(ga.shape[1:])
    cc[...] = mm(dao[...], wa[3].reshape(width, width), NT).astype(BF)
    load["t"].wait()
    xt[...] = xs[...].T
    for s in range(segs):
        for n in "qkv":
            load[n, s].wait()
    need("u")
    need("d")
    vbuf[0] = dvec_in[...]
    ticks = {}
    for i, slots in enumerate(SUM_SLOTS):
        for n, at in enumerate(slots):
            ticks.setdefault(at, []).append((F(i) if i < 2 * groups else A(i - 2 * groups), n))
    def tail(n):
        for w in ticks.get(n, ()):
            stage(*w)
    lane = lax.broadcasted_iota(jnp.int32, (rows, pair_w), 1)
    key_at = lax.broadcasted_iota(jnp.int32, (rows, 1), 0)
    zero = jnp.zeros((), BF)

    def body(it, carry):
        def tick(h):
            for n, what in ticks.items():
                if n % 2 == h and n < 8 * groups:
                    pl.when(it == n // 2)(functools.partial(lambda what: ([stage(*w) for w in what], None)[1], what))
        tick(0)
        g = it // 4
        s = (it // 2) % 2
        i = 2 * g + it % 2
        col = pl.ds(pl.multiple_of(i * pair_w, pair_w), pair_w)
        rr = pl.ds(pl.multiple_of(s * rows, 16), rows)
        live = len_ref[s] + MEM
        usable = (key_at < live) | ((key_at >= seg_rows - MEM) & (key_at < seg_rows))
        bias = jnp.where(usable, 0.0, -1e30).astype(F32)
        q2, k2, v2, g2 = q[rr, col], k[rr, col], v[rr, col], cc[rr, col]
        kt = k2.T
        dvp = jnp.zeros((rows, pair_w), F32)
        dkp = jnp.zeros((rows, pair_w), F32)
        dqt = []
        for h in range(2):
            if h == 1:
                tick(1)
            mine = (lane < HEAD_DIM) if h == 0 else (lane >= HEAD_DIM)
            qh = jnp.where(mine, q2, zero)
            gh = jnp.where(mine, g2, zero)
            p = jnp.exp((mm(k2, qh, NT) + bias) - lse_ref[s, pl.ds(2 * i + h, 1), :])
            dp = mm(v2, gh, NT)
            dvp = dvp + mm(p.astype(BF), gh)
            ds = (p * (dp - jnp.sum(p * dp, axis=0, keepdims=True))).astype(BF)
            dkp = dkp + mm(ds, qh)
            dqt.append(mm(kt[h * HEAD_DIM:(h + 1) * HEAD_DIM], ds))
        v[rr, col] = dvp.astype(BF)
        k[rr, col] = dkp.astype(BF)
        q[rr, col] = (jnp.concatenate(dqt, axis=0).T * (HEAD_DIM ** -0.5)).astype(BF)

        @pl.when(it % 4 == 3)
        def _():
            gcol = pl.ds(pl.multiple_of(g * 2 * pair_w, 2 * pair_w), 2 * pair_w)
            for m, ref in enumerate((q, k, v)):
                ga[m, :, :, :, :, gcol] = mm(xt[...], ref[:, gcol]).astype(BF).reshape(2, 2, 2, part, 2 * pair_w)
            for gg in range(groups):
                pl.when(g == gg)(functools.partial(lambda gg: (begin(A(gg)), None)[1], gg))
        return carry
    lax.fori_loop(0, 4 * groups, body, 0)

    def rest_of_rows(s):
        at = pl.ds(s * rows, rows)
        r = r1f[at, :]
        for m, ref in enumerate((q, k, v)):
            r = r + mm(ref[at, :], wa[m].reshape(width, width), NT)
        ig_o[:, s, :] = r[:seg_rows]
    vbuf[0, 0:1, :] = jnp.sum(q[...].astype(F32), axis=0, keepdims=True)
    vbuf[0, 1:2, :] = jnp.sum(v[...].astype(F32), axis=0, keepdims=True)
    legs.start("v0")
    tail(24)
    tail(25)
    legs.got("v0")
    vbuf[2] = vbuf[0] + vbuf[1]
    legs.start("v1")
    rest_of_rows(0)
    tail(26)
    tail(27)
    legs.got("v1")
    vbuf[4] = vbuf[2] + vbuf[3]
    legs.start("v2")
    rest_of_rows(1)
    tail(28)
    tail(29)
    legs.got("v2")
    vbuf[6 + z] = vbuf[4] + vbuf[5]
    legs.start(*[("v", i) for i in (1, 2, 3)])
    tail(30)
    legs.got(*[("v", i) for i in (1, 2, 3)])
    gv_ref[...] = ((vbuf[6] + vbuf[7]) + vbuf[8]) + vbuf[9]
    legs.sent()


def backward(seg_rows, lengths, x, w, q, k, v, c, dr1, dup, ddn, lse, dvec):
    segs, rows, width = q.shape
    total = segs * rows
    part = w.shape[-2]
    sd = jax.ShapeDtypeStruct
    any_, vm = pl.BlockSpec(memory_space=pl.ANY), whole()
    V = lambda *s, t=BF: pltpu.VMEM(s, t)
    scratch = [V(*w.shape), V(*w.shape)] + [V(total, width)] * 4 + [V(total, width, t=F32), V(total, width), V(width, total), V(total, width)]
    scratch += [V(2, 4, 2, part, width)] * 2 + [V(10, 16, width, t=F32)]
    bufs = [V(*s) for _, _, nc, order, route in sum_plan(width) for s in SumUnit.buffers(order, part, nc, route)]
    return pl.pallas_call(
        functools.partial(backward_kernel, seg_rows, len(bufs)),
        in_specs=[pl.BlockSpec(memory_space=pltpu.SMEM)] + [any_] * 9 + [vm, vm],
        out_specs=[vm] * 5,
        out_shape=[sd((seg_rows, segs, width), F32)] + [sd((part, width), F32)] * 3 + [sd((16, width), F32)],
        scratch_shapes=scratch + bufs + [DMA((N_BACK_LEGS,)), DMA((N_BACK_LEGS,)), DMA((15,))],
        compiler_params=pltpu.CompilerParams(collective_id=1, has_side_effects=True, vmem_limit_bytes=63 << 20),
        name="attention_backward_and_sums",
    )(lengths, x, w, q, k, v, c, dr1, dup, ddn, lse, dvec)

STEPS = 5
beta_first = 0.9
beta_second = 0.999
adam_epsilon = 1e-08
matrix_rate = 0.06
vector_rate = 0.2
weight_decay = 0.01
ORDERS = ("zxyc", "yczx", "yczx")


def adam(weight, moment_one, moment_two, gradient, step_rate, decay_rate):
    first_new = beta_first * moment_one + (1.0 - beta_first) * gradient
    second_new = beta_second * moment_two + (1.0 - beta_second) * gradient * gradient
    first_hat = first_new / (1.0 - beta_first**STEPS)
    second_hat = second_new / (1.0 - beta_second**STEPS)
    update = first_hat / (jnp.sqrt(second_hat) + adam_epsilon)
    return (weight - step_rate * (update + decay_rate * weight), first_new, second_new)


def shards(
    own_plan,
    tokens,
    segment_lengths,
    cotangent,
    attention_master,
    attention_mean,
    attention_square,
    up_master,
    up_mean,
    up_square,
    down_master,
    down_mean,
    down_square,
    vector_master,
    vector_mean,
    vector_square,
):
    width = tokens.shape[2]
    dp_count, tensor_count = lax.axis_size("dp"), lax.axis_size("tensor")
    part, columns = vector_master.shape
    spare = 16 - columns
    vec_low = vector_master.astype(BF).T
    if own_plan:
        piece = jnp.pad(vec_low, ((0, spare), (0, 128 - part)))
        turned = lambda a: a.transpose(1, 0, 2)
        block_output, q, k, v, c, x, w_all, dr1, d_up, d_down, lse, dvec_ffn = forward(
            segment_lengths, turned(tokens), turned(cotangent), attention_master, up_master, down_master, piece
        )
    else:
        low = [m.astype(BF) for m in (attention_master, up_master, down_master)]
        w_all = lax.all_gather(low[0], ("dp", "tensor"), axis=0, tiled=True)
        up_all, down_all = (lax.all_gather(m, ("tensor", "dp"), axis=0, tiled=True) for m in low[1:])
        rows = lax.all_gather(vec_low, "dp", axis=1, tiled=True).astype(F32)
        table = jnp.pad(rows, ((0, spare), (0, 0)))
        w_all = w_all.reshape(4, width, width)
        up_all = up_all.reshape(tensor_count, width, width)
        down_all = down_all.reshape(tensor_count, width, width)
        q, k, v, c, n1, inv, ab, lse = attn_fwd(segment_lengths, tokens, w_all, table)
        block_output, dr1, d_up, d_down, dvec_ffn = ffn(ab, n1, inv, cotangent, up_all, down_all, table)
    if own_plan:
        input_grad, s_attention, s_up, s_down, s_vec = backward(
            tokens.shape[1], segment_lengths, x, w_all, q, k, v, c, dr1, d_up, d_down, lse, dvec_ffn
        )
        block_output, input_grad = turned(block_output), turned(input_grad)
        s_vec = lax.dynamic_slice_in_dim(s_vec, lax.axis_index("dp") * part, part, axis=1)
    else:
        input_grad, d_attention, dvec_att = attn_bwd(segment_lengths, tokens, w_all, q, k, v, c, lse, dr1)
        d_vec = dvec_ffn + dvec_att
        flat = lambda g: g.astype(F32).reshape(-1, width)
        s_attention = lax.psum_scatter(flat(d_attention), ("dp", "tensor"), scatter_dimension=0, tiled=True)
        s_up, s_down = (lax.psum_scatter(flat(g), ("tensor", "dp"), scatter_dimension=0, tiled=True) for g in (d_up, d_down))
        s_vec = lax.psum(lax.psum_scatter(d_vec, "dp", scatter_dimension=1, tiled=True), "tensor")
    s_vec = s_vec[:columns].T

    attention_new = adam(attention_master, attention_mean, attention_square, s_attention, matrix_rate, weight_decay)
    up_new = adam(up_master, up_mean, up_square, s_up, matrix_rate, weight_decay)
    down_new = adam(down_master, down_mean, down_square, s_down, matrix_rate, weight_decay)
    vector_new = adam(vector_master, vector_mean, vector_square, s_vec, vector_rate, 0.0)
    return (block_output, input_grad, *attention_new, *up_new, *down_new, *vector_new)


def solution(mesh):
    rows, cols = P(("dp", "tensor")), P("dp", "tensor")
    own_plan = mesh.shape["dp"] == 8 and mesh.shape["tensor"] == 4
    return jax.shard_map(
        functools.partial(shards, own_plan),
        mesh=mesh,
        in_specs=(rows,) * 6 + (cols,) * 6 + (P("dp"),) * 3,
        out_specs=(rows,) * 5 + (cols,) * 6 + (P("dp"),) * 3,
        check_vma=False,
    )
```

```python
import functools

import jax
import jax.numpy as jnp
from jax import lax
from jax.experimental import pallas as pl
from jax.experimental.pallas import tpu as pltpu
from jax.sharding import PartitionSpec as P


HEAD_DIM = 64
MEM = 10
norm_epsilon = 1e-12
inv_root_two = 0.7071067811865476
inv_root_tau = 0.3989422804014327
F32, BF = jnp.float32, jnp.bfloat16
NT = (((1,), (1,)), ((), ()))
TN = (((0,), (0,)), ((), ()))
NN = (((1,), (0,)), ((), ()))

def mm(a, b, dims=NN):
    return lax.dot_general(a, b, dims, preferred_element_type=F32)

def whole(shape=None):
    return pl.BlockSpec(memory_space=pltpu.VMEM)

def norm_stats(signal, width):
    centre = signal - jnp.sum(signal, axis=-1, keepdims=True) * (1.0 / width)
    inverse = lax.rsqrt(jnp.sum(centre * centre, axis=-1, keepdims=True) * (1.0 / width) + norm_epsilon)
    return centre * inverse, inverse

def norm_back(up, scaled, inverse, width):
    return inverse * (up - jnp.sum(up, axis=-1, keepdims=True) * (1.0 / width)
                      - scaled * (jnp.sum(up * scaled, axis=-1, keepdims=True) * (1.0 / width)))

def attn_fwd_kernel(seg_rows, len_ref, x_ref, w_ref, tab_ref, q_ref, k_ref, v_ref, c_ref, n_ref, inv_ref, ab_ref, lse_ref, xs, ct):
    rows, width = xs.shape
    heads = width // HEAD_DIM
    xs[pl.ds(0, seg_rows), :] = x_ref[0]
    xs[pl.ds(seg_rows, rows - seg_rows), :] = jnp.zeros((rows - seg_rows, width), BF)
    x = xs[...]
    q_ref[0] = ((mm(x, w_ref[0]) + tab_ref[0:1, :]).astype(BF) * BF(HEAD_DIM ** -0.5)).astype(BF)
    k_ref[0] = mm(x, w_ref[1]).astype(BF)
    v_ref[0] = (mm(x, w_ref[2]) + tab_ref[1:2, :]).astype(BF)
    live = len_ref[pl.program_id(0)] + MEM
    key_at = lax.broadcasted_iota(jnp.int32, (rows, 1), 0)
    usable = (key_at < live) | ((key_at >= seg_rows - MEM) & (key_at < seg_rows))
    bias = jnp.where(usable, 0.0, -1e30).astype(F32)
    lane = lax.broadcasted_iota(jnp.int32, (rows, 2 * HEAD_DIM), 1)
    zero = jnp.zeros((), BF)

    def pair(i, carry):
        at = pl.ds(pl.multiple_of(i * 2 * HEAD_DIM, 2 * HEAD_DIM), 2 * HEAD_DIM)
        q2, k2, v2 = q_ref[0, :, at], k_ref[0, :, at], v_ref[0, :, at]
        vt = v2.T
        for h in range(2):
            mine = (lane < HEAD_DIM) if h == 0 else (lane >= HEAD_DIM)
            qh = jnp.where(mine, q2, zero)
            s = mm(k2, qh, NT) + bias
            top = jnp.max(s, axis=0, keepdims=True)
            e = jnp.exp(s - top)
            tot = jnp.sum(e, axis=0, keepdims=True)
            p = (e * (1.0 / tot)).astype(BF)
            ct[pl.ds(pl.multiple_of(i * 2 * HEAD_DIM + h * HEAD_DIM, HEAD_DIM), HEAD_DIM), :] = mm(vt[h * HEAD_DIM:(h + 1) * HEAD_DIM], p)
            lse_ref[0, pl.ds(2 * i + h, 1), :] = top + jnp.log(tot)
        return carry
    lax.fori_loop(0, heads // 2, pair, 0)
    c = ct[...].T.astype(BF)
    c_ref[0] = c
    r = x.astype(F32) + mm(c, w_ref[3]) + tab_ref[2:3, :]
    n, inv = norm_stats(r, width)
    n_ref[0] = n
    inv_ref[0] = jnp.broadcast_to(inv, (rows, 128))
    ab_ref[0] = (n * tab_ref[3:4, :] + tab_ref[4:5, :]).astype(BF)

def attn_fwd(lengths, tokens, weights, table):
    segs, seg_rows, width = tokens.shape
    rows = -(-seg_rows // 16) * 16
    heads = width // HEAD_DIM
    hp = -(-heads // 8) * 8
    seg = lambda *s: pl.BlockSpec((1,) + s, lambda i, L: (i,) + (0,) * len(s))
    full = lambda *s: pl.BlockSpec(s, lambda i, L: (0,) * len(s), pipeline_mode=pl.Buffered(1))
    sd = jax.ShapeDtypeStruct
    return pl.pallas_call(
        functools.partial(attn_fwd_kernel, seg_rows),
        grid_spec=pltpu.PrefetchScalarGridSpec(
            num_scalar_prefetch=1, grid=(segs,),
            in_specs=[seg(seg_rows, width), full(*weights.shape), full(*table.shape)],
            out_specs=[seg(rows, width)] * 5 + [seg(rows, 128), seg(rows, width), seg(hp, rows)],
            scratch_shapes=[pltpu.VMEM((rows, width), BF), pltpu.VMEM((width, rows), F32)]),
        out_shape=[sd((segs, rows, width), BF)] * 4 + [sd((segs, rows, width), F32), sd((segs, rows, 128), F32), sd((segs, rows, width), BF), sd((segs, hp, rows), F32)],
        compiler_params=pltpu.CompilerParams(vmem_limit_bytes=56 << 20),
        name="attention_forward",
    )(lengths, tokens, weights, table)

def ffn_kernel(seg_rows, block, ab_ref, n1_ref, inv_ref, cot_ref, up_ref, down_ref, tab_ref,
               out_ref, dr1_ref, dup_ref, ddown_ref, dvec_ref, hid, slope, dy, du):
    segs, rows, width = n1_ref.shape
    total = segs * rows
    chunks = up_ref.shape[0]
    per = rows // block
    nb = total // block
    def rb(i):
        return pl.ds(pl.multiple_of(i * block, block), block)
    y = dr1_ref
    def fwd(i, carry):
        a = ab_ref[rb(i), :]
        acc = jnp.zeros((block, width), F32)
        for j in range(chunks):
            u = mm(a, up_ref[j]) + tab_ref[8 + j:9 + j, :]
            phi = 0.5 * (1.0 + lax.erf(u * inv_root_two))
            h = (u * phi).astype(BF)
            hid[j, rb(i), :] = h
            slope[j, rb(i), :] = phi + u * jnp.exp(-0.5 * u * u) * inv_root_tau
            acc = acc + mm(h, down_ref[j], NT)
        y[rb(i), :] = acc
        return carry
    lax.fori_loop(0, nb, fwd, 0)
    dvec_ref[...] = jnp.zeros_like(dvec_ref)
    for s in range(segs):
        at = pl.ds(s * rows, rows)
        n1 = n1_ref[s]
        r2 = n1 * tab_ref[3:4, :] + tab_ref[4:5, :] + (y[at, :] + tab_ref[7:8, :])
        n2, inv2 = norm_stats(r2, width)
        out_ref[s] = (n2 * tab_ref[5:6, :] + tab_ref[6:7, :])[:seg_rows].astype(BF)
        live = lax.broadcasted_iota(jnp.int32, (rows, 1), 0) < seg_rows
        e = jnp.concatenate([cot_ref[s].astype(F32), jnp.zeros((rows - seg_rows, width), F32)], axis=0)
        dvec_ref[5:6, :] += jnp.sum(e * n2, axis=0, keepdims=True)
        dvec_ref[6:7, :] += jnp.sum(e, axis=0, keepdims=True)
        dr2 = norm_back(e * tab_ref[5:6, :], n2, inv2, width)
        d16 = dr2.astype(BF)
        y[at, :] = dr2
        dy[at, :] = d16
        dvec_ref[7:8, :] += jnp.sum(d16.astype(F32), axis=0, keepdims=True)
    dyt = dy[...].T
    abt = ab_ref[...].T
    for j in range(chunks):
        def back(i, carry):
            g = dy[rb(i), :]
            d = (mm(g, down_ref[j]) * slope[j, rb(i), :]).astype(BF)
            du[rb(i), :] = d
            return carry + jnp.sum(d.astype(F32), axis=0, keepdims=True)
        dvec_ref[8 + j:9 + j, :] = lax.fori_loop(0, nb, back, jnp.zeros((1, width), F32))
        ddown_ref[j] = mm(dyt, hid[j]).astype(BF)
        dup_ref[j] = mm(abt, du[...]).astype(BF)
        def inner(i, carry):
            part = mm(du[rb(i), :], up_ref[j], NT)
            slope[0, rb(i), :] = part if j == 0 else slope[0, rb(i), :] + part
            return carry
        lax.fori_loop(0, nb, inner, 0)
    for s in range(segs):
        at = pl.ds(s * rows, rows)
        da = y[at, :] + slope[0, at, :].astype(BF).astype(F32)
        n1 = n1_ref[s]
        dvec_ref[3:4, :] += jnp.sum(da * n1, axis=0, keepdims=True)
        dvec_ref[4:5, :] += jnp.sum(da, axis=0, keepdims=True)
        dr1 = norm_back(da * tab_ref[3:4, :], n1, inv_ref[s][:, 0:1], width)
        dr1_ref[at, :] = dr1
        dvec_ref[2:3, :] += jnp.sum(dr1.astype(BF).astype(F32), axis=0, keepdims=True)

def ffn(ab, n1, inv, cot, up, down, table):
    segs, rows, width = n1.shape
    seg_rows = cot.shape[1]
    total = segs * rows
    chunks = up.shape[0]
    sd = jax.ShapeDtypeStruct
    return pl.pallas_call(
        functools.partial(ffn_kernel, seg_rows, rows // 2),
        in_specs=[whole()] * 7, out_specs=[whole()] * 5,
        out_shape=[sd(cot.shape, BF), sd((total, width), F32), sd(up.shape, BF), sd(down.shape, BF), sd((16, width), F32)],
        scratch_shapes=[pltpu.VMEM((chunks, total, width), BF), pltpu.VMEM((chunks, total, width), F32), pltpu.VMEM((total, width), BF), pltpu.VMEM((total, width), BF)],
        compiler_params=pltpu.CompilerParams(vmem_limit_bytes=63 << 20),
        name="feed_forward",
    )(ab.reshape(total, width), n1, inv, cot, up, down, table)

def attn_bwd_kernel(seg_rows, len_ref, x_ref, w_ref, q_ref, k_ref, v_ref, c_ref, lse_ref, dr1_ref,
                    ig_ref, dw_ref, dvec_ref, dao, dc, dq, dk, dv, xs):
    segs, rows, width = q_ref.shape
    total = segs * rows
    heads = width // HEAD_DIM
    for s in range(segs):
        xs[pl.ds(s * rows, seg_rows), :] = x_ref[s]
        xs[pl.ds(s * rows + seg_rows, rows - seg_rows), :] = jnp.zeros((rows - seg_rows, width), BF)
    dao[...] = dr1_ref[...].astype(BF)
    dw_ref[3] = mm(c_ref[...].reshape(total, width).T, dao[...]).astype(BF)
    dc[...] = mm(dao[...], w_ref[3], NT).astype(BF)
    key_at = lax.broadcasted_iota(jnp.int32, (rows, 1), 0)
    lane = lax.broadcasted_iota(jnp.int32, (rows, 2 * HEAD_DIM), 1)
    zero = jnp.zeros((), BF)
    for s in range(segs):
        live = len_ref[s] + MEM
        usable = (key_at < live) | ((key_at >= seg_rows - MEM) & (key_at < seg_rows))
        bias = jnp.where(usable, 0.0, -1e30).astype(F32)
        at_rows = pl.ds(s * rows, rows)
        def pair(i, carry):
            at = pl.ds(pl.multiple_of(i * 2 * HEAD_DIM, 2 * HEAD_DIM), 2 * HEAD_DIM)
            q2, k2, v2 = q_ref[s, :, at], k_ref[s, :, at], v_ref[s, :, at]
            g2 = dc[at_rows, at]
            kt = k2.T
            dvp = jnp.zeros((rows, 2 * HEAD_DIM), F32)
            dkp = jnp.zeros((rows, 2 * HEAD_DIM), F32)
            dqt = []
            for h in range(2):
                mine = (lane < HEAD_DIM) if h == 0 else (lane >= HEAD_DIM)
                qh = jnp.where(mine, q2, zero)
                gh = jnp.where(mine, g2, zero)
                p = jnp.exp((mm(k2, qh, NT) + bias) - lse_ref[s, pl.ds(2 * i + h, 1), :])
                dp = mm(v2, gh, NT)
                dvp = dvp + mm(p.astype(BF), gh)
                ds = (p * (dp - jnp.sum(p * dp, axis=0, keepdims=True))).astype(BF)
                dkp = dkp + mm(ds, qh)
                dqt.append(mm(kt[h * HEAD_DIM:(h + 1) * HEAD_DIM], ds))
            dv[at_rows, at] = dvp.astype(BF)
            dk[at_rows, at] = dkp.astype(BF)
            dq[at_rows, at] = (jnp.concatenate(dqt, axis=0).T * (HEAD_DIM ** -0.5)).astype(BF)
            return carry
        lax.fori_loop(0, heads // 2, pair, 0)
    xt = xs[...].T
    dvec_ref[...] = jnp.zeros_like(dvec_ref)
    for j, g in enumerate((dq, dk, dv)):
        dw_ref[j] = mm(xt, g[...]).astype(BF)
    dvec_ref[0:1, :] = jnp.sum(dq[...].astype(F32), axis=0, keepdims=True)
    dvec_ref[1:2, :] = jnp.sum(dv[...].astype(F32), axis=0, keepdims=True)
    for s in range(segs):
        at = pl.ds(s * rows, rows)
        r = dr1_ref[at, :] + mm(dq[at, :], w_ref[0], NT) + mm(dk[at, :], w_ref[1], NT) + mm(dv[at, :], w_ref[2], NT)
        ig_ref[s] = r[:seg_rows]

def attn_bwd(lengths, tokens, weights, q, k, v, c, lse, dr1):
    segs, seg_rows, width = tokens.shape
    rows = q.shape[1]
    total = segs * rows
    sd = jax.ShapeDtypeStruct
    return pl.pallas_call(
        functools.partial(attn_bwd_kernel, seg_rows),
        in_specs=[pl.BlockSpec(memory_space=pltpu.SMEM)] + [whole()] * 8, out_specs=[whole()] * 3,
        out_shape=[sd(tokens.shape, F32), sd(weights.shape, BF), sd((16, width), F32)],
        scratch_shapes=[pltpu.VMEM((total, width), BF)] * 6,
        compiler_params=pltpu.CompilerParams(vmem_limit_bytes=63 << 20),
        name="attention_backward",
    )(lengths, tokens, weights, q, k, v, c, lse, dr1)

MESH = pl.DeviceIdType.MESH
DMA = pltpu.SemaphoreType.DMA
SHAPE = {"z": 4, "x": 2, "y": 2, "c": 2}
ATT, FFN = "zxyc", "yczx"
ROUTES = ("zxy", "zyx", "xzy", "zyx", "zxy", "yzx")


def place():
    d, t = lax.axis_index("dp"), lax.axis_index("tensor")
    return d // 2, d % 2, t // 2, t % 2


def dev(z, x, y, c):
    return {"dp": z * 2 + x, "tensor": y * 2 + c}


def partners(z, x, y, c):
    return {"x": (z, 1 - x, y, c), "y": (z, x, 1 - y, c), "c": (z, x, y, 1 - c), **{i: ((z + i) % 4, x, y, c) for i in (1, 2, 3)}}


def greet(*here):
    b = pltpu.get_barrier_semaphore()
    for p in partners(*here).values():
        pl.semaphore_signal(b, inc=1, device_id=dev(*p), device_id_type=MESH)
    pl.semaphore_wait(b, 6)


class Legs:
    def __init__(self, here, ssem, rsem):
        self.here, self.peer = dict(zip("zxyc", here)), partners(*here)
        self.ssem, self.rsem, self.make = ssem, rsem, {}

    def add(self, key, src, dst, peer):
        i = len(self.make)
        self.make[key] = lambda: pltpu.make_async_remote_copy(
            src(), dst(), self.ssem.at[i], self.rsem.at[i], device_id=dev(*self.peer[peer]), device_id_type=MESH)

    def start(self, *keys):
        for k in keys:
            self.make[k]().start()

    def got(self, *keys):
        for k in keys:
            self.make[k]().wait_recv()

    def sent(self):
        for m in self.make.values():
            m().wait_send()


def view_of(ref, order, cols):
    return lambda at, rows: ref.at[tuple(at.get(ch, slice(None)) for ch in order) + (rows, cols)]


class GatherUnit:
    def __init__(self, legs, key, view, r0, nr, route):
        self.legs, self.key, self.steps = legs, key, [([], [])]
        me = legs.here
        c = {"c": me["c"]}
        full = pl.ds(r0, nr)

        def leg(name, peer, at):
            f = functools.partial(view, at, full)
            legs.add((key, name), f, f, peer)
            self.steps[-1][1].append((key, name))

        for n, d in enumerate(route + "c"):
            fixed = {**c, **{e: me[e] for e in route[n:]}}
            names = [(d, i) for i in (1, 2, 3)] if d == "z" else [(d, d)]
            for name in names:
                leg(name, name[1], fixed)
            self.steps.append(([(key, name) for name in names], []))

    def go(self, n):
        self.legs.got(*self.steps[n][0])
        self.legs.start(*self.steps[n][1])


class SumUnit:
    @staticmethod
    def buffers(order, nr, nc, route):
        inner = order.replace("c", "")
        out, gone = [], ""
        for d in "c" + route:
            gone += d
            out += [tuple(SHAPE[ch] for ch in inner if ch not in gone) + (nr, nc)] * (3 if d == "z" else 1)
        return out

    def __init__(self, legs, key, given, own, bufs, r0, nr, order, route, finish, ready=None):
        self.legs, self.key, self.own, self.finish, self.ready = legs, key, own, finish, ready
        self.inner = order.replace("c", "")
        self.rows = pl.ds(r0, nr)
        me, bufs, done = legs.here, list(bufs), {"c": legs.here["c"]}
        self.work = []
        for d in "c" + route:
            names = [(d, i) for i in (1, 2, 3)] if d == "z" else [(d, d)]
            got = []
            for name in names:
                to = (me["z"] + name[1]) % 4 if d == "z" else 1 - me[d]
                b = bufs.pop(0)
                got.append(b)
                legs.add((key, name), functools.partial(given if d == "c" else own, {**done, d: to}, self.rows), functools.partial(lambda b: b, b), name[1])
            done = {**done, d: me[d]}
            self.work.append(([(key, name) for name in names], dict(done), got))

    def begin(self):
        self.legs.start(*self.work[0][0])

    def go(self, n):
        names, at, bufs = self.work[n]
        self.legs.got(*names)
        if n == 0 and self.ready is not None:
            self.ready()
        free = [ch for ch in self.inner if ch not in at]

        def total(ref, cut):
            t = ref[...].astype(jnp.float32)
            for b in bufs:
                t = t + cut(b).astype(jnp.float32)
            return t
        if n == len(self.work) - 1:
            self.finish(self.rows, total(self.own(at, self.rows), lambda b: b[...]))
            return
        ch = free[0]

        def body(i, carry):
            ref = self.own({**at, ch: i}, self.rows)
            ref[...] = total(ref, lambda b: b[i]).astype(jnp.bfloat16)
            return carry
        lax.fori_loop(0, SHAPE[ch], body, 0)
        self.legs.start(*self.work[n + 1][0])


N_FORWARD_LEGS = 18 * 6 + 4
GATHER_FIRST = (((0, 0), (1, 0)), ((0, 1), (2, 0)), ((0, 2), (1, 1), (3, 0), (4, 0)), ((0, 3), (2, 1), (1, 2), (5, 0)))
GATHER_SLOTS = {
    0: ((2, 2), (3, 1), (4, 1), (5, 1)),
    4: ((1, 3), (6, 0), (7, 0), (8, 0)),
    6: ((2, 3), (3, 2), (4, 2), (5, 2)),
    8: ((1, 4),),
    14: ((6, 1), (7, 1), (8, 1)),
    16: ((2, 4), (3, 3), (4, 3), (5, 3)),
    18: ((6, 2), (7, 2), (8, 2)),
    28: ((6, 3), (7, 3), (8, 3)),
}


def forward_kernel(seg_rows, len_ref, tok, cot, am, um, dm, vp,
                   out_o, q_o, k_o, v_o, c_o, x_o, w_o, dr1_o, dup_o, ddn_o, lse_ref, dvec_ref,
                   wa, wu, wd, vec, tab, traw, craw, xs, cs, q, k, v, ct, cc, n1, inv, ab, hid, slo, dy, dyt, abt,
                   ssem, rsem, lsem):
    segs, rows, width = q_o.shape
    total = segs * rows
    heads = width // HEAD_DIM
    part = am.shape[0]
    z, x, y, c = here = place()
    lt = pltpu.make_async_copy(tok, traw, lsem.at[0]); lt.start()
    lc = pltpu.make_async_copy(cot, craw, lsem.at[1]); lc.start()
    wa[z, x, y, c] = am[...].astype(BF)
    wu[y, c, z, x] = um[...].astype(BF)
    wd[y, c, z, x] = dm[...].astype(BF)
    vec[z, x] = vp[...]

    legs = Legs(here, ssem, rsem)
    pair_w = 2 * HEAD_DIM
    groups = width // (2 * pair_w)
    units = []
    for name, ref, order in (("a", wa, ATT), ("u", wu, FFN), ("d", wd, FFN)):
        for h in range(2 * groups):
            units.append(GatherUnit(legs, (name, h), view_of(ref, order, pl.ds(h * pair_w, pair_w)), 0, part, ROUTES[h]))
    here_vec = lambda: vec.at[z, x]
    for i in (1, 2, 3):
        legs.add(("v", i), here_vec, here_vec, i)
    legs.add("vx", lambda: vec.at[:, x], lambda: vec.at[:, x], "x")

    def advance(what):
        for i, n in what:
            for unit in units[2 * i:2 * i + 2]:
                unit.go(n)

    greet(*here)
    advance(GATHER_FIRST[0])
    legs.start(*[("v", i) for i in (1, 2, 3)])
    lt.wait()

    def pad_rows(to, raw, s):
        to[pl.ds(s * rows, seg_rows), :] = raw[:, s, :]
        to[pl.ds(s * rows + seg_rows, rows - seg_rows), :] = jnp.zeros((rows - seg_rows, width), BF)

    pad_rows(xs, traw, 0)
    advance(GATHER_FIRST[1])
    for s in range(1, segs):
        pad_rows(xs, traw, s)
    legs.got(*[("v", i) for i in (1, 2, 3)])
    legs.start("vx")
    advance(GATHER_FIRST[2])
    lc.wait()
    for s in range(segs):
        pad_rows(cs, craw, s)
    advance(GATHER_FIRST[3])
    legs.got("vx")
    lane_in = lax.broadcasted_iota(jnp.int32, (128, width), 0)
    lane_out = lax.broadcasted_iota(jnp.int32, (128, width), 1)
    acc = jnp.zeros((16, width), F32)
    for d in range(8):
        move = ((lane_out == lane_in + d * part) & (lane_in < part)).astype(BF)
        acc = acc + mm(vec[d // 2, d % 2], move)
    tab[...] = acc
    advance(((0, 4),))
    lane = lax.broadcasted_iota(jnp.int32, (rows, pair_w), 1)
    key_at = lax.broadcasted_iota(jnp.int32, (rows, 1), 0)
    zero = jnp.zeros((), BF)

    def body(it, carry):
        for n in range(0, 8 * groups, 2):
            if n in GATHER_SLOTS:
                pl.when(2 * it == n)(functools.partial(lambda n: advance(GATHER_SLOTS[n]), n))
        g = it // 4

        @pl.when(it % 4 == 0)
        def _():
            col = pl.ds(pl.multiple_of(g * 2 * pair_w, 2 * pair_w), 2 * pair_w)
            w3 = [wa[m, :, :, :, :, col].reshape(width, 2 * pair_w) for m in range(3)]
            xx = xs[...]
            q[:, col] = ((mm(xx, w3[0]) + tab[0:1, col]).astype(BF) * BF(HEAD_DIM ** -0.5)).astype(BF)
            k[:, col] = mm(xx, w3[1]).astype(BF)
            v[:, col] = (mm(xx, w3[2]) + tab[1:2, col]).astype(BF)

        s = (it // 2) % 2
        i = 2 * g + it % 2
        col = pl.ds(pl.multiple_of(i * pair_w, pair_w), pair_w)
        rr = pl.ds(pl.multiple_of(s * rows, 16), rows)
        live = len_ref[s] + MEM
        usable = (key_at < live) | ((key_at >= seg_rows - MEM) & (key_at < seg_rows))
        bias = jnp.where(usable, 0.0, -1e30).astype(F32)
        q2, k2, v2 = q[rr, col], k[rr, col], v[rr, col]
        vt = v2.T
        for h in range(2):
            mine = (lane < HEAD_DIM) if h == 0 else (lane >= HEAD_DIM)
            if h == 1:
                for n in range(1, 8 * groups, 2):
                    if n in GATHER_SLOTS:
                        pl.when(2 * it + 1 == n)(functools.partial(lambda n: advance(GATHER_SLOTS[n]), n))
            sc = mm(k2, jnp.where(mine, q2, zero), NT) + bias
            top = jnp.max(sc, axis=0, keepdims=True)
            e = jnp.exp(sc - top)
            tot = jnp.sum(e, axis=0, keepdims=True)
            p = (e * (1.0 / tot)).astype(BF)
            at = pl.ds(pl.multiple_of(i * pair_w + h * HEAD_DIM, HEAD_DIM), HEAD_DIM)
            ct[s, at, :] = mm(vt[h * HEAD_DIM:(h + 1) * HEAD_DIM], p).astype(BF)
            lse_ref[s, pl.ds(2 * i + h, 1), :] = top + jnp.log(tot)
        return carry
    lax.fori_loop(0, 4 * groups, body, 0)

    spill = [pltpu.make_async_copy(a.at[pl.ds(s * rows, rows)], o.at[s], lsem.at[2 + 2 * n + s]) for n, (a, o) in enumerate(((q, q_o), (k, k_o), (v, v_o))) for s in range(segs)]
    for cp in spill:
        cp.start()
    wcopy = pltpu.make_async_copy(wa, w_o, lsem.at[8]); wcopy.start()
    xcopy = pltpu.make_async_copy(xs, x_o, lsem.at[15]); xcopy.start()
    for s in range(segs):
        rr = pl.ds(s * rows, rows)
        cs_ = ct[s].T
        cc[rr, :] = cs_
        r = xs[rr, :].astype(F32) + mm(cs_, wa[3].reshape(width, width)) + tab[2:3, :]
        n, iv = norm_stats(r, width)
        n1[rr, :] = n
        inv[rr, :] = jnp.broadcast_to(iv, (rows, 128))
        ab[rr, :] = (n * tab[3:4, :] + tab[4:5, :]).astype(BF)
    ccopy = [pltpu.make_async_copy(cc.at[pl.ds(s * rows, rows)], c_o.at[s], lsem.at[9 + s]) for s in range(segs)]
    for cp in ccopy:
        cp.start()

    block = rows // 2
    nb = total // block
    chunks = 4
    def rb(i):
        return pl.ds(pl.multiple_of(i * block, 16), block)
    def up(j):
        return wu[j // 2, j % 2].reshape(width, width)
    def down(j):
        return wd[j // 2, j % 2].reshape(width, width)
    advance(((3, 4), (4, 4), (5, 4)))

    def fwd(i, carry):
        a = ab[rb(i), :]
        for j in range(chunks):
            for n in range(nb):
                if 8 * groups + 4 * n + j in GATHER_SLOTS:
                    pl.when(i == n)(functools.partial(lambda n: advance(GATHER_SLOTS[n]), 8 * groups + 4 * n + j))
            u = mm(a, up(j)) + tab[8 + j:9 + j, :]
            phi = 0.5 * (1.0 + lax.erf(u * inv_root_two))
            hid[j, rb(i), :] = (u * phi).astype(BF)
            slo[j, rb(i), :] = (phi + u * jnp.exp(-0.5 * u * u) * inv_root_tau).astype(BF)
        return carry
    lax.fori_loop(0, nb, fwd, 0)
    abt[...] = ab[...].T
    advance(((6, 4), (7, 4), (8, 4)))
    dvec_ref[...] = jnp.zeros_like(dvec_ref)
    def mid(i, carry):
        yy = tab[7:8, :]
        for j in range(chunks):
            yy = yy + mm(hid[j, rb(i), :], down(j), NT)
        nn = n1[rb(i), :]
        r2 = nn * tab[3:4, :] + tab[4:5, :] + yy
        n2, inv2 = norm_stats(r2, width)
        e = cs[rb(i), :].astype(F32)
        cs[rb(i), :] = (n2 * tab[5:6, :] + tab[6:7, :]).astype(BF)
        dvec_ref[5:6, :] += jnp.sum(e * n2, axis=0, keepdims=True)
        dvec_ref[6:7, :] += jnp.sum(e, axis=0, keepdims=True)
        dr2 = norm_back(e * tab[5:6, :], n2, inv2, width)
        g16 = dr2.astype(BF)
        dy[rb(i), :] = g16
        dvec_ref[7:8, :] += jnp.sum(g16.astype(F32), axis=0, keepdims=True)
        da = jnp.zeros((block, width), F32)
        for j in range(chunks):
            d16 = (mm(g16, down(j)) * slo[j, rb(i), :].astype(F32)).astype(BF)
            slo[j, rb(i), :] = d16
            dvec_ref[8 + j:9 + j, :] += jnp.sum(d16.astype(F32), axis=0, keepdims=True)
            da = da + mm(d16, up(j), NT)
        da = dr2 + da.astype(BF).astype(F32)
        dvec_ref[3:4, :] += jnp.sum(da * nn, axis=0, keepdims=True)
        dvec_ref[4:5, :] += jnp.sum(da, axis=0, keepdims=True)
        dr1 = norm_back(da * tab[3:4, :], nn, inv[rb(i), 0:1], width)
        n1[rb(i), :] = dr1
        dvec_ref[2:3, :] += jnp.sum(dr1.astype(BF).astype(F32), axis=0, keepdims=True)
        return carry
    lax.fori_loop(0, nb, mid, 0)
    dcopy = pltpu.make_async_copy(n1, dr1_o, lsem.at[0]); dcopy.start()
    for s in range(segs):
        craw[:, s, :] = cs[pl.ds(s * rows, seg_rows), :]
    ocopy = pltpu.make_async_copy(craw, out_o, lsem.at[1]); ocopy.start()
    dyt[...] = dy[...].T
    legs.sent()
    def grad_copies(j):
        return (pltpu.make_async_copy(wd.at[j // 2, j % 2], ddn_o.at[j // 2, j % 2], lsem.at[11 + 2 * (j % 2)]),
                pltpu.make_async_copy(wu.at[j // 2, j % 2], dup_o.at[j // 2, j % 2], lsem.at[12 + 2 * (j % 2)]))
    def grads(j, carry):
        shape = wd.shape[2:]
        @pl.when(j >= 2)
        def _():
            for cp in grad_copies(j - 2):
                cp.wait()
        wd[j // 2, j % 2] = mm(dyt[...], hid[j]).astype(BF).reshape(shape)
        wu[j // 2, j % 2] = mm(abt[...], slo[j]).astype(BF).reshape(shape)
        for cp in grad_copies(j):
            cp.start()
        return carry
    lax.fori_loop(0, chunks, grads, 0)
    for j in (2, 3):
        for cp in grad_copies(j):
            cp.wait()
    for cp in spill + [wcopy, xcopy, dcopy, ocopy] + ccopy:
        cp.wait()

def forward(lengths, tokens, cotangent, att, up, down, piece):
    seg_rows, segs, width = tokens.shape
    part = att.shape[0]
    rows = -(-seg_rows // 16) * 16
    total = segs * rows
    hp = -(-(width // HEAD_DIM) // 8) * 8
    sd = jax.ShapeDtypeStruct
    any_, vm = pl.BlockSpec(memory_space=pl.ANY), whole()
    wshape, fshape = (4, 2, 2, 2, part, width), (2, 2, 4, 2, part, width)
    V = lambda *s, t=BF: pltpu.VMEM(s, t)
    return pl.pallas_call(
        functools.partial(forward_kernel, seg_rows),
        in_specs=[pl.BlockSpec(memory_space=pltpu.SMEM), any_, any_, vm, vm, vm, vm],
        out_specs=[any_] * 10 + [vm, vm],
        out_shape=[sd(cotangent.shape, BF)] + [sd((segs, rows, width), BF)] * 4 + [sd((total, width), BF), sd(wshape, BF), sd((total, width), F32), sd(fshape, BF), sd(fshape, BF), sd((segs, hp, rows), F32), sd((16, width), F32)],
        scratch_shapes=[V(*wshape), V(*fshape), V(*fshape), V(4, 2, 16, 128), V(16, width, t=F32), V(seg_rows, segs, width), V(seg_rows, segs, width),
                        V(total, width), V(total, width), V(total, width), V(total, width), V(total, width), V(segs, width, rows), V(total, width),
                        V(total, width, t=F32), V(total, 128, t=F32), V(total, width), V(4, total, width), V(4, total, width), V(total, width), V(width, total), V(width, total),
                        DMA((N_FORWARD_LEGS,)), DMA((N_FORWARD_LEGS,)), DMA((16,))],
        compiler_params=pltpu.CompilerParams(collective_id=0, has_side_effects=True, vmem_limit_bytes=63 << 20),
        name="forward_and_feed_forward_backward",
    )(lengths, tokens, cotangent, att, up, down, piece)

N_BACK_LEGS = 18 * 6 + 6
SUM_SLOTS = ((0, 6, 12, 16),) * 3 + ((6, 16, 20, 24),) * 3 + ((12, 20, 24, 26), (18, 24, 26, 28), (24, 26, 28, 30))


def sum_plan(width):
    pw = 2 * HEAD_DIM
    return [((name, h), h * pw, pw, order, ROUTES[h][::-1]) for name, order in (("u", FFN), ("d", FFN), ("a", ATT)) for h in range(width // pw)]


def backward_kernel(seg_rows, n_bufs, len_ref, x_i, w_i, q_i, k_i, v_i, c_i, dr1_i, dup, ddn, lse_ref, dvec_in,
                    ig_o, ga_ref, gu_ref, gd_ref, gv_ref,
                    wa, ga, q, k, v, cc, r1f, xs, xt, dao, own_u, own_d, vbuf, *rest):
    bufs, (ssem, rsem, lsem) = list(rest[:n_bufs]), rest[n_bufs:]
    segs, rows, width = q_i.shape
    total = segs * rows
    heads = width // HEAD_DIM
    pair_w = 2 * HEAD_DIM
    groups = width // (2 * pair_w)
    part = ga_ref.shape[0]
    z, x, y, c = here = place()
    legs = Legs(here, ssem, rsem)

    load = {}
    def local(name, src, dst, i):
        load[name] = pltpu.make_async_copy(src, dst, lsem.at[i])
        load[name].start()
    local("dr1", dr1_i, r1f, 0)
    local("w", w_i, wa, 1)
    for s in range(segs):
        rr = pl.ds(s * rows, rows)
        local(("c", s), c_i.at[s], cc.at[rr], 2 + s)

    loaded = set()
    def need(name):
        if name not in loaded:
            loaded.add(name)
            load[name].wait()

    units = {}
    for key, c0, nc, order, route in sum_plan(width):
        mine = bufs[:6]
        del bufs[:6]
        col = pl.ds(c0, nc)
        if key[0] == "a":
            given = own = view_of(ga, ATT, col)
            out, ready = ga_ref, None
        else:
            given = view_of(dup if key[0] == "u" else ddn, FFN, col)
            own = view_of(own_u if key[0] == "u" else own_d, "yzx", col)
            out, ready = (gu_ref, gd_ref)[key[0] == "d"], functools.partial(need, key[0])
        def finish(rr, total, out=out, col=col):
            out[rr, col] = total
        units[key] = SumUnit(legs, key, given, own, mine, 0, part, order, route, finish, ready)
    F = lambda i: [("ud"[i // groups], 2 * (i % groups) + h) for h in range(2)]
    A = lambda g: [("a", 2 * g), ("a", 2 * g + 1)]
    def begin(keys):
        for key in keys:
            units[key].begin()
    def stage(keys, n):
        for key in keys:
            units[key].go(n)

    legs.add("v0", lambda: vbuf.at[0], lambda: vbuf.at[1], "c")
    legs.add("v1", lambda: vbuf.at[2], lambda: vbuf.at[3], "y")
    legs.add("v2", lambda: vbuf.at[4], lambda: vbuf.at[5], "x")
    for i in (1, 2, 3):
        legs.add(("v", i), lambda: vbuf.at[6 + z], lambda: vbuf.at[6 + z], i)

    greet(*here)
    for i in range(2 * groups):
        begin(F(i))
    local("t", x_i, xs, 10)
    for s in range(segs):
        rr = pl.ds(s * rows, rows)
        local(("k", s), k_i.at[s], k.at[rr], 6 + s)
        local(("q", s), q_i.at[s], q.at[rr], 8 + s)
        local(("v", s), v_i.at[s], v.at[rr], 4 + s)
    local("u", dup.at[:, c], own_u, 11)
    local("d", ddn.at[:, c], own_d, 12)
    load["dr1"].wait()
    dao[...] = r1f[...].astype(BF)
    for s in range(segs):
        load["c", s].wait()
    load["w"].wait()
    ga[3] = mm(cc[...].T, dao[...]).astype(BF).reshape(ga.shape[1:])
    cc[...] = mm(dao[...], wa[3].reshape(width, width), NT).astype(BF)
    load["t"].wait()
    xt[...] = xs[...].T
    for s in range(segs):
        for n in "qkv":
            load[n, s].wait()
    need("u")
    need("d")
    vbuf[0] = dvec_in[...]
    ticks = {}
    for i, slots in enumerate(SUM_SLOTS):
        for n, at in enumerate(slots):
            ticks.setdefault(at, []).append((F(i) if i < 2 * groups else A(i - 2 * groups), n))
    def tail(n):
        for w in ticks.get(n, ()):
            stage(*w)
    lane = lax.broadcasted_iota(jnp.int32, (rows, pair_w), 1)
    key_at = lax.broadcasted_iota(jnp.int32, (rows, 1), 0)
    zero = jnp.zeros((), BF)

    def body(it, carry):
        def tick(h):
            for n, what in ticks.items():
                if n % 2 == h and n < 8 * groups:
                    pl.when(it == n // 2)(functools.partial(lambda what: ([stage(*w) for w in what], None)[1], what))
        tick(0)
        g = it // 4
        s = (it // 2) % 2
        i = 2 * g + it % 2
        col = pl.ds(pl.multiple_of(i * pair_w, pair_w), pair_w)
        rr = pl.ds(pl.multiple_of(s * rows, 16), rows)
        live = len_ref[s] + MEM
        usable = (key_at < live) | ((key_at >= seg_rows - MEM) & (key_at < seg_rows))
        bias = jnp.where(usable, 0.0, -1e30).astype(F32)
        q2, k2, v2, g2 = q[rr, col], k[rr, col], v[rr, col], cc[rr, col]
        kt = k2.T
        dvp = jnp.zeros((rows, pair_w), F32)
        dkp = jnp.zeros((rows, pair_w), F32)
        dqt = []
        for h in range(2):
            if h == 1:
                tick(1)
            mine = (lane < HEAD_DIM) if h == 0 else (lane >= HEAD_DIM)
            qh = jnp.where(mine, q2, zero)
            gh = jnp.where(mine, g2, zero)
            p = jnp.exp((mm(k2, qh, NT) + bias) - lse_ref[s, pl.ds(2 * i + h, 1), :])
            dp = mm(v2, gh, NT)
            dvp = dvp + mm(p.astype(BF), gh)
            ds = (p * (dp - jnp.sum(p * dp, axis=0, keepdims=True))).astype(BF)
            dkp = dkp + mm(ds, qh)
            dqt.append(mm(kt[h * HEAD_DIM:(h + 1) * HEAD_DIM], ds))
        v[rr, col] = dvp.astype(BF)
        k[rr, col] = dkp.astype(BF)
        q[rr, col] = (jnp.concatenate(dqt, axis=0).T * (HEAD_DIM ** -0.5)).astype(BF)

        @pl.when(it % 4 == 3)
        def _():
            gcol = pl.ds(pl.multiple_of(g * 2 * pair_w, 2 * pair_w), 2 * pair_w)
            for m, ref in enumerate((q, k, v)):
                ga[m, :, :, :, :, gcol] = mm(xt[...], ref[:, gcol]).astype(BF).reshape(2, 2, 2, part, 2 * pair_w)
            for gg in range(groups):
                pl.when(g == gg)(functools.partial(lambda gg: (begin(A(gg)), None)[1], gg))
        return carry
    lax.fori_loop(0, 4 * groups, body, 0)

    def rest_of_rows(s):
        at = pl.ds(s * rows, rows)
        r = r1f[at, :]
        for m, ref in enumerate((q, k, v)):
            r = r + mm(ref[at, :], wa[m].reshape(width, width), NT)
        ig_o[:, s, :] = r[:seg_rows]
    vbuf[0, 0:1, :] = jnp.sum(q[...].astype(F32), axis=0, keepdims=True)
    vbuf[0, 1:2, :] = jnp.sum(v[...].astype(F32), axis=0, keepdims=True)
    legs.start("v0")
    tail(24)
    tail(25)
    legs.got("v0")
    vbuf[2] = vbuf[0] + vbuf[1]
    legs.start("v1")
    rest_of_rows(0)
    tail(26)
    tail(27)
    legs.got("v1")
    vbuf[4] = vbuf[2] + vbuf[3]
    legs.start("v2")
    rest_of_rows(1)
    tail(28)
    tail(29)
    legs.got("v2")
    vbuf[6 + z] = vbuf[4] + vbuf[5]
    legs.start(*[("v", i) for i in (1, 2, 3)])
    tail(30)
    legs.got(*[("v", i) for i in (1, 2, 3)])
    gv_ref[...] = ((vbuf[6] + vbuf[7]) + vbuf[8]) + vbuf[9]
    legs.sent()


def backward(seg_rows, lengths, x, w, q, k, v, c, dr1, dup, ddn, lse, dvec):
    segs, rows, width = q.shape
    total = segs * rows
    part = w.shape[-2]
    sd = jax.ShapeDtypeStruct
    any_, vm = pl.BlockSpec(memory_space=pl.ANY), whole()
    V = lambda *s, t=BF: pltpu.VMEM(s, t)
    scratch = [V(*w.shape), V(*w.shape)] + [V(total, width)] * 4 + [V(total, width, t=F32), V(total, width), V(width, total), V(total, width)]
    scratch += [V(2, 4, 2, part, width)] * 2 + [V(10, 16, width, t=F32)]
    bufs = [V(*s) for _, _, nc, order, route in sum_plan(width) for s in SumUnit.buffers(order, part, nc, route)]
    return pl.pallas_call(
        functools.partial(backward_kernel, seg_rows, len(bufs)),
        in_specs=[pl.BlockSpec(memory_space=pltpu.SMEM)] + [any_] * 9 + [vm, vm],
        out_specs=[vm] * 5,
        out_shape=[sd((seg_rows, segs, width), F32)] + [sd((part, width), F32)] * 3 + [sd((16, width), F32)],
        scratch_shapes=scratch + bufs + [DMA((N_BACK_LEGS,)), DMA((N_BACK_LEGS,)), DMA((15,))],
        compiler_params=pltpu.CompilerParams(collective_id=1, has_side_effects=True, vmem_limit_bytes=63 << 20),
        name="attention_backward_and_sums",
    )(lengths, x, w, q, k, v, c, dr1, dup, ddn, lse, dvec)

STEPS = 5
beta_first = 0.9
beta_second = 0.999
adam_epsilon = 1e-08
matrix_rate = 0.06
vector_rate = 0.2
weight_decay = 0.01
ORDERS = ("zxyc", "yczx", "yczx")


def adam(weight, moment_one, moment_two, gradient, step_rate, decay_rate):
    first_new = beta_first * moment_one + (1.0 - beta_first) * gradient
    second_new = beta_second * moment_two + (1.0 - beta_second) * gradient * gradient
    first_hat = first_new / (1.0 - beta_first**STEPS)
    second_hat = second_new / (1.0 - beta_second**STEPS)
    update = first_hat / (jnp.sqrt(second_hat) + adam_epsilon)
    return (weight - step_rate * (update + decay_rate * weight), first_new, second_new)


def shards(
    own_plan,
    tokens,
    segment_lengths,
    cotangent,
    attention_master,
    attention_mean,
    attention_square,
    up_master,
    up_mean,
    up_square,
    down_master,
    down_mean,
    down_square,
    vector_master,
    vector_mean,
    vector_square,
):
    width = tokens.shape[2]
    dp_count, tensor_count = lax.axis_size("dp"), lax.axis_size("tensor")
    part, columns = vector_master.shape
    spare = 16 - columns
    vec_low = vector_master.astype(BF).T
    if own_plan:
        piece = jnp.pad(vec_low, ((0, spare), (0, 128 - part)))
        turned = lambda a: a.transpose(1, 0, 2)
        block_output, q, k, v, c, x, w_all, dr1, d_up, d_down, lse, dvec_ffn = forward(
            segment_lengths, turned(tokens), turned(cotangent), attention_master, up_master, down_master, piece
        )
    else:
        low = [m.astype(BF) for m in (attention_master, up_master, down_master)]
        w_all = lax.all_gather(low[0], ("dp", "tensor"), axis=0, tiled=True)
        up_all, down_all = (lax.all_gather(m, ("tensor", "dp"), axis=0, tiled=True) for m in low[1:])
        rows = lax.all_gather(vec_low, "dp", axis=1, tiled=True).astype(F32)
        table = jnp.pad(rows, ((0, spare), (0, 0)))
        w_all = w_all.reshape(4, width, width)
        up_all = up_all.reshape(tensor_count, width, width)
        down_all = down_all.reshape(tensor_count, width, width)
        q, k, v, c, n1, inv, ab, lse = attn_fwd(segment_lengths, tokens, w_all, table)
        block_output, dr1, d_up, d_down, dvec_ffn = ffn(ab, n1, inv, cotangent, up_all, down_all, table)
    if own_plan:
        input_grad, s_attention, s_up, s_down, s_vec = backward(
            tokens.shape[1], segment_lengths, x, w_all, q, k, v, c, dr1, d_up, d_down, lse, dvec_ffn
        )
        block_output, input_grad = turned(block_output), turned(input_grad)
        s_vec = lax.dynamic_slice_in_dim(s_vec, lax.axis_index("dp") * part, part, axis=1)
    else:
        input_grad, d_attention, dvec_att = attn_bwd(segment_lengths, tokens, w_all, q, k, v, c, lse, dr1)
        d_vec = dvec_ffn + dvec_att
        flat = lambda g: g.astype(F32).reshape(-1, width)
        s_attention = lax.psum_scatter(flat(d_attention), ("dp", "tensor"), scatter_dimension=0, tiled=True)
        s_up, s_down = (lax.psum_scatter(flat(g), ("tensor", "dp"), scatter_dimension=0, tiled=True) for g in (d_up, d_down))
        s_vec = lax.psum(lax.psum_scatter(d_vec, "dp", scatter_dimension=1, tiled=True), "tensor")
    s_vec = s_vec[:columns].T

    attention_new = adam(attention_master, attention_mean, attention_square, s_attention, matrix_rate, weight_decay)
    up_new = adam(up_master, up_mean, up_square, s_up, matrix_rate, weight_decay)
    down_new = adam(down_master, down_mean, down_square, s_down, matrix_rate, weight_decay)
    vector_new = adam(vector_master, vector_mean, vector_square, s_vec, vector_rate, 0.0)
    return (block_output, input_grad, *attention_new, *up_new, *down_new, *vector_new)


def solution(mesh):
    rows, cols = P(("dp", "tensor")), P("dp", "tensor")
    own_plan = mesh.shape["dp"] == 8 and mesh.shape["tensor"] == 4
    return jax.shard_map(
        functools.partial(shards, own_plan),
        mesh=mesh,
        in_specs=(rows,) * 6 + (cols,) * 6 + (P("dp"),) * 3,
        out_specs=(rows,) * 5 + (cols,) * 6 + (P("dp"),) * 3,
        check_vma=False,
    )
```
